32 devices in a mesh: dp: 4 (over y, x), seq: 8 (over z, core).
Axes of the slice: x: 2, y: 2, z: 4, core: 2. Of those that a mesh axis runs over, the one named last changes fastest.
Arguments:
- tokens: bfloat16 [4, 4096, 2048], P('dp', 'seq'), may hold values from -6 to 6
- w_query: bfloat16 [2048, 1024], replicated, may hold values from -0.125 to 0.125
- keys: bfloat16 [4, 4096, 1024], P('dp', 'seq'), may hold values from -0.5 to 0.5
- values: bfloat16 [4, 4096, 1024], P('dp', 'seq'), may hold values from -6 to 6
- log_decay: float32 [4, 8, 4096], P('dp', None, 'seq'), may hold values from -0.76640625 to 0, as said below
- regular: float32 [8], replicated, may hold values from 1 to 8
- grad_out: bfloat16 [4, 4096, 1024], P('dp', 'seq'), may hold values from -0.046875 to 0.046875
Outputs:
- mixed: bfloat16 [4, 4096, 1024], P('dp', 'seq')
- query_grad: float32 [1024, 2048], P('dp', 'seq')
The draws below stay inside these ranges and needn't reach their ends.
Inputs may be any that keep to these rules, and one draw needn't show every extreme that they name: `log_decay`: a head's decay varies from position to position.
All inputs are finite; a program needn't handle non-finite values.
Results may differ from the reference program's by a relative error of at most 0.0049.
Values sent between devices are 32-bit elements; how exact they have to be, the bound alone decides.
No kernel may reach another device: no remote copies, remote signals or barrier semaphores. Data moves between devices by JAX's collectives and lax.ppermute only.
A program may use at most 64 MiB of HBM per device.

```python
import math
import jax
import jax.numpy as jnp
from jax import lax

D = 2048
H = 8
DH = 128
GROUP = 512
ITERS = 4
BATCH_SEQUENCES = 4
SEQUENCE_LENGTH = 4096
HD = 1024


def draw_log_decay(key, part):
    sequence_lanes = jax.random.split(key, 6)
    fast_share = 0.5
    head_shape = (BATCH_SEQUENCES, H, 1)
    is_fast = jax.random.uniform(sequence_lanes[0], head_shape) < fast_share
    fast_rate = jnp.exp(jax.random.uniform(sequence_lanes[1], head_shape, minval=math.log(10.0), maxval=math.log(17.0))) / GROUP
    slow_rate = jnp.exp(jax.random.uniform(sequence_lanes[2], head_shape, minval=math.log(0.02), maxval=math.log(0.3))) / SEQUENCE_LENGTH
    event_rate = jnp.where(is_fast, fast_rate, slow_rate)
    random_offset = jnp.exp(jax.random.uniform(sequence_lanes[3], (BATCH_SEQUENCES, H, SEQUENCE_LENGTH), minval=-math.log(2.0), maxval=math.log(2.0)))
    spike_position = jax.random.randint(sequence_lanes[4], (BATCH_SEQUENCES, 2, 1), 0, SEQUENCE_LENGTH)
    token_positions = jnp.arange(SEQUENCE_LENGTH)
    spike_mask = jnp.any(token_positions[None, None, :] == spike_position, axis=1)
    portion_value = jax.random.uniform(sequence_lanes[5], (BATCH_SEQUENCES, H, SEQUENCE_LENGTH), minval=0.2, maxval=0.5)
    spike_event = jnp.where(spike_mask[:, None, :], -jnp.log(1.0 - portion_value), 0.0)
    return (-(event_rate * random_offset) - spike_event).astype(jnp.float32)


def shard_levels(stream_key, shape, cuts, least, largest):
    level, own = 1.0, jax.random.fold_in(stream_key, 6)
    for axis_at, parts in cuts:
        steps = jnp.exp(jax.random.uniform(jax.random.fold_in(own, axis_at), (parts,), jnp.float32, least / len(cuts), largest / len(cuts)))
        level = level * jnp.repeat(steps, shape[axis_at] // parts).reshape([-1 if axis == axis_at else 1 for axis in range(len(shape))])
    return level


def centred(own_key, extent, scale, bound, shards=(), held_as=jnp.bfloat16):
    entries = scale * jax.random.normal(own_key, extent, jnp.float32)
    if shards:
        entries = entries * shard_levels(own_key, extent, shards, -0.22, 0.18)
    return jnp.clip(entries, -bound, bound).astype(held_as)


def setup_inputs(seed: int = 0) -> dict:
    splits = jax.random.split(jax.random.key(seed), 8)
    return {
        "tokens": centred(splits[0], (BATCH_SEQUENCES, SEQUENCE_LENGTH, D), 1.0, 6.0, ((0, 4), (1, 8))),
        "w_query": centred(splits[1], (D, HD), D ** -0.5, 0.125),
        "keys": centred(splits[2], (BATCH_SEQUENCES, SEQUENCE_LENGTH, HD), DH ** -0.5, 0.5, ((0, 4), (1, 8))),
        "values": centred(splits[3], (BATCH_SEQUENCES, SEQUENCE_LENGTH, HD), 1.0, 6.0, ((0, 4), (1, 8))),
        "log_decay": draw_log_decay(jax.random.fold_in(splits[7], 71), 0),
        "regular": jnp.clip(jnp.exp(jax.random.uniform(splits[5], (H,), jnp.float32, math.log(1.0), math.log(8.0))), 1.0, 8.0),
        "grad_out": centred(splits[6], (BATCH_SEQUENCES, SEQUENCE_LENGTH, HD), (BATCH_SEQUENCES * SEQUENCE_LENGTH) ** -0.5, 0.046875, ((0, 4), (1, 8))),
    }


exact_mode = lax.Precision.HIGHEST


def product(left, right):
    return jnp.dot(left, right, precision=exact_mode)


def decay_table(cumulative):
    token_positions = jnp.arange(cumulative.shape[0])
    lower_mask = token_positions[:, None] >= token_positions[None, :]
    spread = cumulative[:, None] - cumulative[None, :]
    return jnp.where(lower_mask, jnp.exp(jnp.where(lower_mask, spread, 0.0)), 0.0)


def chebyshev(right_side, apply_fn, center, half_span):
    solution = jnp.zeros_like(right_side)
    residual = right_side
    search = right_side
    step_size = 1.0 / center
    for index_step in range(ITERS):
        if index_step > 0:
            factor = 0.5 if index_step == 1 else 0.25
            momentum = factor * (half_span * step_size) ** 2
            step_size = 1.0 / (center - momentum / step_size)
            search = residual + momentum * search
        solution = solution + step_size * search
        if index_step + 1 < ITERS:
            residual = residual - step_size * apply_fn(search)
    return solution


def solve_group(queries, key_rows, value_rows, grad_rows, cumulative, ridge, gram_state, memory):
    weights = decay_table(cumulative)
    scale = jnp.exp(cumulative)[:, None]
    trace_rows = scale[:, 0] * jnp.trace(gram_state) + product(weights, jnp.sum(key_rows * key_rows, axis=1))
    half_span = 0.5 * trace_rows[:, None]
    center = ridge + half_span

    def apply_fn(search):
        return ridge * search + scale * product(search, gram_state) + product(weights * product(search, key_rows.T), key_rows)

    solved = chebyshev(queries, apply_fn, center, half_span)
    output = scale * product(solved, memory.T) + product(weights * product(solved, key_rows.T), value_rows)
    pulled = scale * product(grad_rows, memory) + product(weights * product(grad_rows, value_rows.T), key_rows)
    query_rows = chebyshev(pulled, apply_fn, center, half_span)
    return output, query_rows


def local_states(key_rows, value_rows, cumulative):
    tail_weight = jnp.exp(cumulative[-1] - cumulative)[:, None]
    return product((key_rows * tail_weight).T, key_rows), product((value_rows * tail_weight).T, key_rows)


def run_head(item_set):
    queries, key_rows, value_rows, grad_rows, log_steps, ridge = item_set
    zero_state = jnp.zeros((queries.shape[-1], queries.shape[-1]), queries.dtype)

    def group_step(carried, pieces):
        gram_state, memory = carried
        group_query, group_key, group_value, group_grad, group_log = pieces
        cumulative = jnp.cumsum(group_log)
        output, query_rows = solve_group(group_query, group_key, group_value, group_grad, cumulative, ridge, gram_state, memory)
        gram_local, memory_local = local_states(group_key, group_value, cumulative)
        last_decay = jnp.exp(cumulative[-1])
        return (last_decay * gram_state + gram_local, last_decay * memory + memory_local), (output, query_rows)

    final_state, results = lax.scan(group_step, (zero_state, zero_state), (queries, key_rows, value_rows, grad_rows, log_steps))
    return results


def to_heads(array):
    shaped = array.reshape(BATCH_SEQUENCES, SEQUENCE_LENGTH, H, DH).transpose(0, 2, 1, 3)
    return shaped.reshape(BATCH_SEQUENCES * H, SEQUENCE_LENGTH // GROUP, GROUP, DH).astype(jnp.float32)


def from_heads(array):
    return array.reshape(BATCH_SEQUENCES, H, SEQUENCE_LENGTH, DH).transpose(0, 2, 1, 3).reshape(BATCH_SEQUENCES, SEQUENCE_LENGTH, H * DH)


def reference(tokens, w_query, keys, values, log_decay, regular, grad_out):
    flat_tokens = tokens.reshape(BATCH_SEQUENCES * SEQUENCE_LENGTH, D)
    queries = jnp.dot(flat_tokens, w_query, preferred_element_type=jnp.float32).astype(jnp.bfloat16)
    queries = lax.optimization_barrier(queries)
    ridge = jnp.broadcast_to(regular[None, :], (BATCH_SEQUENCES, H)).reshape(BATCH_SEQUENCES * H)
    log_steps = log_decay.reshape(BATCH_SEQUENCES * H, SEQUENCE_LENGTH // GROUP, GROUP)
    outputs, query_rows = lax.map(run_head, (to_heads(queries), to_heads(keys), to_heads(values), to_heads(grad_out), log_steps, ridge))
    mixed = from_heads(outputs).astype(jnp.bfloat16)
    grad_flat = from_heads(query_rows).astype(jnp.bfloat16).reshape(BATCH_SEQUENCES * SEQUENCE_LENGTH, H * DH)
    query_grad = lax.dot_general(grad_flat, flat_tokens, (((0,), (0,)), ((), ())), preferred_element_type=jnp.float32)
    return mixed, query_grad
```

```python
import functools

import jax
import jax.numpy as jnp
from jax import lax
from jax.experimental import pallas as pl
from jax.experimental.pallas import tpu as pltpu
from jax.sharding import PartitionSpec as P

ITERS = 4
SUB = 128
EXTRA = 8


F32 = jnp.float32
BF16 = jnp.bfloat16


def dot(left, right):
    return jnp.dot(left, right, preferred_element_type=F32)


def split(value):
    high = value.astype(BF16)
    low = (value - high.astype(F32)).astype(BF16)
    return high, low


def wide(value, axis=1):
    return jnp.concatenate(split(value), axis=axis)


def lane_shift(value, step):
    lanes = lax.broadcasted_iota(jnp.int32, value.shape, 1)
    return jnp.where(lanes >= step, pltpu.roll(value, step, 1), 0.0), lanes >= step


def cumulative_rows(value):
    step = 1
    while step < value.shape[1]:
        value = value + lane_shift(value, step)[0]
        step *= 2
    return value


def decayed_rows(value, cumulative):
    step = 1
    while step < value.shape[1]:
        earlier, inside = lane_shift(cumulative, step)
        factor = jnp.exp(jnp.where(inside, cumulative - earlier, 0.0))
        value = value + factor * lane_shift(value, step)[0]
        step *= 2
    return value


def states_kernel(half, per, core_ref, keys_ref, values_ref, decay_ref, *rest):
    outs, (cumulative_ref, trace_ref), square_ref = rest[: 2 * per], rest[2 * per : 2 * per + 2], rest[-1]
    rows, dim = keys_ref.shape[0], SUB
    core = core_ref[0]
    pieces = rows // SUB
    offset = jnp.zeros((decay_ref.shape[0], 1), F32)
    full = []
    for c in range(pieces):
        part = cumulative_rows(decay_ref[:, c * SUB : (c + 1) * SUB])
        cumulative_ref[:, c * SUB : (c + 1) * SUB] = part
        full.append(part + offset)
        offset = offset + part[:, SUB - 1 : SUB]
    total = offset
    tails = jnp.exp(total - jnp.concatenate(full, axis=1))
    square_ref[0] = tails
    square_ref[2] = jnp.broadcast_to(jnp.exp(total), tails.shape)
    for k in range(per):
        for side in range(2):
            for i in range(half):
                block = (core if side == 0 else 1 - core) * half + i
                head = block * per + k
                column = pl.ds(pl.multiple_of(head * dim, dim), dim)
                key = keys_ref[:, column]
                tail = square_ref[0, pl.ds(head, 1), :]
                key_turned = key.astype(F32).T
                value_turned = values_ref[:, column].astype(F32).T
                square_ref[1, pl.ds(head, 1), :] = jnp.sum(key_turned * key_turned, axis=0, keepdims=True)
                both = jnp.concatenate([key_turned * tail, value_turned * tail], axis=0)
                high, low = split(both)
                out = outs[2 * k + side]
                out[i, 0 : 2 * dim, :] = dot(high, key) + dot(low, key)
                decay = square_ref[2, pl.ds(head, 1), :][:, 0:SUB]
                out[i, 2 * dim : 2 * dim + EXTRA, :] = jnp.broadcast_to(decay, (EXTRA, dim))
    carry = jnp.zeros_like(total)
    for c in range(pieces):
        lanes = slice(c * SUB, (c + 1) * SUB)
        part = decayed_rows(square_ref[1, :, lanes], cumulative_ref[:, lanes])
        part = part + jnp.exp(cumulative_ref[:, lanes]) * carry
        trace_ref[:, lanes] = part
        carry = part[:, SUB - 1 : SUB]


def local_states(core, keys, values, decay, half, per):
    rows, columns = keys.shape
    heads = decay.shape[0]
    dim = columns // heads
    state = jax.ShapeDtypeStruct((half, 2 * dim + EXTRA, dim), F32)
    table = jax.ShapeDtypeStruct((heads, rows), F32)
    vmem = pl.BlockSpec(memory_space=pltpu.VMEM)
    return pl.pallas_call(
        functools.partial(states_kernel, half, per),
        out_shape=[state] * (2 * per) + [table] * 2,
        in_specs=[pl.BlockSpec(memory_space=pltpu.SMEM)] + [vmem] * 3,
        out_specs=[vmem] * (2 * per + 2),
        scratch_shapes=[pltpu.VMEM((3, heads, rows), F32)],
        cost_estimate=pl.CostEstimate(
            flops=8 * rows * dim * dim * heads, bytes_accessed=8 * rows * columns, transcendentals=0
        ),
        name="local_states",
    )(core, keys, values, decay)


def solve_kernel(
    first_ref, regular_ref, q_ref, k_ref, v_ref, g_ref, cumulative_ref, trace_ref, state_ref, *rest
):
    mixed_ref, turned_ref = rest[-2:]
    rows, dim = q_ref.shape
    step = pl.program_id(0)
    head = first_ref[0] + step * first_ref[1]
    ridge = regular_ref[head]
    gram = state_ref[0, 0:dim, :]
    memory = state_ref[0, dim : 2 * dim, :]
    row_at = lax.broadcasted_iota(jnp.int32, (SUB, SUB), 0)
    column_at = lax.broadcasted_iota(jnp.int32, (SUB, SUB), 1)
    lower = row_at >= column_at
    start_trace = jnp.sum(jnp.where(row_at == column_at, gram, 0.0), axis=0, keepdims=True)
    start_trace = jnp.sum(start_trace, axis=1, keepdims=True)
    offset = jnp.zeros((1, 1), F32)
    cumulative_row = cumulative_ref[pl.ds(head, 1), :]
    trace_row = trace_ref[pl.ds(head, 1), :]
    for c in range(rows // SUB):
        place = slice(c * SUB, (c + 1) * SUB)
        cumulative = cumulative_row[:, place]
        last = cumulative[:, SUB - 1 : SUB]
        trace = jnp.exp(cumulative + offset) * start_trace + trace_row[:, place]
        half = 0.5 * trace
        center = ridge + half
        alphas = [1.0 / center]
        betas = []
        for i in range(1, ITERS):
            factor = 0.5 if i == 1 else 0.25
            product = half * alphas[-1]
            betas.append(factor * product * product)
            alphas.append(1.0 / (center - factor * half * product))
        table = jnp.concatenate(alphas + betas + [cumulative], axis=0).T

        def column(index):
            return jnp.broadcast_to(table[:, index : index + 1], (SUB, SUB))

        alpha = [column(i) for i in range(ITERS)]
        beta = [column(ITERS + i) for i in range(ITERS - 1)]
        rise = column(2 * ITERS - 1)
        weights = jnp.where(lower, jnp.exp(jnp.where(lower, rise - cumulative, 0.0)), 0.0)
        scale = jnp.exp(rise)

        key = k_ref[place, :]
        value = v_ref[place, :]
        query = q_ref[place, :]
        grad = g_ref[place, :]
        key_long = key.astype(F32)
        key_turned = key_long.T
        key_turned_half = key_turned.astype(BF16)
        value_turned = value.astype(F32).T
        key_twice = jnp.concatenate([key, key], axis=0)
        value_twice = jnp.concatenate([value, value], axis=0)
        gram_high, gram_low = split(gram)
        memory_turned_high, memory_turned_low = split(memory.T)

        pulled = scale * dot(jnp.concatenate([grad, grad], axis=1), wide(memory, 0))
        score = weights * dot(grad, value_turned.astype(BF16))
        pulled = pulled + dot(wide(score), key_twice)

        search_right = jnp.concatenate([key_turned_half, gram_high], axis=1)
        search_right = jnp.concatenate([search_right, search_right], axis=0)

        def pair(left, right):
            return jnp.concatenate([left, right], axis=0)

        def apply_fn(search):
            high, low = split(search)
            first = dot(jnp.concatenate([high, low], axis=1), search_right)
            second = dot(high, gram_low)
            score = first[:, 0:SUB] * pair(weights, weights)
            return (
                ridge * search
                + pair(scale, scale) * (first[:, SUB:] + second)
                + dot(wide(score), key_twice)
            )

        residual = pair(query.astype(F32), pulled)
        search = residual
        solution = pair(alpha[0], alpha[0]) * search
        for i in range(1, ITERS):
            residual = residual - pair(alpha[i - 1], alpha[i - 1]) * apply_fn(search)
            search = residual + pair(beta[i - 1], beta[i - 1]) * search
            solution = solution + pair(alpha[i], alpha[i]) * search
        solved, query_rows = solution[0:SUB], solution[SUB:]

        high, low = split(solved)
        read_right = jnp.concatenate([key_turned_half, memory_turned_high], axis=1)
        read_right = jnp.concatenate([read_right, read_right], axis=0)
        first = dot(jnp.concatenate([high, low], axis=1), read_right)
        second = dot(high, memory_turned_low)
        output = scale * (first[:, SUB:] + second) + dot(wide(weights * first[:, 0:SUB]), value_twice)
        mixed_ref[place, :] = output.astype(BF16)
        turned_ref[0, :, place] = query_rows.T.astype(BF16).astype(F32)

        if (c + 1) * SUB < rows:
            tail = jnp.exp(last - cumulative)
            decay = jnp.exp(last)
            both = jnp.concatenate([key_turned * tail, value_turned * tail], axis=0)
            grown = dot(wide(both), key_twice)
            gram = decay * gram + grown[0:dim]
            memory = decay * memory + grown[dim:]
            offset = offset + last


def solve_heads(first, regular, queries, keys, values, grads, cumulative, trace, states, mixed):
    rows, columns = keys.shape
    heads = regular.shape[0]
    dim = columns // heads
    count = states.shape[0]

    def at_head(step, first_ref, regular_ref):
        return (0, first_ref[0] + step * first_ref[1])

    wide_spec = pl.BlockSpec((rows, dim), at_head)
    whole = pl.BlockSpec((heads, rows), lambda step, *_: (0, 0))
    operands = [queries, keys, values, grads, cumulative, trace, states]
    in_specs = [wide_spec] * 4 + [whole] * 2
    in_specs.append(pl.BlockSpec((1,) + states.shape[1:], lambda step, *_: (step, 0, 0)))
    aliases = {}
    if mixed is not None:
        operands.append(mixed)
        in_specs.append(pl.BlockSpec(memory_space=pl.ANY))
        aliases = {2 + len(operands) - 1: 0}
    return pl.pallas_call(
        solve_kernel,
        out_shape=[
            jax.ShapeDtypeStruct((rows, columns), BF16),
            jax.ShapeDtypeStruct((count, dim, rows), F32),
        ],
        grid_spec=pltpu.PrefetchScalarGridSpec(
            num_scalar_prefetch=2,
            grid=(count,),
            in_specs=in_specs,
            out_specs=[wide_spec, pl.BlockSpec((1, dim, rows), lambda step, *_: (step, 0, 0))],
        ),
        input_output_aliases=aliases,
        cost_estimate=pl.CostEstimate(
            flops=count * 80 * rows * dim * dim, bytes_accessed=count * 14 * rows * dim, transcendentals=0
        ),
        name="solve_heads",
    )(first, regular, *operands)


def pick_kernel(core_ref, tokens_ref, out_ref):
    out_ref[0] = tokens_ref[...].astype(F32)


def pick_columns(core, tokens, blocks):
    rows, width = tokens.shape
    size = width // (2 * blocks)
    return pl.pallas_call(
        pick_kernel,
        out_shape=jax.ShapeDtypeStruct((blocks, rows, size), F32),
        grid_spec=pltpu.PrefetchScalarGridSpec(
            num_scalar_prefetch=1,
            grid=(blocks,),
            in_specs=[pl.BlockSpec((rows, size), lambda z, core_ref: (0, 2 * z + 1 - core_ref[0]))],
            out_specs=pl.BlockSpec((1, rows, size), lambda z, core_ref: (z, 0, 0)),
        ),
        cost_estimate=pl.CostEstimate(flops=0, bytes_accessed=3 * rows * width, transcendentals=0),
        name="pick_columns",
    )(core, tokens)


def gradient_kernel(order, place_ref, own0, own1, far0, far1, tokens_ref, other_ref, *rest):
    outs, left_ref = rest[:-1], rest[-1]
    core, group, chip = place_ref[0], place_ref[1], place_ref[2]
    half, dim, rows = own0.shape
    blocks = other_ref.shape[0]
    size = other_ref.shape[2]
    for i in range(half):
        near, away = core * half + i, (1 - core) * half + i
        left_ref[near, :, 0:rows] = own0[i].astype(BF16)
        left_ref[away, :, 0:rows] = own1[i].astype(BF16)
        left_ref[near, :, rows:] = far1[i].astype(BF16)
        left_ref[away, :, rows:] = far0[i].astype(BF16)
    left = jnp.concatenate([left_ref[group ^ d] for d in range(2 * half)], axis=0)
    middle = dim // 2
    for z in range(blocks):
        at = chip ^ z
        start = pl.multiple_of((2 * at + core) * size, size)
        right = jnp.concatenate([tokens_ref[:, pl.ds(start, size)], other_ref[at].astype(BF16)], axis=0)
        result = dot(left, right)
        for d in range(2 * half):
            for path in range(2):
                piece = result[d * dim + path * middle : d * dim + (path + 1) * middle]
                which, index = order[path][(d, z)]
                outs[2 * path + which][index] = piece


def gradient_blocks(place, own, far, tokens, other, order):
    half, dim, rows = own[0].shape
    blocks, _, size = other.shape
    count = half * blocks
    vmem = pl.BlockSpec(memory_space=pltpu.VMEM)
    return pl.pallas_call(
        functools.partial(gradient_kernel, order),
        out_shape=[jax.ShapeDtypeStruct((count, dim // 2, size), F32)] * 4,
        in_specs=[pl.BlockSpec(memory_space=pltpu.SMEM)] + [vmem] * 6,
        out_specs=[vmem] * 4,
        scratch_shapes=[pltpu.VMEM((2 * half, dim, 2 * rows), BF16)],
        cost_estimate=pl.CostEstimate(
            flops=2 * 2 * half * dim * 2 * rows * blocks * size,
            bytes_accessed=4 * (4 * half * dim * rows + blocks * rows * size + 2 * count * dim * size),
            transcendentals=0,
        ),
        name="gradient_blocks",
    )(place, *own, *far, tokens, other)


def bit_order(path_bits, dp_bits, seq_bits):
    table = {}
    for d in range(1 << dp_bits):
        for z in range(1 << seq_bits):
            code = 0
            for axis, bit in path_bits:
                code = 2 * code + (((d if axis == "dp" else z) >> bit) & 1)
            half = 1 << (dp_bits + seq_bits - 1)
            table[(d, z)] = (code // half, code % half)
    return table


def flip(axis, bit, sizes):
    shift = bit if axis == "dp" else bit + 1
    return [(i, i ^ (1 << shift)) for i in range(sizes[axis])]


def per_device(sizes, tokens, w_query, keys, values, log_decay, regular, grad_out):
    groups, steps = sizes["dp"], sizes["seq"]
    chips = steps // 2
    heads = log_decay.shape[1]
    rows, width = tokens.shape[1:]
    columns = keys.shape[2]
    dim = columns // heads
    per = heads // groups
    half = groups // 2
    tokens, keys, values, grads, decay = tokens[0], keys[0], values[0], grad_out[0], log_decay[0]
    here = lax.axis_index("seq")
    core = here % 2
    core_row = core.reshape(1).astype(jnp.int32)
    partner = [(i, i ^ 1) for i in range(steps)]

    results = local_states(core_row, keys, values, decay, half, per)
    states, (cumulative, trace) = results[: 2 * per], results[2 * per :]

    def decay_of(state):
        return state[:, 2 * dim : 2 * dim + 1, :]

    is_first = core == 0
    starts = []
    for k in range(per):
        own, sent = states[2 * k], states[2 * k + 1]
        came = lax.ppermute(sent, "seq", partner)
        early = jnp.where(is_first, own, came)
        late = jnp.where(is_first, came, own)
        chip_decay = decay_of(early) * decay_of(late)
        chip_state = decay_of(late) * early + late
        before = jnp.zeros_like(own)
        for t in range(chips - 1):
            pairs = [(2 * t + c, 2 * t + 2 + c) for c in range(2)]
            before = before + lax.ppermute(chip_decay * before + chip_state, "seq", pairs)
        after = decay_of(early) * before + early
        mine = jnp.where(is_first, before, after)
        starts.append((mine, lax.ppermute(jnp.where(is_first, after, before), "seq", partner)))

    queries = jnp.dot(tokens, w_query, preferred_element_type=F32).astype(BF16)
    other = lax.ppermute(pick_columns(core_row, tokens, chips), "seq", partner)

    dp_bits = groups.bit_length() - 1
    seq_bits = chips.bit_length() - 1
    seq_path = [("seq", b) for b in range(seq_bits)]
    paths = [
        [("dp", b) for b in range(dp_bits)] + seq_path,
        [("dp", b) for b in reversed(range(dp_bits))] + seq_path,
    ]
    order = [bit_order(path, dp_bits, seq_bits) for path in paths]
    place = jnp.stack([core, lax.axis_index("dp"), here // 2]).astype(jnp.int32)

    mixed = None
    finished = []
    for k in range(per):
        own, far = [], []
        for side in range(2):
            block = core if side == 0 else 1 - core
            first = jnp.stack([block * half * per + k, jnp.full_like(core, per)]).astype(jnp.int32)
            mixed, turned = solve_heads(
                first, regular, queries, keys, values, grads, cumulative, trace, starts[k][side], mixed
            )
            own.append(turned)
            far.append(lax.ppermute(turned, "seq", partner))
        blocks = gradient_blocks(place, own, far, tokens, other, order)
        parts = []
        for index, path in enumerate(paths):
            keep, send = blocks[2 * index], blocks[2 * index + 1]
            for at, (axis, bit) in enumerate(path):
                total = keep + lax.ppermute(send, axis, flip(axis, bit, sizes))
                middle = total.shape[0] // 2
                keep, send = total[:middle], total[middle:]
            parts.append(total[0])
        finished.append(jnp.concatenate(parts, axis=0))
    return mixed[None], jnp.concatenate(finished, axis=0)


def solution(mesh):
    sizes = dict(mesh.shape)
    in_specs = (
        P("dp", "seq", None),
        P(),
        P("dp", "seq", None),
        P("dp", "seq", None),
        P("dp", None, "seq"),
        P(),
        P("dp", "seq", None),
    )
    out_specs = (P("dp", "seq", None), P("dp", "seq"))
    return jax.shard_map(
        functools.partial(per_device, sizes),
        mesh=mesh,
        in_specs=in_specs,
        out_specs=out_specs,
        check_vma=False,
    )
```

```python
import functools

import jax
import jax.numpy as jnp
from jax import lax
from jax.experimental import pallas as pl
from jax.experimental.pallas import tpu as pltpu
from jax.sharding import PartitionSpec as P

ITERS = 4
SUB = 128
EXTRA = 8


F32 = jnp.float32
BF16 = jnp.bfloat16


def dot(left, right):
    return jnp.dot(left, right, preferred_element_type=F32)


def split(value):
    high = value.astype(BF16)
    low = (value - high.astype(F32)).astype(BF16)
    return high, low


def wide(value, axis=1):
    return jnp.concatenate(split(value), axis=axis)


def lane_shift(value, step):
    lanes = lax.broadcasted_iota(jnp.int32, value.shape, 1)
    return jnp.where(lanes >= step, pltpu.roll(value, step, 1), 0.0), lanes >= step


def cumulative_rows(value):
    step = 1
    while step < value.shape[1]:
        value = value + lane_shift(value, step)[0]
        step *= 2
    return value


def decayed_rows(value, cumulative):
    step = 1
    while step < value.shape[1]:
        earlier, inside = lane_shift(cumulative, step)
        factor = jnp.exp(jnp.where(inside, cumulative - earlier, 0.0))
        value = value + factor * lane_shift(value, step)[0]
        step *= 2
    return value


def decay_tables(decay_ref):
    rows = decay_ref.shape[1]
    offset = jnp.zeros((decay_ref.shape[0], 1), F32)
    local, full = [], []
    for c in range(rows // SUB):
        part = cumulative_rows(decay_ref[:, c * SUB : (c + 1) * SUB])
        local.append(part)
        full.append(part + offset)
        offset = offset + part[:, SUB - 1 : SUB]
    return local, jnp.exp(offset - jnp.concatenate(full, axis=1)), jnp.exp(offset)


def states_kernel(half, per, k, core_ref, keys_ref, values_ref, decay_ref, near_ref, away_ref, table_ref, work_ref):
    rows, dim = keys_ref.shape[0], SUB
    core = core_ref[0]
    local, tails, total = decay_tables(decay_ref)
    work_ref[0] = tails
    work_ref[2] = jnp.broadcast_to(total, tails.shape)
    work_ref[1] = jnp.zeros_like(tails)
    for out, block in ((away_ref, 1 - core), (near_ref, core)):
        for i in range(half):
            head = (block * half + i) * per + k
            column = pl.ds(pl.multiple_of(head * dim, dim), dim)
            key = keys_ref[:, column]
            tail = work_ref[0, pl.ds(head, 1), :]
            key_turned = key.astype(F32).T
            value_turned = values_ref[:, column].astype(F32).T
            work_ref[1, pl.ds(head, 1), :] = jnp.sum(key_turned * key_turned, axis=0, keepdims=True)
            high, low = split(jnp.concatenate([key_turned * tail, value_turned * tail], axis=0))
            out[i, 0 : 2 * dim, :] = dot(high, key) + dot(low, key)
            decay = work_ref[2, pl.ds(head, 1), :][:, 0:SUB]
            out[i, 2 * dim : 2 * dim + EXTRA, :] = jnp.broadcast_to(decay, (EXTRA, dim))
    carry = jnp.zeros_like(total)
    for c in range(rows // SUB):
        lanes = slice(c * SUB, (c + 1) * SUB)
        part = decayed_rows(work_ref[1, :, lanes], local[c]) + jnp.exp(local[c]) * carry
        table_ref[0, :, lanes] = local[c]
        table_ref[1, :, lanes] = part
        carry = part[:, SUB - 1 : SUB]


def local_states(core, keys, values, decay, half, per, k):
    rows, columns = keys.shape
    heads = decay.shape[0]
    dim = columns // heads
    state = jax.ShapeDtypeStruct((half, 2 * dim + EXTRA, dim), F32)
    vmem = pl.BlockSpec(memory_space=pltpu.VMEM)
    return pl.pallas_call(
        functools.partial(states_kernel, half, per, k),
        out_shape=[state, state, jax.ShapeDtypeStruct((2, heads, rows), F32)],
        in_specs=[pl.BlockSpec(memory_space=pltpu.SMEM)] + [vmem] * 3,
        out_specs=[vmem] * 3,
        scratch_shapes=[pltpu.VMEM((3, heads, rows), F32)],
        cost_estimate=pl.CostEstimate(
            flops=16 * rows * dim * dim * half, bytes_accessed=8 * rows * columns, transcendentals=0
        ),
        name="local_states",
    )(core, keys, values, decay)


def solve_kernel(
    first_ref, regular_ref, q_ref, k_ref, v_ref, g_ref, rows_ref, state_ref, *rest
):
    mixed_ref, turned_ref = rest[-2:]
    rows, dim = q_ref.shape
    pieces = range(rows // SUB)
    place = [slice(c * SUB, (c + 1) * SUB) for c in pieces]
    step = pl.program_id(0)
    head = first_ref[0] + step * first_ref[1]
    ridge = regular_ref[head]
    row_at = lax.broadcasted_iota(jnp.int32, (SUB, SUB), 0)
    column_at = lax.broadcasted_iota(jnp.int32, (SUB, SUB), 1)
    lower = row_at >= column_at

    gram = [state_ref[0, 0:dim, :]]
    memory = [state_ref[0, dim : 2 * dim, :]]
    start_trace = jnp.sum(jnp.where(row_at == column_at, gram[0], 0.0), axis=0, keepdims=True)
    start_trace = jnp.sum(start_trace, axis=1, keepdims=True)
    cumulative_row = rows_ref[0, pl.ds(head, 1), :]
    cumulative = [cumulative_row[:, at] for at in place]
    last = [row[:, SUB - 1 : SUB] for row in cumulative]
    whole, offset = [], jnp.zeros((1, 1), F32)
    for c in pieces:
        whole.append(cumulative[c] + offset)
        offset = offset + last[c]
    trace = jnp.exp(jnp.concatenate(whole, axis=1)) * start_trace + rows_ref[1, pl.ds(head, 1), :]
    half = 0.5 * trace
    center = ridge + half
    alphas, gammas = [1.0 / center], []
    for i in range(1, ITERS):
        factor = 0.5 if i == 1 else 0.25
        product = half * alphas[-1]
        alphas.append(1.0 / (center - factor * half * product))
        gammas.append(alphas[-1] * (factor * half * product))
    table = jnp.concatenate(alphas + gammas + [cumulative_row], axis=0).T

    def column(index):
        return [jnp.broadcast_to(table[at, index : index + 1], (SUB, SUB)) for at in place]

    rise = column(2 * ITERS - 1)
    weights = [
        jnp.where(lower, jnp.exp(jnp.where(lower, rise[c] - cumulative[c], 0.0)), 0.0) for c in pieces
    ]
    scale = [jnp.exp(r) for r in rise]

    keys = [k_ref[at, :] for at in place]
    values = [v_ref[at, :] for at in place]
    keys_turned = [key.astype(F32).T for key in keys]
    values_turned = [value.astype(F32).T for value in values]
    for c in pieces[:-1]:
        tail = jnp.exp(last[c] - cumulative[c])
        decay = jnp.exp(last[c])
        both = jnp.concatenate([keys_turned[c] * tail, values_turned[c] * tail], axis=0)
        grown = dot(wide(both), jnp.concatenate([keys[c], keys[c]], axis=0))
        gram.append(decay * gram[-1] + grown[0:dim])
        memory.append(decay * memory[-1] + grown[dim:])
    keys_turned = [key.astype(BF16) for key in keys_turned]
    values_turned = [value.astype(BF16) for value in values_turned]

    def pair(left, right):
        return jnp.concatenate([left, right], axis=0)

    residual = []
    for c in pieces:
        grad = g_ref[place[c], :]
        pulled = scale[c] * dot(jnp.concatenate([grad, grad], axis=1), wide(memory[c], 0))
        score = weights[c] * dot(grad, values_turned[c])
        pulled = pulled + dot(wide(score), pair(keys[c], keys[c]))
        residual.append(pair(q_ref[place[c], :].astype(F32), pulled))

    alpha = column(0)
    change = [pair(alpha[c], alpha[c]) * residual[c] for c in pieces]
    solution = list(change)
    rights = [jnp.concatenate([keys_turned[c], gram[c].astype(BF16)], axis=1) for c in pieces]
    for i in range(1, ITERS):
        alpha, gamma = column(i), column(ITERS + i - 1)
        first = [dot(change[c].astype(BF16), rights[c]) for c in pieces]
        second = [
            dot((first[c][:, 0:SUB] * pair(weights[c], weights[c])).astype(BF16), keys[c]) for c in pieces
        ]
        for c in pieces:
            applied = ridge * change[c] + (pair(scale[c], scale[c]) * first[c][:, SUB:] + second[c])
            residual[c] = residual[c] - applied
            change[c] = pair(alpha[c], alpha[c]) * residual[c] + pair(gamma[c], gamma[c]) * change[c]
            solution[c] = solution[c] + change[c]

    for c in pieces:
        turned_ref[0, :, place[c]] = solution[c][SUB:].T.astype(BF16).astype(F32)
    for c in pieces:
        high, low = split(solution[c][0:SUB])
        memory_high, memory_low = split(memory[c].T)
        right = jnp.concatenate([keys_turned[c], memory_high], axis=1)
        first = dot(jnp.concatenate([high, low], axis=1), pair(right, right))
        second = first[:, SUB:] + dot(high, memory_low)
        score = weights[c] * first[:, 0:SUB]
        output = scale[c] * second + dot(wide(score), pair(values[c], values[c]))
        mixed_ref[place[c], :] = output.astype(BF16)


def solve_heads(first, regular, queries, keys, values, grads, table, states, mixed, after):
    rows, columns = keys.shape
    heads = regular.shape[0]
    dim = columns // heads
    count = states.shape[0]

    def at_head(step, first_ref, regular_ref):
        return (0, first_ref[0] + step * first_ref[1])

    wide_spec = pl.BlockSpec((rows, dim), at_head)
    operands = [queries, keys, values, grads, table, states]
    in_specs = [wide_spec] * 4 + [pl.BlockSpec(table.shape, lambda step, *_: (0, 0, 0))]
    in_specs.append(pl.BlockSpec((1,) + states.shape[1:], lambda step, *_: (step, 0, 0)))
    aliases = {}
    if mixed is not None:
        operands.append(mixed)
        in_specs.append(pl.BlockSpec(memory_space=pl.ANY))
        aliases = {2 + len(operands) - 1: 0}
    if after is not None:
        operands.append(after)
        in_specs.append(pl.BlockSpec(memory_space=pl.ANY))
    return pl.pallas_call(
        solve_kernel,
        out_shape=[
            jax.ShapeDtypeStruct((rows, columns), BF16),
            jax.ShapeDtypeStruct((count, dim, rows), F32),
        ],
        grid_spec=pltpu.PrefetchScalarGridSpec(
            num_scalar_prefetch=2,
            grid=(count,),
            in_specs=in_specs,
            out_specs=[wide_spec, pl.BlockSpec((1, dim, rows), lambda step, *_: (step, 0, 0))],
        ),
        input_output_aliases=aliases,
        cost_estimate=pl.CostEstimate(
            flops=count * 80 * rows * dim * dim, bytes_accessed=count * 14 * rows * dim, transcendentals=0
        ),
        name="solve_heads",
    )(first, regular, *operands)


def pick_kernel(core_ref, tokens_ref, out_ref):
    out_ref[0] = tokens_ref[...].astype(F32)


def pick_columns(core, tokens, blocks):
    rows, width = tokens.shape
    size = width // (2 * blocks)
    return pl.pallas_call(
        pick_kernel,
        out_shape=jax.ShapeDtypeStruct((blocks, rows, size), F32),
        grid_spec=pltpu.PrefetchScalarGridSpec(
            num_scalar_prefetch=1,
            grid=(blocks,),
            in_specs=[pl.BlockSpec((rows, size), lambda z, core_ref: (0, 2 * z + 1 - core_ref[0]))],
            out_specs=pl.BlockSpec((1, rows, size), lambda z, core_ref: (z, 0, 0)),
        ),
        cost_estimate=pl.CostEstimate(flops=0, bytes_accessed=3 * rows * width, transcendentals=0),
        name="pick_columns",
    )(core, tokens)


def narrow_kernel(in_ref, out_ref):
    out_ref[...] = in_ref[...].astype(BF16)


def narrow(blocks):
    spec = pl.BlockSpec((1,) + blocks.shape[1:], lambda z: (z, 0, 0))
    return pl.pallas_call(
        narrow_kernel,
        out_shape=jax.ShapeDtypeStruct(blocks.shape, BF16),
        grid=(blocks.shape[0],),
        in_specs=[spec],
        out_specs=spec,
        cost_estimate=pl.CostEstimate(flops=0, bytes_accessed=6 * blocks.size, transcendentals=0),
        name="narrow",
    )(blocks)


def gradient_kernel(order, place_ref, own0, own1, far0, far1, tokens_ref, other_ref, *rest):
    outs, left_ref = rest[:-1], rest[-1]
    core, group = place_ref[0], place_ref[1]
    half, dim, rows = own0.shape
    middle = dim // 2

    @pl.when(pl.program_id(0) == 0)
    def _():
        for i in range(half):
            near, away = (core * half + i) ^ group, ((1 - core) * half + i) ^ group
            left_ref[near, :, 0:rows] = own0[i].astype(BF16)
            left_ref[away, :, 0:rows] = own1[i].astype(BF16)
            left_ref[near, :, rows:] = far1[i].astype(BF16)
            left_ref[away, :, rows:] = far0[i].astype(BF16)

    left = left_ref[...].reshape(2 * half * dim, 2 * rows)
    result = dot(left, jnp.concatenate([tokens_ref[...], other_ref[0]], axis=0))
    for d in range(2 * half):
        for path in range(2):
            which, index = order[path][d]
            start = d * dim + path * middle
            outs[2 * path + which][index, 0] = result[start : start + middle]


def gradient_blocks(place, own, far, tokens, other, order):
    half, dim, rows = own[0].shape
    blocks, _, size = other.shape
    out = jax.ShapeDtypeStruct((half, blocks, dim // 2, size), F32)
    turned_spec = pl.BlockSpec((half, dim, rows), lambda z, p: (0, 0, 0))
    return pl.pallas_call(
        functools.partial(gradient_kernel, order),
        out_shape=[out] * 4,
        grid_spec=pltpu.PrefetchScalarGridSpec(
            num_scalar_prefetch=1,
            grid=(blocks,),
            in_specs=[turned_spec] * 4
            + [
                pl.BlockSpec((rows, size), lambda z, p: (0, 2 * (p[2] ^ z) + p[0])),
                pl.BlockSpec((1, rows, size), lambda z, p: (p[2] ^ z, 0, 0)),
            ],
            out_specs=[pl.BlockSpec((half, 1, dim // 2, size), lambda z, p: (0, z, 0, 0))] * 4,
            scratch_shapes=[pltpu.VMEM((2 * half, dim, 2 * rows), BF16)],
        ),
        cost_estimate=pl.CostEstimate(
            flops=8 * half * dim * rows * blocks * size,
            bytes_accessed=4 * (4 * half * dim * rows + blocks * rows * size + 2 * half * blocks * dim * size),
            transcendentals=0,
        ),
        name="gradient_blocks",
    )(place, *own, *far, tokens, other)


def bit_order(bits):
    table = []
    for d in range(1 << len(bits)):
        code = 0
        for bit in bits:
            code = 2 * code + ((d >> bit) & 1)
        table.append(divmod(code, 1 << (len(bits) - 1)))
    return table


def per_device(sizes, tokens, w_query, keys, values, log_decay, regular, grad_out):
    groups, steps = sizes["dp"], sizes["seq"]
    chips = steps // 2
    heads = log_decay.shape[1]
    rows, width = tokens.shape[1:]
    columns = keys.shape[2]
    dim = columns // heads
    per = heads // groups
    half = groups // 2
    tokens, keys, values, grads, decay = tokens[0], keys[0], values[0], grad_out[0], log_decay[0]
    here = lax.axis_index("seq")
    core = here % 2
    core_row = core.reshape(1).astype(jnp.int32)
    partner = [(i, i ^ 1) for i in range(steps)]
    is_first = core == 0

    def decay_of(state):
        return state[:, 2 * dim : 2 * dim + 1, :]

    def join(earlier, later):
        body = lax.broadcasted_iota(jnp.int32, later.shape, 1) < 2 * dim
        return decay_of(later) * earlier + jnp.where(body, later, 0.0)

    locals_, tables = [], []
    for k in range(per):
        near, away, table = local_states(core_row, keys, values, decay, half, per, k)
        locals_.append((near, lax.ppermute(away, "seq", partner)))
        tables.append(table)

    befores = []
    for own, came in locals_:
        chip_state = join(jnp.where(is_first, own, came), jnp.where(is_first, came, own))
        window, before = 0, None
        while window < chips - 1:
            sent = chip_state if before is None else join(before, chip_state)
            shift = 2 * (window + 1)
            moved = lax.ppermute(sent, "seq", [(i, i + shift) for i in range(steps - shift)])
            before = moved if before is None else join(moved, before)
            window = 2 * window + 1
        befores.append(before)
    starts = []
    for (own, came), before in zip(locals_, befores):
        early = jnp.where(is_first, own, came)
        after = join(before, early)
        mine = jnp.where(is_first, before, after)
        starts.append((mine, lax.ppermute(jnp.where(is_first, after, before), "seq", partner)))

    other = narrow(lax.ppermute(pick_columns(core_row, tokens, chips), "seq", partner))
    queries = jnp.dot(tokens, w_query, preferred_element_type=F32).astype(BF16)

    dp_bits = groups.bit_length() - 1
    paths = [list(range(dp_bits)), list(reversed(range(dp_bits)))]
    order = [bit_order(path) for path in paths]
    place = jnp.stack([core, lax.axis_index("dp"), here // 2]).astype(jnp.int32)

    turned, mixed = {}, None

    def solve(k, side, mixed, after):
        block = core if side == 0 else 1 - core
        first = jnp.stack([block * half * per + k, jnp.full_like(core, per)]).astype(jnp.int32)
        mixed, out = solve_heads(
            first, regular, queries, keys, values, grads, tables[k], starts[k][side], mixed, after
        )
        turned[k, side] = (out, lax.ppermute(out, "seq", partner))
        return mixed

    def gradient(k):
        own = [turned[k, side][0] for side in range(2)]
        far = [turned[k, side][1] for side in range(2)]
        return gradient_blocks(place, own, far, tokens, other, order)

    products = []
    for k in range(per):
        mixed = solve(k, 0, mixed, None)
        if k > 0:
            products.append(gradient(k - 1))
        mixed = solve(k, 1, mixed, products[-1][0] if k > 0 else None)
    products.append(gradient(per - 1))

    finished = []
    for blocks in products:
        parts = []
        for index, path in enumerate(paths):
            keep, send = blocks[2 * index], blocks[2 * index + 1]
            for bit in path:
                total = keep + lax.ppermute(send, "dp", [(i, i ^ (1 << bit)) for i in range(groups)])
                middle = total.shape[0] // 2
                keep, send = total[:middle], total[middle:]
            parts.append(total[0])
        total = jnp.concatenate(parts, axis=1)
        out = total[0]
        for z in range(1, chips):
            out = out + lax.ppermute(total[z], "seq", [(i, i ^ (2 * z)) for i in range(steps)])
        finished.append(out)
    return mixed[None], jnp.concatenate(finished, axis=0)


def solution(mesh):
    sizes = dict(mesh.shape)
    in_specs = (
        P("dp", "seq", None),
        P(),
        P("dp", "seq", None),
        P("dp", "seq", None),
        P("dp", None, "seq"),
        P(),
        P("dp", "seq", None),
    )
    out_specs = (P("dp", "seq", None), P("dp", "seq"))
    return jax.shard_map(
        functools.partial(per_device, sizes),
        mesh=mesh,
        in_specs=in_specs,
        out_specs=out_specs,
        check_vma=False,
    )
```

```python
import functools

import jax
import jax.numpy as jnp
from jax import lax
from jax.experimental import pallas as pl
from jax.experimental.pallas import tpu as pltpu
from jax.sharding import PartitionSpec as P

ITERS = 4
SUB = 128
EXTRA = 8


F32 = jnp.float32
BF16 = jnp.bfloat16


def dot(left, right):
    return jnp.dot(left, right, preferred_element_type=F32)


def split(value):
    high = value.astype(BF16)
    low = (value - high.astype(F32)).astype(BF16)
    return high, low


def wide(value, axis=1):
    return jnp.concatenate(split(value), axis=axis)


def lane_shift(value, step):
    lanes = lax.broadcasted_iota(jnp.int32, value.shape, 1)
    return jnp.where(lanes >= step, pltpu.roll(value, step, 1), 0.0), lanes >= step


def cumulative_rows(value):
    step = 1
    while step < value.shape[1]:
        value = value + lane_shift(value, step)[0]
        step *= 2
    return value


def decayed_rows(value, cumulative):
    step = 1
    while step < value.shape[1]:
        earlier, inside = lane_shift(cumulative, step)
        factor = jnp.exp(jnp.where(inside, cumulative - earlier, 0.0))
        value = value + factor * lane_shift(value, step)[0]
        step *= 2
    return value


def decay_tables(decay_ref):
    rows = decay_ref.shape[1]
    offset = jnp.zeros((decay_ref.shape[0], 1), F32)
    local, full = [], []
    for c in range(rows // SUB):
        part = cumulative_rows(decay_ref[:, c * SUB : (c + 1) * SUB])
        local.append(part)
        full.append(part + offset)
        offset = offset + part[:, SUB - 1 : SUB]
    return local, jnp.exp(offset - jnp.concatenate(full, axis=1)), jnp.exp(offset)


def states_kernel(half, per, k, core_ref, keys_ref, values_ref, decay_ref, near_ref, away_ref, table_ref, work_ref):
    rows, dim = keys_ref.shape[0], SUB
    core = core_ref[0]
    local, tails, total = decay_tables(decay_ref)
    work_ref[0] = tails
    work_ref[2] = jnp.broadcast_to(total, tails.shape)
    work_ref[1] = jnp.zeros_like(tails)
    for out, block in ((away_ref, 1 - core), (near_ref, core)):
        for i in range(half):
            head = (block * half + i) * per + k
            column = pl.ds(pl.multiple_of(head * dim, dim), dim)
            key = keys_ref[:, column]
            tail = work_ref[0, pl.ds(head, 1), :]
            key_turned = key.astype(F32).T
            value_turned = values_ref[:, column].astype(F32).T
            work_ref[1, pl.ds(head, 1), :] = jnp.sum(key_turned * key_turned, axis=0, keepdims=True)
            high, low = split(jnp.concatenate([key_turned * tail, value_turned * tail], axis=0))
            out[i, 0 : 2 * dim, :] = dot(high, key) + dot(low, key)
            decay = work_ref[2, pl.ds(head, 1), :][:, 0:SUB]
            out[i, 2 * dim : 2 * dim + EXTRA, :] = jnp.broadcast_to(decay, (EXTRA, dim))
    carry = jnp.zeros_like(total)
    for c in range(rows // SUB):
        lanes = slice(c * SUB, (c + 1) * SUB)
        part = decayed_rows(work_ref[1, :, lanes], local[c]) + jnp.exp(local[c]) * carry
        table_ref[0, :, lanes] = local[c]
        table_ref[1, :, lanes] = part
        carry = part[:, SUB - 1 : SUB]


def local_states(core, keys, values, decay, half, per, k):
    rows, columns = keys.shape
    heads = decay.shape[0]
    dim = columns // heads
    state = jax.ShapeDtypeStruct((half, 2 * dim + EXTRA, dim), F32)
    vmem = pl.BlockSpec(memory_space=pltpu.VMEM)
    return pl.pallas_call(
        functools.partial(states_kernel, half, per, k),
        out_shape=[state, state, jax.ShapeDtypeStruct((2, heads, rows), F32)],
        in_specs=[pl.BlockSpec(memory_space=pltpu.SMEM)] + [vmem] * 3,
        out_specs=[vmem] * 3,
        scratch_shapes=[pltpu.VMEM((3, heads, rows), F32)],
        cost_estimate=pl.CostEstimate(
            flops=16 * rows * dim * dim * half, bytes_accessed=8 * rows * columns, transcendentals=0
        ),
        name="local_states",
    )(core, keys, values, decay)


def solve_kernel(
    first_ref, regular_ref, q_ref, k_ref, v_ref, g_ref, rows_ref, state_ref, *rest
):
    mixed_ref, turned_ref = rest[-2:]
    rows, dim = q_ref.shape
    pieces = range(rows // SUB)
    place = [slice(c * SUB, (c + 1) * SUB) for c in pieces]
    step = pl.program_id(0)
    head = first_ref[0] + step * first_ref[1]
    ridge = regular_ref[head]
    row_at = lax.broadcasted_iota(jnp.int32, (SUB, SUB), 0)
    column_at = lax.broadcasted_iota(jnp.int32, (SUB, SUB), 1)
    lower = row_at >= column_at

    gram = [state_ref[0, 0:dim, :]]
    memory = [state_ref[0, dim : 2 * dim, :]]
    start_trace = jnp.sum(jnp.where(row_at == column_at, gram[0], 0.0), axis=0, keepdims=True)
    start_trace = jnp.sum(start_trace, axis=1, keepdims=True)
    cumulative_row = rows_ref[0, pl.ds(head, 1), :]
    cumulative = [cumulative_row[:, at] for at in place]
    last = [row[:, SUB - 1 : SUB] for row in cumulative]
    whole, offset = [], jnp.zeros((1, 1), F32)
    for c in pieces:
        whole.append(cumulative[c] + offset)
        offset = offset + last[c]
    trace = jnp.exp(jnp.concatenate(whole, axis=1)) * start_trace + rows_ref[1, pl.ds(head, 1), :]
    half = 0.5 * trace
    center = ridge + half
    alphas, gammas = [1.0 / center], []
    for i in range(1, ITERS):
        factor = 0.5 if i == 1 else 0.25
        product = half * alphas[-1]
        alphas.append(1.0 / (center - factor * half * product))
        gammas.append(alphas[-1] * (factor * half * product))
    table = jnp.concatenate(alphas + gammas + [cumulative_row], axis=0).T

    def column(index):
        return [jnp.broadcast_to(table[at, index : index + 1], (SUB, SUB)) for at in place]

    rise = column(2 * ITERS - 1)
    weights = [
        jnp.where(lower, jnp.exp(jnp.where(lower, rise[c] - cumulative[c], 0.0)), 0.0) for c in pieces
    ]
    scale = [jnp.exp(r) for r in rise]

    keys = [k_ref[at, :] for at in place]
    values = [v_ref[at, :] for at in place]
    keys_turned = [key.astype(F32).T for key in keys]
    values_turned = [value.astype(F32).T for value in values]
    for c in pieces[:-1]:
        tail = jnp.exp(last[c] - cumulative[c])
        decay = jnp.exp(last[c])
        both = jnp.concatenate([keys_turned[c] * tail, values_turned[c] * tail], axis=0)
        grown = dot(wide(both), jnp.concatenate([keys[c], keys[c]], axis=0))
        gram.append(decay * gram[-1] + grown[0:dim])
        memory.append(decay * memory[-1] + grown[dim:])
    keys_turned = [key.astype(BF16) for key in keys_turned]
    values_turned = [value.astype(BF16) for value in values_turned]

    def pair(left, right):
        return jnp.concatenate([left, right], axis=0)

    residual = []
    for c in pieces:
        grad = g_ref[place[c], :]
        pulled = scale[c] * dot(jnp.concatenate([grad, grad], axis=1), wide(memory[c], 0))
        score = weights[c] * dot(grad, values_turned[c])
        pulled = pulled + dot(wide(score), pair(keys[c], keys[c]))
        residual.append(pair(q_ref[place[c], :].astype(F32), pulled))

    alpha = column(0)
    change = [pair(alpha[c], alpha[c]) * residual[c] for c in pieces]
    solution = list(change)
    rights = [jnp.concatenate([keys_turned[c], gram[c].astype(BF16)], axis=1) for c in pieces]
    for i in range(1, ITERS):
        alpha, gamma = column(i), column(ITERS + i - 1)
        first = [dot(change[c].astype(BF16), rights[c]) for c in pieces]
        second = [
            dot((first[c][:, 0:SUB] * pair(weights[c], weights[c])).astype(BF16), keys[c]) for c in pieces
        ]
        for c in pieces:
            applied = ridge * change[c] + (pair(scale[c], scale[c]) * first[c][:, SUB:] + second[c])
            residual[c] = residual[c] - applied
            change[c] = pair(alpha[c], alpha[c]) * residual[c] + pair(gamma[c], gamma[c]) * change[c]
            solution[c] = solution[c] + change[c]

    for c in pieces:
        turned_ref[0, :, place[c]] = solution[c][SUB:].T.astype(BF16).astype(F32)
    for c in pieces:
        high, low = split(solution[c][0:SUB])
        memory_high, memory_low = split(memory[c].T)
        right = jnp.concatenate([keys_turned[c], memory_high], axis=1)
        first = dot(jnp.concatenate([high, low], axis=1), pair(right, right))
        second = first[:, SUB:] + dot(high, memory_low)
        score = weights[c] * first[:, 0:SUB]
        output = scale[c] * second + dot(wide(score), pair(values[c], values[c]))
        mixed_ref[place[c], :] = output.astype(BF16)


def solve_heads(first, regular, queries, keys, values, grads, table, states, mixed, after):
    rows, columns = keys.shape
    heads = regular.shape[0]
    dim = columns // heads
    count = states.shape[0]

    def at_head(step, first_ref, regular_ref):
        return (0, first_ref[0] + step * first_ref[1])

    wide_spec = pl.BlockSpec((rows, dim), at_head)
    operands = [queries, keys, values, grads, table, states]
    in_specs = [wide_spec] * 4 + [pl.BlockSpec(table.shape, lambda step, *_: (0, 0, 0))]
    in_specs.append(pl.BlockSpec((1,) + states.shape[1:], lambda step, *_: (step, 0, 0)))
    aliases = {}
    if mixed is not None:
        operands.append(mixed)
        in_specs.append(pl.BlockSpec(memory_space=pl.ANY))
        aliases = {2 + len(operands) - 1: 0}
    if after is not None:
        operands.append(after)
        in_specs.append(pl.BlockSpec(memory_space=pl.ANY))
    return pl.pallas_call(
        solve_kernel,
        out_shape=[
            jax.ShapeDtypeStruct((rows, columns), BF16),
            jax.ShapeDtypeStruct((count, dim, rows), F32),
        ],
        grid_spec=pltpu.PrefetchScalarGridSpec(
            num_scalar_prefetch=2,
            grid=(count,),
            in_specs=in_specs,
            out_specs=[wide_spec, pl.BlockSpec((1, dim, rows), lambda step, *_: (step, 0, 0))],
        ),
        input_output_aliases=aliases,
        cost_estimate=pl.CostEstimate(
            flops=count * 80 * rows * dim * dim, bytes_accessed=count * 14 * rows * dim, transcendentals=0
        ),
        name="solve_heads",
    )(first, regular, *operands)


def pick_kernel(core_ref, tokens_ref, out_ref):
    out_ref[0] = tokens_ref[...].astype(F32)


def pick_columns(core, tokens, blocks):
    rows, width = tokens.shape
    size = width // (2 * blocks)
    return pl.pallas_call(
        pick_kernel,
        out_shape=jax.ShapeDtypeStruct((blocks, rows, size), F32),
        grid_spec=pltpu.PrefetchScalarGridSpec(
            num_scalar_prefetch=1,
            grid=(blocks,),
            in_specs=[pl.BlockSpec((rows, size), lambda z, core_ref: (0, 2 * z + 1 - core_ref[0]))],
            out_specs=pl.BlockSpec((1, rows, size), lambda z, core_ref: (z, 0, 0)),
        ),
        cost_estimate=pl.CostEstimate(flops=0, bytes_accessed=3 * rows * width, transcendentals=0),
        name="pick_columns",
    )(core, tokens)


def narrow_kernel(in_ref, out_ref):
    out_ref[...] = in_ref[...].astype(BF16)


def narrow(blocks):
    spec = pl.BlockSpec((1,) + blocks.shape[1:], lambda z: (z, 0, 0))
    return pl.pallas_call(
        narrow_kernel,
        out_shape=jax.ShapeDtypeStruct(blocks.shape, BF16),
        grid=(blocks.shape[0],),
        in_specs=[spec],
        out_specs=spec,
        cost_estimate=pl.CostEstimate(flops=0, bytes_accessed=6 * blocks.size, transcendentals=0),
        name="narrow",
    )(blocks)


def gradient_kernel(order, place_ref, own0, own1, far0, far1, tokens_ref, other_ref, *rest):
    outs, left_ref = rest[:-1], rest[-1]
    core, group = place_ref[0], place_ref[1]
    half, dim, rows = own0.shape
    middle = dim // 2

    @pl.when(pl.program_id(0) == 0)
    def _():
        for i in range(half):
            near, away = (core * half + i) ^ group, ((1 - core) * half + i) ^ group
            left_ref[near, :, 0:rows] = own0[i].astype(BF16)
            left_ref[away, :, 0:rows] = own1[i].astype(BF16)
            left_ref[near, :, rows:] = far1[i].astype(BF16)
            left_ref[away, :, rows:] = far0[i].astype(BF16)

    left = left_ref[...].reshape(2 * half * dim, 2 * rows)
    result = dot(left, jnp.concatenate([tokens_ref[...], other_ref[0]], axis=0))
    for d in range(2 * half):
        for path in range(2):
            which, index = order[path][d]
            start = d * dim + path * middle
            outs[2 * path + which][index, 0] = result[start : start + middle]


def gradient_blocks(place, own, far, tokens, other, order):
    half, dim, rows = own[0].shape
    blocks, _, size = other.shape
    out = jax.ShapeDtypeStruct((half, blocks, dim // 2, size), F32)
    turned_spec = pl.BlockSpec((half, dim, rows), lambda z, p: (0, 0, 0))
    return pl.pallas_call(
        functools.partial(gradient_kernel, order),
        out_shape=[out] * 4,
        grid_spec=pltpu.PrefetchScalarGridSpec(
            num_scalar_prefetch=1,
            grid=(blocks,),
            in_specs=[turned_spec] * 4
            + [
                pl.BlockSpec((rows, size), lambda z, p: (0, 2 * (p[2] ^ z) + p[0])),
                pl.BlockSpec((1, rows, size), lambda z, p: (p[2] ^ z, 0, 0)),
            ],
            out_specs=[pl.BlockSpec((half, 1, dim // 2, size), lambda z, p: (0, z, 0, 0))] * 4,
            scratch_shapes=[pltpu.VMEM((2 * half, dim, 2 * rows), BF16)],
        ),
        cost_estimate=pl.CostEstimate(
            flops=8 * half * dim * rows * blocks * size,
            bytes_accessed=4 * (4 * half * dim * rows + blocks * rows * size + 2 * half * blocks * dim * size),
            transcendentals=0,
        ),
        name="gradient_blocks",
    )(place, *own, *far, tokens, other)


def bit_order(bits):
    table = []
    for d in range(1 << len(bits)):
        code = 0
        for bit in bits:
            code = 2 * code + ((d >> bit) & 1)
        table.append(divmod(code, 1 << (len(bits) - 1)))
    return table


def per_device(sizes, *arrays):
    return program(sizes, *arrays)


def program(sizes, tokens, w_query, keys, values, log_decay, regular, grad_out):
    groups, steps = sizes["dp"], sizes["seq"]
    chips = steps // 2
    heads = log_decay.shape[1]
    columns = keys.shape[2]
    dim = columns // heads
    per = heads // groups
    half = groups // 2
    tokens, keys, values, grads, decay = tokens[0], keys[0], values[0], grad_out[0], log_decay[0]
    here = lax.axis_index("seq")
    core = here % 2
    core_row = core.reshape(1).astype(jnp.int32)
    partner = [(i, i ^ 1) for i in range(steps)]
    is_first = core == 0

    def decay_of(state):
        return state[:, 2 * dim : 2 * dim + 1, :]

    def join(earlier, later):
        body = lax.broadcasted_iota(jnp.int32, later.shape, 1) < 2 * dim
        return decay_of(later) * earlier + jnp.where(body, later, 0.0)

    locals_, tables = [], []
    for k in range(per):
        near, away, table = local_states(core_row, keys, values, decay, half, per, k)
        locals_.append((near, lax.ppermute(away, "seq", partner)))
        tables.append(table)

    befores = []
    for own, came in locals_:
        chip_state = join(jnp.where(is_first, own, came), jnp.where(is_first, came, own))
        window, before = 0, None
        while window < chips - 1:
            sent = chip_state if before is None else join(before, chip_state)
            shift = 2 * (window + 1)
            pairs = [(i, i + shift) for i in range(steps - shift)]
            came_up = lax.ppermute(sent, "seq", pairs)
            before = came_up if before is None else join(came_up, before)
            window = 2 * window + 1
        befores.append(before)
    starts = []
    for (own, came), before in zip(locals_, befores):
        early = jnp.where(is_first, own, came)
        after = join(before, early)
        mine = jnp.where(is_first, before, after)
        starts.append((mine, lax.ppermute(jnp.where(is_first, after, before), "seq", partner)))

    picked = pick_columns(core_row, tokens, chips)
    other = lax.ppermute(picked, "seq", partner)
    other = narrow(other)
    queries = jnp.dot(tokens, w_query, preferred_element_type=F32).astype(BF16)

    dp_bits = groups.bit_length() - 1
    paths = [list(range(dp_bits)), list(reversed(range(dp_bits)))]
    order = [bit_order(path) for path in paths]
    place = jnp.stack([core, lax.axis_index("dp"), here // 2]).astype(jnp.int32)

    turned, mixed = {}, None

    def solve(k, side, mixed, after):
        block = core if side == 0 else 1 - core
        first = jnp.stack([block * half * per + k, jnp.full_like(core, per)]).astype(jnp.int32)
        mixed, out = solve_heads(
            first, regular, queries, keys, values, grads, tables[k], starts[k][side], mixed, after
        )
        turned[k, side] = (out, lax.ppermute(out, "seq", partner))
        return mixed

    def gradient(k):
        own = [turned[k, side][0] for side in range(2)]
        far = [turned[k, side][1] for side in range(2)]
        return gradient_blocks(place, own, far, tokens, other, order)

    products = []
    for k in range(per):
        mixed = solve(k, 0, mixed, None)
        if k > 0:
            products.append(gradient(k - 1))
        mixed = solve(k, 1, mixed, products[-1][0] if k > 0 else None)
    products.append(gradient(per - 1))

    finished = []
    for blocks in products:
        parts = []
        for index, path in enumerate(paths):
            keep, send = blocks[2 * index], blocks[2 * index + 1]
            for bit in path:
                pairs = [(i, i ^ (1 << bit)) for i in range(groups)]
                total = keep + lax.ppermute(send, "dp", pairs)
                middle = total.shape[0] // 2
                keep, send = total[:middle], total[middle:]
            parts.append(total[0])
        total = jnp.concatenate(parts, axis=1)
        out = total[0]
        for z in range(1, chips):
            out = out + lax.ppermute(total[z], "seq", [(i, i ^ (2 * z)) for i in range(steps)])
        finished.append(out)
    return mixed[None], jnp.concatenate(finished, axis=0)


def solution(mesh):
    sizes = dict(mesh.shape)
    in_specs = (
        P("dp", "seq", None),
        P(),
        P("dp", "seq", None),
        P("dp", "seq", None),
        P("dp", None, "seq"),
        P(),
        P("dp", "seq", None),
    )
    out_specs = (P("dp", "seq", None), P("dp", "seq"))
    return jax.shard_map(
        functools.partial(per_device, sizes),
        mesh=mesh,
        in_specs=in_specs,
        out_specs=out_specs,
        check_vma=False,
    )
```

```python
import functools

import jax
import jax.numpy as jnp
from jax import lax
from jax.experimental import pallas as pl
from jax.experimental.pallas import tpu as pltpu
from jax.sharding import PartitionSpec as P

ITERS = 4
SUB = 128
EXTRA = 8


F32 = jnp.float32
BF16 = jnp.bfloat16


def dot(left, right):
    return jnp.dot(left, right, preferred_element_type=F32)


def split(value):
    high = value.astype(BF16)
    low = (value - high.astype(F32)).astype(BF16)
    return high, low


def wide(value, axis=1):
    return jnp.concatenate(split(value), axis=axis)


def lane_shift(value, step):
    lanes = lax.broadcasted_iota(jnp.int32, value.shape, 1)
    return jnp.where(lanes >= step, pltpu.roll(value, step, 1), 0.0), lanes >= step


def cumulative_rows(value):
    step = 1
    while step < value.shape[1]:
        value = value + lane_shift(value, step)[0]
        step *= 2
    return value


def decayed_rows(value, cumulative):
    step = 1
    while step < value.shape[1]:
        earlier, inside = lane_shift(cumulative, step)
        factor = jnp.exp(jnp.where(inside, cumulative - earlier, 0.0))
        value = value + factor * lane_shift(value, step)[0]
        step *= 2
    return value


def decay_tables(decay_ref):
    rows = decay_ref.shape[1]
    offset = jnp.zeros((decay_ref.shape[0], 1), F32)
    local, full = [], []
    for c in range(rows // SUB):
        part = cumulative_rows(decay_ref[:, c * SUB : (c + 1) * SUB])
        local.append(part)
        full.append(part + offset)
        offset = offset + part[:, SUB - 1 : SUB]
    return local, jnp.exp(offset - jnp.concatenate(full, axis=1)), jnp.exp(offset)


def states_kernel(half, per, k, core_ref, keys_ref, values_ref, decay_ref, near_ref, away_ref, table_ref, work_ref):
    rows, dim = keys_ref.shape[0], SUB
    core = core_ref[0]
    row_at = lax.broadcasted_iota(jnp.int32, (dim, dim), 0)
    column_at = lax.broadcasted_iota(jnp.int32, (dim, dim), 1)
    local, tails, total = decay_tables(decay_ref)
    work_ref[0] = tails
    work_ref[2] = jnp.broadcast_to(total, tails.shape)
    work_ref[1] = jnp.zeros_like(tails)
    for out, block in ((away_ref, 1 - core), (near_ref, core)):
        for i in range(half):
            head = (block * half + i) * per + k
            column = pl.ds(pl.multiple_of(head * dim, dim), dim)
            key = keys_ref[:, column]
            tail = work_ref[0, pl.ds(head, 1), :]
            key_turned = key.astype(F32).T
            value_turned = values_ref[:, column].astype(F32).T
            work_ref[1, pl.ds(head, 1), :] = jnp.sum(key_turned * key_turned, axis=0, keepdims=True)
            high, low = split(jnp.concatenate([key_turned * tail, value_turned * tail], axis=0))
            state = dot(high, key) + dot(low, key)
            gram = state[0:dim]
            at, second = i // 2, i % 2
            out[at, (1 + second) * dim : (2 + second) * dim, :] = state[dim:]
            out[at, 3 * dim + second : 3 * dim + second + 1, :] = work_ref[2, pl.ds(head, 1), :][:, 0:SUB]
            if second == 0:
                first_gram = gram
            else:
                out[at, 0:dim, :] = jnp.where(row_at <= column_at, first_gram, gram)
                diagonal = jnp.sum(jnp.where(row_at == column_at, gram, 0.0), axis=0, keepdims=True)
                out[at, 3 * dim + 2 : 3 * dim + 3, :] = diagonal
                out[at, 3 * dim + 3 :, :] = jnp.zeros((EXTRA - 3, dim), F32)
    carry = jnp.zeros_like(total)
    for c in range(rows // SUB):
        lanes = slice(c * SUB, (c + 1) * SUB)
        part = decayed_rows(work_ref[1, :, lanes], local[c]) + jnp.exp(local[c]) * carry
        table_ref[0, :, lanes] = local[c]
        table_ref[1, :, lanes] = part
        carry = part[:, SUB - 1 : SUB]


def local_states(core, keys, values, decay, half, per, k):
    rows, columns = keys.shape
    heads = decay.shape[0]
    dim = columns // heads
    state = jax.ShapeDtypeStruct((half // 2, 3 * dim + EXTRA, dim), F32)
    vmem = pl.BlockSpec(memory_space=pltpu.VMEM)
    return pl.pallas_call(
        functools.partial(states_kernel, half, per, k),
        out_shape=[state, state, jax.ShapeDtypeStruct((2, heads, rows), F32)],
        in_specs=[pl.BlockSpec(memory_space=pltpu.SMEM)] + [vmem] * 3,
        out_specs=[vmem] * 3,
        scratch_shapes=[pltpu.VMEM((3, heads, rows), F32)],
        cost_estimate=pl.CostEstimate(
            flops=16 * rows * dim * dim * half, bytes_accessed=8 * rows * columns, transcendentals=0
        ),
        name="local_states",
    )(core, keys, values, decay)


def join(earlier, later, dim):
    row_at = lax.broadcasted_iota(jnp.int32, later.shape, 1)
    column_at = lax.broadcasted_iota(jnp.int32, later.shape, 2)
    is_first = (row_at < dim) & (row_at <= column_at) | (row_at >= dim) & (row_at < 2 * dim)
    is_first = is_first | (row_at == 3 * dim)
    is_decay = (row_at == 3 * dim) | (row_at == 3 * dim + 1)
    factor = jnp.where(is_first, later[:, 3 * dim : 3 * dim + 1], later[:, 3 * dim + 1 : 3 * dim + 2])
    return factor * earlier + jnp.where(is_decay, 0.0, later)


def chip_kernel(dim, place_ref, own_ref, came_ref, out_ref):
    is_first = place_ref[0] == 0
    own, came = own_ref[...], came_ref[...]
    out_ref[...] = join(jnp.where(is_first, own, came), jnp.where(is_first, came, own), dim)


def join_kernel(dim, place_ref, earlier_ref, later_ref, out_ref):
    out_ref[...] = join(earlier_ref[...], later_ref[...], dim)


def start_kernel(dim, place_ref, far_ref, near_ref, own_ref, came_ref, mine_ref, other_ref):
    is_first = place_ref[0] == 0
    before = join(far_ref[...], near_ref[...], dim)
    after = join(before, jnp.where(is_first, own_ref[...], came_ref[...]), dim)
    mine_ref[...] = jnp.where(is_first, before, after)
    other_ref[...] = jnp.where(is_first, after, before)


def combine(kernel, dim, place, *arrays, outs=1):
    vmem = pl.BlockSpec(memory_space=pltpu.VMEM)
    shape = jax.ShapeDtypeStruct(arrays[0].shape, F32)
    results = pl.pallas_call(
        functools.partial(kernel, dim),
        out_shape=[shape] * outs,
        in_specs=[pl.BlockSpec(memory_space=pltpu.SMEM)] + [vmem] * len(arrays),
        out_specs=[vmem] * outs,
        cost_estimate=pl.CostEstimate(
            flops=0, bytes_accessed=4 * arrays[0].size * (len(arrays) + outs), transcendentals=0
        ),
    )(place, *arrays)
    return results[0] if outs == 1 else results


def solve_kernel(
    head_of, place_ref, regular_ref, q_ref, k_ref, v_ref, g_ref, rows_ref, state_ref, *rest
):
    mixed_ref, turned_ref = rest[-2:]
    rows, dim = q_ref.shape
    pieces = range(rows // SUB)
    place = [slice(c * SUB, (c + 1) * SUB) for c in pieces]
    step = pl.program_id(0)
    head = head_of(step, place_ref)
    ridge = regular_ref[head]
    row_at = lax.broadcasted_iota(jnp.int32, (SUB, SUB), 0)
    column_at = lax.broadcasted_iota(jnp.int32, (SUB, SUB), 1)
    lower = row_at >= column_at

    is_second = lax.rem(step, 2) == 1
    packed = state_ref[0, 0:dim, :]
    direct = (row_at > column_at) == is_second
    start = jnp.where(direct, packed, packed.T)
    diagonal = state_ref[0, 3 * dim + 2 : 3 * dim + 3, :]
    gram = [jnp.where((row_at == column_at) & is_second, diagonal, start)]
    memory = [state_ref[0, pl.ds(pl.multiple_of((1 + lax.rem(step, 2)) * dim, dim), dim), :]]
    start_trace = jnp.sum(jnp.where(row_at == column_at, gram[0], 0.0), axis=0, keepdims=True)
    start_trace = jnp.sum(start_trace, axis=1, keepdims=True)
    cumulative_row = rows_ref[0, pl.ds(head, 1), :]
    cumulative = [cumulative_row[:, at] for at in place]
    last = [row[:, SUB - 1 : SUB] for row in cumulative]
    whole, offset = [], jnp.zeros((1, 1), F32)
    for c in pieces:
        whole.append(cumulative[c] + offset)
        offset = offset + last[c]
    trace = jnp.exp(jnp.concatenate(whole, axis=1)) * start_trace + rows_ref[1, pl.ds(head, 1), :]
    half = 0.5 * trace
    center = ridge + half
    alphas, gammas = [1.0 / center], []
    for i in range(1, ITERS):
        factor = 0.5 if i == 1 else 0.25
        product = half * alphas[-1]
        alphas.append(1.0 / (center - factor * half * product))
        gammas.append(alphas[-1] * (factor * half * product))
    table = jnp.concatenate(alphas + gammas + [cumulative_row], axis=0).T

    def column(index):
        return [jnp.broadcast_to(table[at, index : index + 1], (SUB, SUB)) for at in place]

    rise = column(2 * ITERS - 1)
    weights = [
        jnp.where(lower, jnp.exp(jnp.where(lower, rise[c] - cumulative[c], 0.0)), 0.0) for c in pieces
    ]
    scale = [jnp.exp(r) for r in rise]

    keys = [k_ref[at, :] for at in place]
    values = [v_ref[at, :] for at in place]
    keys_turned = [key.astype(F32).T for key in keys]
    values_turned = [value.astype(F32).T for value in values]
    for c in pieces[:-1]:
        tail = jnp.exp(last[c] - cumulative[c])
        decay = jnp.exp(last[c])
        both = jnp.concatenate([keys_turned[c] * tail, values_turned[c] * tail], axis=0)
        grown = dot(wide(both), jnp.concatenate([keys[c], keys[c]], axis=0))
        gram.append(decay * gram[-1] + grown[0:dim])
        memory.append(decay * memory[-1] + grown[dim:])
    keys_turned = [key.astype(BF16) for key in keys_turned]
    values_turned = [value.astype(BF16) for value in values_turned]

    def pair(left, right):
        return jnp.concatenate([left, right], axis=0)

    residual = []
    for c in pieces:
        grad = g_ref[place[c], :]
        pulled = scale[c] * dot(jnp.concatenate([grad, grad], axis=1), wide(memory[c], 0))
        score = weights[c] * dot(grad, values_turned[c])
        pulled = pulled + dot(wide(score), pair(keys[c], keys[c]))
        residual.append(pair(q_ref[place[c], :].astype(F32), pulled))

    alpha = column(0)
    change = [pair(alpha[c], alpha[c]) * residual[c] for c in pieces]
    solution = list(change)
    rights = [jnp.concatenate([keys_turned[c], gram[c].astype(BF16)], axis=1) for c in pieces]
    for i in range(1, ITERS):
        alpha, gamma = column(i), column(ITERS + i - 1)
        first = [dot(change[c].astype(BF16), rights[c]) for c in pieces]
        second = [
            dot((first[c][:, 0:SUB] * pair(weights[c], weights[c])).astype(BF16), keys[c]) for c in pieces
        ]
        for c in pieces:
            applied = ridge * change[c] + (pair(scale[c], scale[c]) * first[c][:, SUB:] + second[c])
            residual[c] = residual[c] - applied
            change[c] = pair(alpha[c], alpha[c]) * residual[c] + pair(gamma[c], gamma[c]) * change[c]
            solution[c] = solution[c] + change[c]

    for c in pieces:
        turned_ref[0, :, place[c]] = solution[c][SUB:].T.astype(BF16).astype(F32)
    for c in pieces:
        high, low = split(solution[c][0:SUB])
        memory_high, memory_low = split(memory[c].T)
        right = jnp.concatenate([keys_turned[c], memory_high], axis=1)
        first = dot(jnp.concatenate([high, low], axis=1), pair(right, right))
        second = first[:, SUB:] + dot(high, memory_low)
        score = weights[c] * first[:, 0:SUB]
        output = scale[c] * second + dot(wide(score), pair(values[c], values[c]))
        mixed_ref[place[c], :] = output.astype(BF16)


def solve_heads(place, k, side, per, regular, queries, keys, values, grads, table, states, mixed, after):
    rows, columns = keys.shape
    heads = regular.shape[0]
    dim = columns // heads
    count = 2 * states.shape[0]

    def head_of(step, place_ref):
        block = place_ref[0] if side == 0 else 1 - place_ref[0]
        return (block * count + step) * per + k

    def at_head(step, place_ref, regular_ref):
        return (0, head_of(step, place_ref))

    wide_spec = pl.BlockSpec((rows, dim), at_head)
    operands = [queries, keys, values, grads, table, states]
    in_specs = [wide_spec] * 4 + [pl.BlockSpec(table.shape, lambda step, *_: (0, 0, 0))]
    in_specs.append(pl.BlockSpec((1,) + states.shape[1:], lambda step, *_: (step // 2, 0, 0)))
    aliases = {}
    if mixed is not None:
        operands.append(mixed)
        in_specs.append(pl.BlockSpec(memory_space=pl.ANY))
        aliases = {2 + len(operands) - 1: 0}
    if after is not None:
        operands.append(after)
        in_specs.append(pl.BlockSpec(memory_space=pl.ANY))
    return pl.pallas_call(
        functools.partial(solve_kernel, head_of),
        out_shape=[
            jax.ShapeDtypeStruct((rows, columns), BF16),
            jax.ShapeDtypeStruct((count, dim, rows), F32),
        ],
        grid_spec=pltpu.PrefetchScalarGridSpec(
            num_scalar_prefetch=2,
            grid=(count,),
            in_specs=in_specs,
            out_specs=[wide_spec, pl.BlockSpec((1, dim, rows), lambda step, *_: (step, 0, 0))],
        ),
        input_output_aliases=aliases,
        cost_estimate=pl.CostEstimate(
            flops=count * 80 * rows * dim * dim, bytes_accessed=count * 14 * rows * dim, transcendentals=0
        ),
        name="solve_heads",
    )(place, regular, *operands)


def pick_kernel(core_ref, tokens_ref, out_ref):
    out_ref[0] = tokens_ref[...].astype(F32)


def pick_columns(core, tokens, blocks):
    rows, width = tokens.shape
    size = width // (2 * blocks)
    return pl.pallas_call(
        pick_kernel,
        out_shape=jax.ShapeDtypeStruct((blocks, rows, size), F32),
        grid_spec=pltpu.PrefetchScalarGridSpec(
            num_scalar_prefetch=1,
            grid=(blocks,),
            in_specs=[pl.BlockSpec((rows, size), lambda z, core_ref: (0, 2 * z + 1 - core_ref[0]))],
            out_specs=pl.BlockSpec((1, rows, size), lambda z, core_ref: (z, 0, 0)),
        ),
        cost_estimate=pl.CostEstimate(flops=0, bytes_accessed=3 * rows * width, transcendentals=0),
        name="pick_columns",
    )(core, tokens)


def narrow_kernel(in_ref, out_ref):
    out_ref[...] = in_ref[...].astype(BF16)


def narrow(blocks):
    spec = pl.BlockSpec((1,) + blocks.shape[1:], lambda z: (z, 0, 0))
    return pl.pallas_call(
        narrow_kernel,
        out_shape=jax.ShapeDtypeStruct(blocks.shape, BF16),
        grid=(blocks.shape[0],),
        in_specs=[spec],
        out_specs=spec,
        cost_estimate=pl.CostEstimate(flops=0, bytes_accessed=6 * blocks.size, transcendentals=0),
        name="narrow",
    )(blocks)


def gradient_kernel(order, place_ref, own0, own1, far0, far1, tokens_ref, other_ref, *rest):
    outs, left_ref = rest[:-1], rest[-1]
    core, group = place_ref[0], place_ref[1]
    half, dim, rows = own0.shape
    middle = dim // 2

    @pl.when(pl.program_id(0) == 0)
    def _():
        for i in range(half):
            near, away = (core * half + i) ^ group, ((1 - core) * half + i) ^ group
            left_ref[near, :, 0:rows] = own0[i].astype(BF16)
            left_ref[away, :, 0:rows] = own1[i].astype(BF16)
            left_ref[near, :, rows:] = far1[i].astype(BF16)
            left_ref[away, :, rows:] = far0[i].astype(BF16)

    left = left_ref[...].reshape(2 * half * dim, 2 * rows)
    result = dot(left, jnp.concatenate([tokens_ref[...], other_ref[0]], axis=0))
    for d in range(2 * half):
        for path in range(2):
            which, index = order[path][d]
            start = d * dim + path * middle
            outs[2 * path + which][index, 0] = result[start : start + middle]


def gradient_blocks(place, own, far, tokens, other, order):
    half, dim, rows = own[0].shape
    blocks, _, size = other.shape
    out = jax.ShapeDtypeStruct((half, blocks, dim // 2, size), F32)
    turned_spec = pl.BlockSpec((half, dim, rows), lambda z, p: (0, 0, 0))
    return pl.pallas_call(
        functools.partial(gradient_kernel, order),
        out_shape=[out] * 4,
        grid_spec=pltpu.PrefetchScalarGridSpec(
            num_scalar_prefetch=1,
            grid=(blocks,),
            in_specs=[turned_spec] * 4
            + [
                pl.BlockSpec((rows, size), lambda z, p: (0, 2 * (p[2] ^ z) + p[0])),
                pl.BlockSpec((1, rows, size), lambda z, p: (p[2] ^ z, 0, 0)),
            ],
            out_specs=[pl.BlockSpec((half, 1, dim // 2, size), lambda z, p: (0, z, 0, 0))] * 4,
            scratch_shapes=[pltpu.VMEM((2 * half, dim, 2 * rows), BF16)],
        ),
        cost_estimate=pl.CostEstimate(
            flops=8 * half * dim * rows * blocks * size,
            bytes_accessed=4 * (4 * half * dim * rows + blocks * rows * size + 2 * half * blocks * dim * size),
            transcendentals=0,
        ),
        name="gradient_blocks",
    )(place, *own, *far, tokens, other)


def bit_order(bits):
    table = []
    for d in range(1 << len(bits)):
        code = 0
        for bit in bits:
            code = 2 * code + ((d >> bit) & 1)
        table.append(divmod(code, 1 << (len(bits) - 1)))
    return table


def per_device(sizes, *arrays):
    return program(sizes, *arrays)


def program(sizes, tokens, w_query, keys, values, log_decay, regular, grad_out):
    groups, steps = sizes["dp"], sizes["seq"]
    chips = steps // 2
    heads = log_decay.shape[1]
    columns = keys.shape[2]
    dim = columns // heads
    per = heads // groups
    half = groups // 2
    tokens, keys, values, grads, decay = tokens[0], keys[0], values[0], grad_out[0], log_decay[0]
    here = lax.axis_index("seq")
    core = here % 2
    place = jnp.stack([core, lax.axis_index("dp"), here // 2]).astype(jnp.int32)
    partner = [(i, i ^ 1) for i in range(steps)]

    locals_, tables = [], []
    for k in range(per):
        near, away, table = local_states(place, keys, values, decay, half, per, k)
        locals_.append((near, lax.ppermute(away, "seq", partner)))
        tables.append(table)

    starts = []
    for own, came in locals_:
        chip_state = combine(chip_kernel, dim, place, own, came)
        window, near, far = 0, None, None
        while window < chips - 1:
            if far is not None:
                near = combine(join_kernel, dim, place, far, near)
            sent = chip_state if near is None else combine(join_kernel, dim, place, near, chip_state)
            shift = 2 * (window + 1)
            pairs = [(i, i + shift) for i in range(steps - shift)]
            came_up = lax.ppermute(sent, "seq", pairs)
            near, far = (came_up, None) if near is None else (near, came_up)
            window = 2 * window + 1
        mine, others = combine(start_kernel, dim, place, far, near, own, came, outs=2)
        starts.append((mine, lax.ppermute(others, "seq", partner)))

    picked = pick_columns(place, tokens, chips)
    other = lax.ppermute(picked, "seq", partner)
    other = narrow(other)
    queries = jnp.dot(tokens, w_query, preferred_element_type=F32).astype(BF16)

    dp_bits = groups.bit_length() - 1
    paths = [list(range(dp_bits)), list(reversed(range(dp_bits)))]
    order = [bit_order(path) for path in paths]

    turned, mixed = {}, None

    def solve(k, side, mixed, after):
        mixed, out = solve_heads(
            place, k, side, per, regular, queries, keys, values, grads, tables[k], starts[k][side], mixed, after
        )
        turned[k, side] = (out, lax.ppermute(out, "seq", partner))
        return mixed

    def gradient(k):
        own = [turned[k, side][0] for side in range(2)]
        far = [turned[k, side][1] for side in range(2)]
        return gradient_blocks(place, own, far, tokens, other, order)

    products = []
    for k in range(per):
        mixed = solve(k, 0, mixed, None)
        if k > 0:
            products.append(gradient(k - 1))
        mixed = solve(k, 1, mixed, products[-1][0] if k > 0 else None)
    products.append(gradient(per - 1))

    finished = []
    for blocks in products:
        parts = []
        for index, path in enumerate(paths):
            keep, send = blocks[2 * index], blocks[2 * index + 1]
            for bit in path:
                pairs = [(i, i ^ (1 << bit)) for i in range(groups)]
                total = keep + lax.ppermute(send, "dp", pairs)
                middle = total.shape[0] // 2
                keep, send = total[:middle], total[middle:]
            parts.append(total[0])
        total = jnp.concatenate(parts, axis=1)
        out = total[0]
        for z in range(1, chips):
            out = out + lax.ppermute(total[z], "seq", [(i, i ^ (2 * z)) for i in range(steps)])
        finished.append(out)
    return mixed[None], jnp.concatenate(finished, axis=0)


def solution(mesh):
    sizes = dict(mesh.shape)
    in_specs = (
        P("dp", "seq", None),
        P(),
        P("dp", "seq", None),
        P("dp", "seq", None),
        P("dp", None, "seq"),
        P(),
        P("dp", "seq", None),
    )
    out_specs = (P("dp", "seq", None), P("dp", "seq"))
    return jax.shard_map(
        functools.partial(per_device, sizes),
        mesh=mesh,
        in_specs=in_specs,
        out_specs=out_specs,
        check_vma=False,
    )
```

```python
import functools

import jax
import jax.numpy as jnp
from jax import lax
from jax.experimental import pallas as pl
from jax.experimental.pallas import tpu as pltpu
from jax.sharding import PartitionSpec as P

ITERS = 4
SUB = 128
EXTRA = 8


F32 = jnp.float32
BF16 = jnp.bfloat16


def dot(left, right):
    return jnp.dot(left, right, preferred_element_type=F32)


def split(value):
    high = value.astype(BF16)
    low = (value - high.astype(F32)).astype(BF16)
    return high, low


def wide(value, axis=1):
    return jnp.concatenate(split(value), axis=axis)


def lane_shift(value, step):
    lanes = lax.broadcasted_iota(jnp.int32, value.shape, 1)
    return jnp.where(lanes >= step, pltpu.roll(value, step, 1), 0.0), lanes >= step


def cumulative_rows(value):
    step = 1
    while step < value.shape[1]:
        value = value + lane_shift(value, step)[0]
        step *= 2
    return value


def decayed_rows(value, cumulative):
    step = 1
    while step < value.shape[1]:
        earlier, inside = lane_shift(cumulative, step)
        factor = jnp.exp(jnp.where(inside, cumulative - earlier, 0.0))
        value = value + factor * lane_shift(value, step)[0]
        step *= 2
    return value


def decay_tables(decay_ref):
    rows = decay_ref.shape[1]
    offset = jnp.zeros((decay_ref.shape[0], 1), F32)
    local, full = [], []
    for c in range(rows // SUB):
        part = cumulative_rows(decay_ref[:, c * SUB : (c + 1) * SUB])
        local.append(part)
        full.append(part + offset)
        offset = offset + part[:, SUB - 1 : SUB]
    return local, jnp.exp(offset - jnp.concatenate(full, axis=1)), jnp.exp(offset)


def states_kernel(half, per, k, core_ref, keys_ref, values_ref, decay_ref, near_ref, away_ref, table_ref, work_ref):
    rows, dim = keys_ref.shape[0], SUB
    core = core_ref[0]
    row_at = lax.broadcasted_iota(jnp.int32, (dim, dim), 0)
    column_at = lax.broadcasted_iota(jnp.int32, (dim, dim), 1)
    local, tails, total = decay_tables(decay_ref)
    work_ref[0] = tails
    work_ref[2] = jnp.broadcast_to(total, tails.shape)
    work_ref[1] = jnp.zeros_like(tails)
    for out, block in ((away_ref, 1 - core), (near_ref, core)):
        for i in range(half):
            head = (block * half + i) * per + k
            column = pl.ds(pl.multiple_of(head * dim, dim), dim)
            key = keys_ref[:, column]
            tail = work_ref[0, pl.ds(head, 1), :]
            key_turned = key.astype(F32).T
            value_turned = values_ref[:, column].astype(F32).T
            work_ref[1, pl.ds(head, 1), :] = jnp.sum(key_turned * key_turned, axis=0, keepdims=True)
            high, low = split(jnp.concatenate([key_turned * tail, value_turned * tail], axis=0))
            state = dot(high, key) + dot(low, key)
            gram = state[0:dim]
            at, second = i // 2, i % 2
            out[at, (1 + second) * dim : (2 + second) * dim, :] = state[dim:]
            out[at, 3 * dim + second : 3 * dim + second + 1, :] = work_ref[2, pl.ds(head, 1), :][:, 0:SUB]
            if second == 0:
                first_gram = gram
            else:
                out[at, 0:dim, :] = jnp.where(row_at <= column_at, first_gram, gram)
                diagonal = jnp.sum(jnp.where(row_at == column_at, gram, 0.0), axis=0, keepdims=True)
                out[at, 3 * dim + 2 : 3 * dim + 3, :] = diagonal
                out[at, 3 * dim + 3 :, :] = jnp.zeros((EXTRA - 3, dim), F32)
    carry = jnp.zeros_like(total)
    for c in range(rows // SUB):
        lanes = slice(c * SUB, (c + 1) * SUB)
        part = decayed_rows(work_ref[1, :, lanes], local[c]) + jnp.exp(local[c]) * carry
        table_ref[0, :, lanes] = local[c]
        table_ref[1, :, lanes] = part
        carry = part[:, SUB - 1 : SUB]


def local_states(core, keys, values, decay, half, per, k):
    rows, columns = keys.shape
    heads = decay.shape[0]
    dim = columns // heads
    state = jax.ShapeDtypeStruct((half // 2, 3 * dim + EXTRA, dim), F32)
    vmem = pl.BlockSpec(memory_space=pltpu.VMEM)
    return pl.pallas_call(
        functools.partial(states_kernel, half, per, k),
        out_shape=[state, state, jax.ShapeDtypeStruct((2, heads, rows), F32)],
        in_specs=[pl.BlockSpec(memory_space=pltpu.SMEM)] + [vmem] * 3,
        out_specs=[vmem] * 3,
        scratch_shapes=[pltpu.VMEM((3, heads, rows), F32)],
        cost_estimate=pl.CostEstimate(
            flops=16 * rows * dim * dim * half, bytes_accessed=8 * rows * columns, transcendentals=0
        ),
        name="local_states",
    )(core, keys, values, decay)


def join(earlier, later, dim):
    row_at = lax.broadcasted_iota(jnp.int32, later.shape, 1)
    column_at = lax.broadcasted_iota(jnp.int32, later.shape, 2)
    is_first = (row_at < dim) & (row_at <= column_at) | (row_at >= dim) & (row_at < 2 * dim)
    is_first = is_first | (row_at == 3 * dim)
    is_decay = (row_at == 3 * dim) | (row_at == 3 * dim + 1)
    factor = jnp.where(is_first, later[:, 3 * dim : 3 * dim + 1], later[:, 3 * dim + 1 : 3 * dim + 2])
    return factor * earlier + jnp.where(is_decay, 0.0, later)


def chip_kernel(dim, place_ref, own_ref, came_ref, out_ref):
    is_first = place_ref[0] == 0
    own, came = own_ref[...], came_ref[...]
    out_ref[...] = join(jnp.where(is_first, own, came), jnp.where(is_first, came, own), dim)


def join_kernel(dim, place_ref, earlier_ref, later_ref, out_ref):
    out_ref[...] = join(earlier_ref[...], later_ref[...], dim)


def start_kernel(dim, place_ref, far_ref, near_ref, own_ref, came_ref, mine_ref, other_ref):
    is_first = place_ref[0] == 0
    before = join(far_ref[...], near_ref[...], dim)
    after = join(before, jnp.where(is_first, own_ref[...], came_ref[...]), dim)
    mine_ref[...] = jnp.where(is_first, before, after)
    other_ref[...] = jnp.where(is_first, after, before)


def combine(kernel, dim, place, *arrays, outs=1):
    vmem = pl.BlockSpec(memory_space=pltpu.VMEM)
    shape = jax.ShapeDtypeStruct(arrays[0].shape, F32)
    results = pl.pallas_call(
        functools.partial(kernel, dim),
        out_shape=[shape] * outs,
        in_specs=[pl.BlockSpec(memory_space=pltpu.SMEM)] + [vmem] * len(arrays),
        out_specs=[vmem] * outs,
        cost_estimate=pl.CostEstimate(
            flops=0, bytes_accessed=4 * arrays[0].size * (len(arrays) + outs), transcendentals=0
        ),
    )(place, *arrays)
    return results[0] if outs == 1 else results


def solve_kernel(is_query, head_of, place_ref, regular_ref, row_ref, k_ref, v_ref, rows_ref, state_ref, *rest):
    out_ref = rest[-1]
    rows, dim = row_ref.shape
    pieces = range(rows // SUB)
    place = [slice(c * SUB, (c + 1) * SUB) for c in pieces]
    step = pl.program_id(0)
    head = head_of(step, place_ref)
    ridge = regular_ref[head]
    row_at = lax.broadcasted_iota(jnp.int32, (SUB, SUB), 0)
    column_at = lax.broadcasted_iota(jnp.int32, (SUB, SUB), 1)
    lower = row_at >= column_at

    is_second = lax.rem(step, 2) == 1
    packed = state_ref[0, 0:dim, :]
    direct = (row_at > column_at) == is_second
    start = jnp.where(direct, packed, packed.T)
    diagonal = state_ref[0, 3 * dim + 2 : 3 * dim + 3, :]
    gram = [jnp.where((row_at == column_at) & is_second, diagonal, start)]
    memory = [state_ref[0, pl.ds(pl.multiple_of((1 + lax.rem(step, 2)) * dim, dim), dim), :]]
    start_trace = jnp.sum(jnp.where(row_at == column_at, gram[0], 0.0), axis=0, keepdims=True)
    start_trace = jnp.sum(start_trace, axis=1, keepdims=True)
    cumulative_row = rows_ref[0, pl.ds(head, 1), :]
    cumulative = [cumulative_row[:, at] for at in place]
    last = [row[:, SUB - 1 : SUB] for row in cumulative]
    whole, offset = [], jnp.zeros((1, 1), F32)
    for c in pieces:
        whole.append(cumulative[c] + offset)
        offset = offset + last[c]
    trace = jnp.exp(jnp.concatenate(whole, axis=1)) * start_trace + rows_ref[1, pl.ds(head, 1), :]
    half = 0.5 * trace
    center = ridge + half
    alphas, gammas = [1.0 / center], []
    for i in range(1, ITERS):
        factor = 0.5 if i == 1 else 0.25
        product = half * alphas[-1]
        alphas.append(1.0 / (center - factor * half * product))
        gammas.append(alphas[-1] * (factor * half * product))
    table = jnp.concatenate(alphas + gammas + [cumulative_row], axis=0).T

    def column(index):
        return [jnp.broadcast_to(table[at, index : index + 1], (SUB, SUB)) for at in place]

    rise = column(2 * ITERS - 1)
    weights = [
        jnp.where(lower, jnp.exp(jnp.where(lower, rise[c] - cumulative[c], 0.0)), 0.0) for c in pieces
    ]
    scale = [jnp.exp(r) for r in rise]

    def twice(value, axis=0):
        return jnp.concatenate([value, value], axis=axis)

    keys = [k_ref[at, :] for at in place]
    values = [v_ref[at, :] for at in place]
    keys_turned = [key.astype(F32).T for key in keys]
    values_turned = [value.astype(F32).T for value in values]
    for c in pieces[:-1]:
        tail = jnp.exp(last[c] - cumulative[c])
        decay = jnp.exp(last[c])
        both = jnp.concatenate([keys_turned[c] * tail, values_turned[c] * tail], axis=0)
        grown = dot(wide(both), twice(keys[c]))
        gram.append(decay * gram[-1] + grown[0:dim])
        memory.append(decay * memory[-1] + grown[dim:])
    keys_turned = [key.astype(BF16) for key in keys_turned]

    if is_query:
        residual = [row_ref[at, :].astype(F32) for at in place]
    else:
        residual = []
        for c in pieces:
            grad = row_ref[place[c], :]
            pulled = scale[c] * dot(twice(grad, 1), wide(memory[c], 0))
            score = weights[c] * dot(grad, values_turned[c].astype(BF16))
            residual.append(pulled + dot(wide(score), twice(keys[c])))

    alpha = column(0)
    change = [alpha[c] * residual[c] for c in pieces]
    solution = list(change)
    rights = [jnp.concatenate([keys_turned[c], gram[c].astype(BF16)], axis=1) for c in pieces]
    for i in range(1, ITERS):
        alpha, gamma = column(i), column(ITERS + i - 1)
        first = [dot(change[c].astype(BF16), rights[c]) for c in pieces]
        second = [dot((first[c][:, 0:SUB] * weights[c]).astype(BF16), keys[c]) for c in pieces]
        for c in pieces:
            applied = ridge * change[c] + (scale[c] * first[c][:, SUB:] + second[c])
            residual[c] = residual[c] - applied
            change[c] = alpha[c] * residual[c] + gamma[c] * change[c]
            solution[c] = solution[c] + change[c]

    for c in pieces:
        if not is_query:
            out_ref[0, :, place[c]] = solution[c].T.astype(BF16).astype(F32)
            continue
        high, low = split(solution[c])
        memory_high, memory_low = split(memory[c].T)
        right = jnp.concatenate([keys_turned[c], memory_high], axis=1)
        first = dot(jnp.concatenate([high, low], axis=1), twice(right))
        second = first[:, SUB:] + dot(high, memory_low)
        score = weights[c] * first[:, 0:SUB]
        output = scale[c] * second + dot(wide(score), twice(values[c]))
        out_ref[place[c], :] = output.astype(BF16)


def solve_heads(is_query, place, k, side, per, regular, sides, keys, values, table, states, mixed, after):
    rows, columns = keys.shape
    heads = regular.shape[0]
    dim = columns // heads
    count = 2 * states.shape[0]

    def head_of(step, place_ref):
        block = place_ref[0] if side == 0 else 1 - place_ref[0]
        return (block * count + step) * per + k

    def at_head(step, place_ref, regular_ref):
        return (0, head_of(step, place_ref))

    head_spec = pl.BlockSpec((rows, dim), at_head)
    operands = [sides, keys, values, table, states]
    in_specs = [head_spec] * 3 + [pl.BlockSpec(table.shape, lambda step, *_: (0, 0, 0))]
    in_specs.append(pl.BlockSpec((1,) + states.shape[1:], lambda step, *_: (step // 2, 0, 0)))
    aliases = {}
    if mixed is not None:
        operands.append(mixed)
        in_specs.append(pl.BlockSpec(memory_space=pl.ANY))
        aliases = {2 + len(operands) - 1: 0}
    if after is not None:
        operands.append(after)
        in_specs.append(pl.BlockSpec(memory_space=pl.ANY))
    if is_query:
        shape, spec = jax.ShapeDtypeStruct((rows, columns), BF16), head_spec
    else:
        shape = jax.ShapeDtypeStruct((count, dim, rows), F32)
        spec = pl.BlockSpec((1, dim, rows), lambda step, *_: (step, 0, 0))
    return pl.pallas_call(
        functools.partial(solve_kernel, is_query, head_of),
        out_shape=shape,
        grid_spec=pltpu.PrefetchScalarGridSpec(
            num_scalar_prefetch=2, grid=(count,), in_specs=in_specs, out_specs=spec
        ),
        input_output_aliases=aliases,
        cost_estimate=pl.CostEstimate(
            flops=count * 80 * rows * dim * dim, bytes_accessed=count * 14 * rows * dim, transcendentals=0
        ),
        name="solve_queries" if is_query else "solve_gradients",
    )(place, regular, *operands)


def pick_kernel(core_ref, tokens_ref, out_ref):
    out_ref[0] = tokens_ref[...].astype(F32)


def pick_columns(core, tokens, blocks):
    rows, width = tokens.shape
    size = width // (2 * blocks)
    return pl.pallas_call(
        pick_kernel,
        out_shape=jax.ShapeDtypeStruct((blocks, rows, size), F32),
        grid_spec=pltpu.PrefetchScalarGridSpec(
            num_scalar_prefetch=1,
            grid=(blocks,),
            in_specs=[pl.BlockSpec((rows, size), lambda z, core_ref: (0, 2 * z + 1 - core_ref[0]))],
            out_specs=pl.BlockSpec((1, rows, size), lambda z, core_ref: (z, 0, 0)),
        ),
        cost_estimate=pl.CostEstimate(flops=0, bytes_accessed=3 * rows * width, transcendentals=0),
        name="pick_columns",
    )(core, tokens)


def narrow_kernel(in_ref, out_ref):
    out_ref[...] = in_ref[...].astype(BF16)


def narrow(blocks):
    spec = pl.BlockSpec((1,) + blocks.shape[1:], lambda z: (z, 0, 0))
    return pl.pallas_call(
        narrow_kernel,
        out_shape=jax.ShapeDtypeStruct(blocks.shape, BF16),
        grid=(blocks.shape[0],),
        in_specs=[spec],
        out_specs=spec,
        cost_estimate=pl.CostEstimate(flops=0, bytes_accessed=6 * blocks.size, transcendentals=0),
        name="narrow",
    )(blocks)


def gradient_kernel(order, place_ref, own0, own1, far0, far1, tokens_ref, other_ref, *rest):
    outs, left_ref = rest[:-1], rest[-1]
    core, group = place_ref[0], place_ref[1]
    half, dim, rows = own0.shape
    middle = dim // 2

    @pl.when(pl.program_id(0) == 0)
    def _():
        for i in range(half):
            near, away = (core * half + i) ^ group, ((1 - core) * half + i) ^ group
            left_ref[near, :, 0:rows] = own0[i].astype(BF16)
            left_ref[away, :, 0:rows] = own1[i].astype(BF16)
            left_ref[near, :, rows:] = far1[i].astype(BF16)
            left_ref[away, :, rows:] = far0[i].astype(BF16)

    left = left_ref[...].reshape(2 * half * dim, 2 * rows)
    result = dot(left, jnp.concatenate([tokens_ref[...], other_ref[0]], axis=0))
    for d in range(2 * half):
        for path in range(2):
            which, index = order[path][d]
            start = d * dim + path * middle
            outs[2 * path + which][index, 0] = result[start : start + middle]


def gradient_blocks(place, own, far, tokens, other, order):
    half, dim, rows = own[0].shape
    blocks, _, size = other.shape
    out = jax.ShapeDtypeStruct((half, blocks, dim // 2, size), F32)
    turned_spec = pl.BlockSpec((half, dim, rows), lambda z, p: (0, 0, 0))
    return pl.pallas_call(
        functools.partial(gradient_kernel, order),
        out_shape=[out] * 4,
        grid_spec=pltpu.PrefetchScalarGridSpec(
            num_scalar_prefetch=1,
            grid=(blocks,),
            in_specs=[turned_spec] * 4
            + [
                pl.BlockSpec((rows, size), lambda z, p: (0, 2 * (p[2] ^ z) + p[0])),
                pl.BlockSpec((1, rows, size), lambda z, p: (p[2] ^ z, 0, 0)),
            ],
            out_specs=[pl.BlockSpec((half, 1, dim // 2, size), lambda z, p: (0, z, 0, 0))] * 4,
            scratch_shapes=[pltpu.VMEM((2 * half, dim, 2 * rows), BF16)],
        ),
        cost_estimate=pl.CostEstimate(
            flops=8 * half * dim * rows * blocks * size,
            bytes_accessed=4 * (4 * half * dim * rows + blocks * rows * size + 2 * half * blocks * dim * size),
            transcendentals=0,
        ),
        name="gradient_blocks",
    )(place, *own, *far, tokens, other)


def bit_order(bits):
    table = []
    for d in range(1 << len(bits)):
        code = 0
        for bit in bits:
            code = 2 * code + ((d >> bit) & 1)
        table.append(divmod(code, 1 << (len(bits) - 1)))
    return table


def per_device(sizes, *arrays):
    return program(sizes, *arrays)


def program(sizes, tokens, w_query, keys, values, log_decay, regular, grad_out):
    groups, steps = sizes["dp"], sizes["seq"]
    chips = steps // 2
    heads = log_decay.shape[1]
    columns = keys.shape[2]
    dim = columns // heads
    per = heads // groups
    half = groups // 2
    tokens, keys, values, grads, decay = tokens[0], keys[0], values[0], grad_out[0], log_decay[0]
    here = lax.axis_index("seq")
    core = here % 2
    place = jnp.stack([core, lax.axis_index("dp"), here // 2]).astype(jnp.int32)
    partner = [(i, i ^ 1) for i in range(steps)]

    locals_, tables = [], []
    for k in range(per):
        near, away, table = local_states(place, keys, values, decay, half, per, k)
        locals_.append((near, lax.ppermute(away, "seq", partner)))
        tables.append(table)

    starts = []
    for own, came in locals_:
        chip_state = combine(chip_kernel, dim, place, own, came)
        window, near, far = 0, None, None
        while window < chips - 1:
            if far is not None:
                near = combine(join_kernel, dim, place, far, near)
            sent = chip_state if near is None else combine(join_kernel, dim, place, near, chip_state)
            shift = 2 * (window + 1)
            pairs = [(i, i + shift) for i in range(steps - shift)]
            came_up = lax.ppermute(sent, "seq", pairs)
            near, far = (came_up, None) if near is None else (near, came_up)
            window = 2 * window + 1
        mine, others = combine(start_kernel, dim, place, far, near, own, came, outs=2)
        starts.append((mine, lax.ppermute(others, "seq", partner)))

    picked = pick_columns(place, tokens, chips)
    other = lax.ppermute(picked, "seq", partner)
    other = narrow(other)
    queries = jnp.dot(tokens, w_query, preferred_element_type=F32).astype(BF16)

    dp_bits = groups.bit_length() - 1
    paths = [list(range(dp_bits)), list(reversed(range(dp_bits)))]
    order = [bit_order(path) for path in paths]

    turned = {}

    def solve(k, side, after):
        out = solve_heads(
            False, place, k, side, per, regular, grads, keys, values, tables[k], starts[k][side], None, after
        )
        turned[k, side] = (out, lax.ppermute(out, "seq", partner))

    def gradient(k):
        own = [turned[k, side][0] for side in range(2)]
        far = [turned[k, side][1] for side in range(2)]
        return gradient_blocks(place, own, far, tokens, other, order)

    products = []
    for k in range(per):
        after = products[-1][0] if k > 0 else None
        solve(k, 0, after)
        solve(k, 1, after)
        products.append(gradient(k))

    mixed = None
    for k in range(per):
        for side in range(2):
            after = turned[per - 1, 1][0] if mixed is None else None
            mixed = solve_heads(
                True, place, k, side, per, regular, queries, keys, values, tables[k], starts[k][side], mixed, after
            )

    finished = []
    for blocks in products:
        parts = []
        for index, path in enumerate(paths):
            keep, send = blocks[2 * index], blocks[2 * index + 1]
            for bit in path:
                pairs = [(i, i ^ (1 << bit)) for i in range(groups)]
                total = keep + lax.ppermute(send, "dp", pairs)
                middle = total.shape[0] // 2
                keep, send = total[:middle], total[middle:]
            parts.append(total[0])
        total = jnp.concatenate(parts, axis=1)
        out = total[0]
        for z in range(1, chips):
            out = out + lax.ppermute(total[z], "seq", [(i, i ^ (2 * z)) for i in range(steps)])
        finished.append(out)
    return mixed[None], jnp.concatenate(finished, axis=0)


def solution(mesh):
    sizes = dict(mesh.shape)
    in_specs = (
        P("dp", "seq", None),
        P(),
        P("dp", "seq", None),
        P("dp", "seq", None),
        P("dp", None, "seq"),
        P(),
        P("dp", "seq", None),
    )
    out_specs = (P("dp", "seq", None), P("dp", "seq"))
    return jax.shard_map(
        functools.partial(per_device, sizes),
        mesh=mesh,
        in_specs=in_specs,
        out_specs=out_specs,
        check_vma=False,
    )
```

```python
import functools

import jax
import jax.numpy as jnp
from jax import lax
from jax.experimental import pallas as pl
from jax.experimental.pallas import tpu as pltpu
from jax.sharding import PartitionSpec as P

ITERS = 4
SUB = 128
EXTRA = 8


F32 = jnp.float32
BF16 = jnp.bfloat16


def dot(left, right):
    return jnp.dot(left, right, preferred_element_type=F32)


def split(value):
    high = value.astype(BF16)
    low = (value - high.astype(F32)).astype(BF16)
    return high, low


def wide(value, axis=1):
    return jnp.concatenate(split(value), axis=axis)


def lane_shift(value, step):
    lanes = lax.broadcasted_iota(jnp.int32, value.shape, 1)
    return jnp.where(lanes >= step, pltpu.roll(value, step, 1), 0.0), lanes >= step


def cumulative_rows(value):
    step = 1
    while step < value.shape[1]:
        value = value + lane_shift(value, step)[0]
        step *= 2
    return value


def decayed_rows(value, cumulative):
    step = 1
    while step < value.shape[1]:
        earlier, inside = lane_shift(cumulative, step)
        factor = jnp.exp(jnp.where(inside, cumulative - earlier, 0.0))
        value = value + factor * lane_shift(value, step)[0]
        step *= 2
    return value


def decay_tables(decay_ref):
    rows = decay_ref.shape[1]
    offset = jnp.zeros((decay_ref.shape[0], 1), F32)
    local, full = [], []
    for c in range(rows // SUB):
        part = cumulative_rows(decay_ref[:, c * SUB : (c + 1) * SUB])
        local.append(part)
        full.append(part + offset)
        offset = offset + part[:, SUB - 1 : SUB]
    return local, jnp.exp(offset - jnp.concatenate(full, axis=1)), jnp.exp(offset)


def states_kernel(half, per, place_ref, keys_ref, values_ref, decay_ref, near_ref, away_ref, table_ref, work_ref):
    rows, dim = keys_ref.shape[0], SUB
    core = place_ref[0]
    row_at = lax.broadcasted_iota(jnp.int32, (dim, dim), 0)
    column_at = lax.broadcasted_iota(jnp.int32, (dim, dim), 1)
    local, tails, total = decay_tables(decay_ref)
    work_ref[0] = tails
    work_ref[2] = jnp.broadcast_to(total, tails.shape)
    for out, block in ((away_ref, 1 - core), (near_ref, core)):
        for k in range(per):
            for i in range(half):
                head = (block * half + i) * per + k
                column = pl.ds(pl.multiple_of(head * dim, dim), dim)
                key = keys_ref[:, column]
                tail = work_ref[0, pl.ds(head, 1), :]
                key_turned = key.astype(F32).T
                value_turned = values_ref[:, column].astype(F32).T
                work_ref[1, pl.ds(head, 1), :] = jnp.sum(key_turned * key_turned, axis=0, keepdims=True)
                high, low = split(jnp.concatenate([key_turned * tail, value_turned * tail], axis=0))
                state = dot(high, key) + dot(low, key)
                gram = state[0:dim]
                at, second = i // 2, i % 2
                out[k, at, (1 + second) * dim : (2 + second) * dim, :] = state[dim:]
                decay = work_ref[2, pl.ds(head, 1), :][:, 0:SUB]
                out[k, at, 3 * dim + second : 3 * dim + second + 1, :] = decay
                if second == 0:
                    first_gram = gram
                else:
                    out[k, at, 0:dim, :] = jnp.where(row_at <= column_at, first_gram, gram)
                    diagonal = jnp.sum(jnp.where(row_at == column_at, gram, 0.0), axis=0, keepdims=True)
                    out[k, at, 3 * dim + 2 : 3 * dim + 3, :] = diagonal
                    out[k, at, 3 * dim + 3 :, :] = jnp.zeros((EXTRA - 3, dim), F32)
    carry = jnp.zeros_like(total)
    for c in range(rows // SUB):
        lanes = slice(c * SUB, (c + 1) * SUB)
        part = decayed_rows(work_ref[1, :, lanes], local[c]) + jnp.exp(local[c]) * carry
        table_ref[0, :, lanes] = local[c]
        table_ref[1, :, lanes] = part
        carry = part[:, SUB - 1 : SUB]


def local_states(place, keys, values, decay, half, per):
    rows, columns = keys.shape
    heads = decay.shape[0]
    dim = columns // heads
    state = jax.ShapeDtypeStruct((per, half // 2, 3 * dim + EXTRA, dim), F32)
    vmem = pl.BlockSpec(memory_space=pltpu.VMEM)
    return pl.pallas_call(
        functools.partial(states_kernel, half, per),
        out_shape=[state, state, jax.ShapeDtypeStruct((2, heads, rows), F32)],
        in_specs=[pl.BlockSpec(memory_space=pltpu.SMEM)] + [vmem] * 3,
        out_specs=[vmem] * 3,
        scratch_shapes=[pltpu.VMEM((3, heads, rows), F32)],
        cost_estimate=pl.CostEstimate(
            flops=16 * rows * dim * dim * half * per, bytes_accessed=8 * rows * columns, transcendentals=0
        ),
        name="local_states",
    )(place, keys, values, decay)


def join(earlier, later, dim):
    row_at = lax.broadcasted_iota(jnp.int32, later.shape, 1)
    column_at = lax.broadcasted_iota(jnp.int32, later.shape, 2)
    is_first = (row_at < dim) & (row_at <= column_at) | (row_at >= dim) & (row_at < 2 * dim)
    is_first = is_first | (row_at == 3 * dim)
    is_decay = (row_at == 3 * dim) | (row_at == 3 * dim + 1)
    factor = jnp.where(is_first, later[:, 3 * dim : 3 * dim + 1], later[:, 3 * dim + 1 : 3 * dim + 2])
    return factor * earlier + jnp.where(is_decay, 0.0, later)


def chip_kernel(dim, place_ref, own_ref, came_ref, *out_refs):
    is_first = place_ref[0] == 0
    for k, out_ref in enumerate(out_refs):
        own, came = own_ref[k], came_ref[k]
        out_ref[...] = join(jnp.where(is_first, own, came), jnp.where(is_first, came, own), dim)


def join_kernel(dim, place_ref, earlier_ref, later_ref, out_ref):
    out_ref[...] = join(earlier_ref[...], later_ref[...], dim)


def start_kernel(dim, k, place_ref, far_ref, near_ref, own_ref, came_ref, mine_ref, other_ref):
    is_first = place_ref[0] == 0
    before = join(far_ref[...], near_ref[...], dim)
    after = join(before, jnp.where(is_first, own_ref[k], came_ref[k]), dim)
    mine_ref[...] = jnp.where(is_first, before, after)
    other_ref[...] = jnp.where(is_first, after, before)


def combine(kernel, place, arrays, shape, outs):
    return pl.pallas_call(
        kernel,
        out_shape=[jax.ShapeDtypeStruct(shape, F32)] * outs,
        in_specs=[pl.BlockSpec(memory_space=pltpu.SMEM)] + [pl.BlockSpec(memory_space=pltpu.VMEM)] * len(arrays),
        out_specs=[pl.BlockSpec(memory_space=pltpu.VMEM)] * outs,
        cost_estimate=pl.CostEstimate(
            flops=0, bytes_accessed=8 * sum(a.size for a in arrays), transcendentals=0
        ),
    )(place, *arrays)


def solve_kernel(
    head_of, place_ref, regular_ref, q_ref, k_ref, v_ref, g_ref, rows_ref, state_ref, *rest
):
    mixed_ref, turned_ref = rest[-2:]
    rows, dim = q_ref.shape
    pieces = range(rows // SUB)
    place = [slice(c * SUB, (c + 1) * SUB) for c in pieces]
    step = pl.program_id(0)
    head = head_of(step, place_ref)
    ridge = regular_ref[head]
    row_at = lax.broadcasted_iota(jnp.int32, (SUB, SUB), 0)
    column_at = lax.broadcasted_iota(jnp.int32, (SUB, SUB), 1)
    lower = row_at >= column_at

    is_second = lax.rem(step, 2) == 1
    packed = state_ref[0, 0:dim, :]
    direct = (row_at > column_at) == is_second
    start = jnp.where(direct, packed, packed.T)
    diagonal = state_ref[0, 3 * dim + 2 : 3 * dim + 3, :]
    gram = [jnp.where((row_at == column_at) & is_second, diagonal, start)]
    memory = [state_ref[0, pl.ds(pl.multiple_of((1 + lax.rem(step, 2)) * dim, dim), dim), :]]
    start_trace = jnp.sum(jnp.where(row_at == column_at, gram[0], 0.0), axis=0, keepdims=True)
    start_trace = jnp.sum(start_trace, axis=1, keepdims=True)
    cumulative_row = rows_ref[0, pl.ds(head, 1), :]
    cumulative = [cumulative_row[:, at] for at in place]
    last = [row[:, SUB - 1 : SUB] for row in cumulative]
    whole, offset = [], jnp.zeros((1, 1), F32)
    for c in pieces:
        whole.append(cumulative[c] + offset)
        offset = offset + last[c]
    trace = jnp.exp(jnp.concatenate(whole, axis=1)) * start_trace + rows_ref[1, pl.ds(head, 1), :]
    half = 0.5 * trace
    center = ridge + half
    alphas, gammas = [1.0 / center], []
    for i in range(1, ITERS):
        factor = 0.5 if i == 1 else 0.25
        product = half * alphas[-1]
        alphas.append(1.0 / (center - factor * half * product))
        gammas.append(alphas[-1] * (factor * half * product))
    table = jnp.concatenate(alphas + gammas + [cumulative_row], axis=0).T

    def column(index):
        return [jnp.broadcast_to(table[at, index : index + 1], (SUB, SUB)) for at in place]

    rise = column(2 * ITERS - 1)
    weights = [
        jnp.where(lower, jnp.exp(jnp.where(lower, rise[c] - cumulative[c], 0.0)), 0.0) for c in pieces
    ]
    scale = [jnp.exp(r) for r in rise]

    keys = [k_ref[at, :] for at in place]
    values = [v_ref[at, :] for at in place]
    keys_turned = [key.astype(F32).T for key in keys]
    values_turned = [value.astype(F32).T for value in values]
    for c in pieces[:-1]:
        tail = jnp.exp(last[c] - cumulative[c])
        decay = jnp.exp(last[c])
        both = jnp.concatenate([keys_turned[c] * tail, values_turned[c] * tail], axis=0)
        grown = dot(wide(both), jnp.concatenate([keys[c], keys[c]], axis=0))
        gram.append(decay * gram[-1] + grown[0:dim])
        memory.append(decay * memory[-1] + grown[dim:])
    keys_turned = [key.astype(BF16) for key in keys_turned]
    values_turned = [value.astype(BF16) for value in values_turned]

    def pair(left, right):
        return jnp.concatenate([left, right], axis=0)

    residual = []
    for c in pieces:
        grad = g_ref[place[c], :]
        pulled = scale[c] * dot(jnp.concatenate([grad, grad], axis=1), wide(memory[c], 0))
        score = weights[c] * dot(grad, values_turned[c])
        pulled = pulled + dot(wide(score), pair(keys[c], keys[c]))
        residual.append(pair(q_ref[place[c], :].astype(F32), pulled))

    alpha = column(0)
    change = [pair(alpha[c], alpha[c]) * residual[c] for c in pieces]
    solution = list(change)
    rights = [jnp.concatenate([keys_turned[c], gram[c].astype(BF16)], axis=1) for c in pieces]
    for i in range(1, ITERS):
        alpha, gamma = column(i), column(ITERS + i - 1)
        first = [dot(change[c].astype(BF16), rights[c]) for c in pieces]
        second = [
            dot((first[c][:, 0:SUB] * pair(weights[c], weights[c])).astype(BF16), keys[c]) for c in pieces
        ]
        for c in pieces:
            applied = ridge * change[c] + (pair(scale[c], scale[c]) * first[c][:, SUB:] + second[c])
            residual[c] = residual[c] - applied
            change[c] = pair(alpha[c], alpha[c]) * residual[c] + pair(gamma[c], gamma[c]) * change[c]
            solution[c] = solution[c] + change[c]

    for c in pieces:
        turned_ref[0, :, place[c]] = solution[c][SUB:].T.astype(BF16).astype(F32)
    for c in pieces:
        high, low = split(solution[c][0:SUB])
        memory_high, memory_low = split(memory[c].T)
        right = jnp.concatenate([keys_turned[c], memory_high], axis=1)
        first = dot(jnp.concatenate([high, low], axis=1), pair(right, right))
        second = first[:, SUB:] + dot(high, memory_low)
        score = weights[c] * first[:, 0:SUB]
        output = scale[c] * second + dot(wide(score), pair(values[c], values[c]))
        mixed_ref[place[c], :] = output.astype(BF16)


def solve_heads(place, k, side, per, regular, queries, keys, values, grads, table, states, mixed, after):
    rows, columns = keys.shape
    heads = regular.shape[0]
    dim = columns // heads
    count = 2 * states.shape[0]

    def head_of(step, place_ref):
        block = place_ref[0] if side == 0 else 1 - place_ref[0]
        return (block * count + step) * per + k

    def at_head(step, place_ref, regular_ref):
        return (0, head_of(step, place_ref))

    wide_spec = pl.BlockSpec((rows, dim), at_head)
    operands = [queries, keys, values, grads, table, states]
    in_specs = [wide_spec] * 4 + [pl.BlockSpec(table.shape, lambda step, *_: (0, 0, 0))]
    in_specs.append(pl.BlockSpec((1,) + states.shape[1:], lambda step, *_: (step // 2, 0, 0)))
    aliases = {}
    if mixed is not None:
        operands.append(mixed)
        in_specs.append(pl.BlockSpec(memory_space=pl.ANY))
        aliases = {2 + len(operands) - 1: 0}
    if after is not None:
        operands.append(after)
        in_specs.append(pl.BlockSpec(memory_space=pl.ANY))
    return pl.pallas_call(
        functools.partial(solve_kernel, head_of),
        out_shape=[
            jax.ShapeDtypeStruct((rows, columns), BF16),
            jax.ShapeDtypeStruct((count, dim, rows), F32),
        ],
        grid_spec=pltpu.PrefetchScalarGridSpec(
            num_scalar_prefetch=2,
            grid=(count,),
            in_specs=in_specs,
            out_specs=[wide_spec, pl.BlockSpec((1, dim, rows), lambda step, *_: (step, 0, 0))],
        ),
        input_output_aliases=aliases,
        cost_estimate=pl.CostEstimate(
            flops=count * 80 * rows * dim * dim, bytes_accessed=count * 14 * rows * dim, transcendentals=0
        ),
        name="solve_heads",
    )(place, regular, *operands)


def pick_kernel(core_ref, tokens_ref, out_ref):
    out_ref[0] = tokens_ref[...].astype(F32)


def pick_columns(core, tokens, blocks):
    rows, width = tokens.shape
    size = width // (2 * blocks)
    return pl.pallas_call(
        pick_kernel,
        out_shape=jax.ShapeDtypeStruct((blocks, rows, size), F32),
        grid_spec=pltpu.PrefetchScalarGridSpec(
            num_scalar_prefetch=1,
            grid=(blocks,),
            in_specs=[pl.BlockSpec((rows, size), lambda z, core_ref: (0, 2 * z + 1 - core_ref[0]))],
            out_specs=pl.BlockSpec((1, rows, size), lambda z, core_ref: (z, 0, 0)),
        ),
        cost_estimate=pl.CostEstimate(flops=0, bytes_accessed=3 * rows * width, transcendentals=0),
        name="pick_columns",
    )(core, tokens)


def narrow_kernel(in_ref, out_ref):
    out_ref[...] = in_ref[...].astype(BF16)


def narrow(blocks):
    spec = pl.BlockSpec((1,) + blocks.shape[1:], lambda z: (z, 0, 0))
    return pl.pallas_call(
        narrow_kernel,
        out_shape=jax.ShapeDtypeStruct(blocks.shape, BF16),
        grid=(blocks.shape[0],),
        in_specs=[spec],
        out_specs=spec,
        cost_estimate=pl.CostEstimate(flops=0, bytes_accessed=6 * blocks.size, transcendentals=0),
        name="narrow",
    )(blocks)


def gradient_kernel(order, place_ref, own0, own1, far0, far1, tokens_ref, other_ref, *rest):
    outs, left_ref = rest[:-1], rest[-1]
    core, group = place_ref[0], place_ref[1]
    half, dim, rows = own0.shape
    middle = dim // 2

    @pl.when(pl.program_id(0) == 0)
    def _():
        for i in range(half):
            near, away = (core * half + i) ^ group, ((1 - core) * half + i) ^ group
            left_ref[near, :, 0:rows] = own0[i].astype(BF16)
            left_ref[away, :, 0:rows] = own1[i].astype(BF16)
            left_ref[near, :, rows:] = far1[i].astype(BF16)
            left_ref[away, :, rows:] = far0[i].astype(BF16)

    left = left_ref[...].reshape(2 * half * dim, 2 * rows)
    result = dot(left, jnp.concatenate([tokens_ref[...], other_ref[0]], axis=0))
    for d in range(2 * half):
        for path in range(2):
            which, index = order[path][d]
            start = d * dim + path * middle
            outs[2 * path + which][index, 0] = result[start : start + middle]


def gradient_blocks(place, own, far, tokens, other, order):
    half, dim, rows = own[0].shape
    blocks, _, size = other.shape
    out = jax.ShapeDtypeStruct((half, blocks, dim // 2, size), F32)
    turned_spec = pl.BlockSpec((half, dim, rows), lambda z, p: (0, 0, 0))
    return pl.pallas_call(
        functools.partial(gradient_kernel, order),
        out_shape=[out] * 4,
        grid_spec=pltpu.PrefetchScalarGridSpec(
            num_scalar_prefetch=1,
            grid=(blocks,),
            in_specs=[turned_spec] * 4
            + [
                pl.BlockSpec((rows, size), lambda z, p: (0, 2 * (p[2] ^ z) + p[0])),
                pl.BlockSpec((1, rows, size), lambda z, p: (p[2] ^ z, 0, 0)),
            ],
            out_specs=[pl.BlockSpec((half, 1, dim // 2, size), lambda z, p: (0, z, 0, 0))] * 4,
            scratch_shapes=[pltpu.VMEM((2 * half, dim, 2 * rows), BF16)],
        ),
        cost_estimate=pl.CostEstimate(
            flops=8 * half * dim * rows * blocks * size,
            bytes_accessed=4 * (4 * half * dim * rows + blocks * rows * size + 2 * half * blocks * dim * size),
            transcendentals=0,
        ),
        name="gradient_blocks",
    )(place, *own, *far, tokens, other)


def merge_kernel(count, *refs):
    sums, outs = refs[: 2 * count], refs[2 * count :]
    rows = sums[0].shape[2]
    for z, out in enumerate(outs):
        for i in range(count):
            out[i * rows : (i + 1) * rows, :] = sums[2 * i][0, z] + sums[2 * i + 1][0, z]


def merge_blocks(sums):
    _, chips, rows, size = sums[0].shape
    count = len(sums) // 2
    vmem = pl.BlockSpec(memory_space=pltpu.VMEM)
    return pl.pallas_call(
        functools.partial(merge_kernel, count),
        out_shape=[jax.ShapeDtypeStruct((count * rows, size), F32)] * chips,
        in_specs=[vmem] * len(sums),
        out_specs=[vmem] * chips,
        cost_estimate=pl.CostEstimate(
            flops=0, bytes_accessed=6 * sum(a.size for a in sums), transcendentals=0
        ),
        name="merge_blocks",
    )(*sums)


def bit_order(bits):
    table = []
    for d in range(1 << len(bits)):
        code = 0
        for bit in bits:
            code = 2 * code + ((d >> bit) & 1)
        table.append(divmod(code, 1 << (len(bits) - 1)))
    return table


def per_device(sizes, *arrays):
    return program(sizes, *arrays)


def program(sizes, tokens, w_query, keys, values, log_decay, regular, grad_out):
    groups, steps = sizes["dp"], sizes["seq"]
    chips = steps // 2
    heads = log_decay.shape[1]
    columns = keys.shape[2]
    dim = columns // heads
    per = heads // groups
    half = groups // 2
    tokens, keys, values, grads, decay = tokens[0], keys[0], values[0], grad_out[0], log_decay[0]
    here = lax.axis_index("seq")
    core = here % 2
    place = jnp.stack([core, lax.axis_index("dp"), here // 2]).astype(jnp.int32)
    partner = [(i, i ^ 1) for i in range(steps)]

    own, away, table = local_states(place, keys, values, decay, half, per)
    came = lax.ppermute(away, "seq", partner)
    shape = own.shape[1:]
    chip_states = combine(functools.partial(chip_kernel, dim), place, [own, came], shape, per)
    joined = functools.partial(join_kernel, dim)
    starts = []
    for k, chip_state in enumerate(chip_states):
        window, near, far = 0, None, None
        while window < chips - 1:
            if far is not None:
                (near,) = combine(joined, place, [far, near], shape, 1)
            sent = chip_state
            if near is not None:
                (sent,) = combine(joined, place, [near, chip_state], shape, 1)
            shift = 2 * (window + 1)
            pairs = [(i, i + shift) for i in range(steps - shift)]
            came_up = lax.ppermute(sent, "seq", pairs)
            near, far = (came_up, None) if near is None else (near, came_up)
            window = 2 * window + 1
        starting = functools.partial(start_kernel, dim, k)
        mine, others = combine(starting, place, [far, near, own, came], shape, 2)
        starts.append((mine, lax.ppermute(others, "seq", partner)))

    picked = pick_columns(place, tokens, chips)
    other = lax.ppermute(picked, "seq", partner)
    other = narrow(other)
    queries = jnp.dot(tokens, w_query, preferred_element_type=F32).astype(BF16)

    dp_bits = groups.bit_length() - 1
    paths = [list(range(dp_bits)), list(reversed(range(dp_bits)))]
    order = [bit_order(path) for path in paths]

    turned, mixed = {}, None

    def solve(k, side, mixed, after):
        mixed, out = solve_heads(
            place, k, side, per, regular, queries, keys, values, grads, table, starts[k][side], mixed, after
        )
        turned[k, side] = (out, lax.ppermute(out, "seq", partner))
        return mixed

    def gradient(k):
        own = [turned[k, side][0] for side in range(2)]
        far = [turned[k, side][1] for side in range(2)]
        return gradient_blocks(place, own, far, tokens, other, order)

    products = []
    for k in range(per):
        mixed = solve(k, 0, mixed, None)
        if k > 0:
            products.append(gradient(k - 1))
        mixed = solve(k, 1, mixed, products[-1][0] if k > 0 else None)
    products.append(gradient(per - 1))

    finished = []
    for blocks in products:
        sums = []
        for index, path in enumerate(paths):
            keep, send = blocks[2 * index], blocks[2 * index + 1]
            for bit in path:
                pairs = [(i, i ^ (1 << bit)) for i in range(groups)]
                came = lax.ppermute(send, "dp", pairs)
                if bit == path[-1]:
                    sums += [keep, came]
                else:
                    total = keep + came
                    keep, send = jnp.split(total, 2, axis=0)
        out, *others = merge_blocks(sums)
        for z, other_block in enumerate(others, 1):
            pairs = [(i, i ^ (2 * z)) for i in range(steps)]
            out = out + lax.ppermute(other_block, "seq", pairs)
        finished.append(out)
    return mixed[None], jnp.concatenate(finished, axis=0)


def solution(mesh):
    sizes = dict(mesh.shape)
    in_specs = (
        P("dp", "seq", None),
        P(),
        P("dp", "seq", None),
        P("dp", "seq", None),
        P("dp", None, "seq"),
        P(),
        P("dp", "seq", None),
    )
    out_specs = (P("dp", "seq", None), P("dp", "seq"))
    return jax.shard_map(
        functools.partial(per_device, sizes),
        mesh=mesh,
        in_specs=in_specs,
        out_specs=out_specs,
        check_vma=False,
    )
```

```python
import functools

import jax
import jax.numpy as jnp
from jax import lax
from jax.experimental import pallas as pl
from jax.experimental.pallas import tpu as pltpu
from jax.sharding import PartitionSpec as P

ITERS = 4
SUB = 128
EXTRA = 8


F32 = jnp.float32
BF16 = jnp.bfloat16


def dot(left, right):
    return jnp.dot(left, right, preferred_element_type=F32)


def split(value):
    high = value.astype(BF16)
    low = (value - high.astype(F32)).astype(BF16)
    return high, low


def wide(value, axis=1):
    return jnp.concatenate(split(value), axis=axis)


def lane_shift(value, step):
    lanes = lax.broadcasted_iota(jnp.int32, value.shape, 1)
    return jnp.where(lanes >= step, pltpu.roll(value, step, 1), 0.0), lanes >= step


def cumulative_rows(value):
    step = 1
    while step < value.shape[1]:
        value = value + lane_shift(value, step)[0]
        step *= 2
    return value


def decayed_rows(value, cumulative):
    step = 1
    while step < value.shape[1]:
        earlier, inside = lane_shift(cumulative, step)
        factor = jnp.exp(jnp.where(inside, cumulative - earlier, 0.0))
        value = value + factor * lane_shift(value, step)[0]
        step *= 2
    return value


def decay_tables(decay_ref):
    rows = decay_ref.shape[1]
    offset = jnp.zeros((decay_ref.shape[0], 1), F32)
    local, full = [], []
    for c in range(rows // SUB):
        part = cumulative_rows(decay_ref[:, c * SUB : (c + 1) * SUB])
        local.append(part)
        full.append(part + offset)
        offset = offset + part[:, SUB - 1 : SUB]
    return local, jnp.exp(offset - jnp.concatenate(full, axis=1)), jnp.exp(offset)


def states_kernel(half, per, place_ref, keys_ref, values_ref, decay_ref, near_ref, away_ref, table_ref, work_ref):
    rows, dim = keys_ref.shape[0], SUB
    core = place_ref[0]
    row_at = lax.broadcasted_iota(jnp.int32, (dim, dim), 0)
    column_at = lax.broadcasted_iota(jnp.int32, (dim, dim), 1)
    local, tails, total = decay_tables(decay_ref)
    work_ref[0] = tails
    work_ref[2] = jnp.broadcast_to(total, tails.shape)
    for out, block in ((away_ref, 1 - core), (near_ref, core)):
        for k in range(per):
            for i in range(half):
                head = (block * half + i) * per + k
                column = pl.ds(pl.multiple_of(head * dim, dim), dim)
                key = keys_ref[:, column]
                tail = work_ref[0, pl.ds(head, 1), :]
                key_turned = key.astype(F32).T
                value_turned = values_ref[:, column].astype(F32).T
                work_ref[1, pl.ds(head, 1), :] = jnp.sum(key_turned * key_turned, axis=0, keepdims=True)
                high, low = split(jnp.concatenate([key_turned * tail, value_turned * tail], axis=0))
                state = dot(high, key) + dot(low, key)
                gram = state[0:dim]
                at, second = i // 2, i % 2
                out[k, at, (1 + second) * dim : (2 + second) * dim, :] = state[dim:]
                decay = work_ref[2, pl.ds(head, 1), :][:, 0:SUB]
                out[k, at, 3 * dim + second : 3 * dim + second + 1, :] = decay
                if second == 0:
                    first_gram = gram
                else:
                    out[k, at, 0:dim, :] = jnp.where(row_at <= column_at, first_gram, gram)
                    diagonal = jnp.sum(jnp.where(row_at == column_at, gram, 0.0), axis=0, keepdims=True)
                    out[k, at, 3 * dim + 2 : 3 * dim + 3, :] = diagonal
                    out[k, at, 3 * dim + 3 :, :] = jnp.zeros((EXTRA - 3, dim), F32)
    carry = jnp.zeros_like(total)
    for c in range(rows // SUB):
        lanes = slice(c * SUB, (c + 1) * SUB)
        part = decayed_rows(work_ref[1, :, lanes], local[c]) + jnp.exp(local[c]) * carry
        table_ref[0, :, lanes] = local[c]
        table_ref[1, :, lanes] = part
        carry = part[:, SUB - 1 : SUB]


def local_states(place, keys, values, decay, half, per):
    rows, columns = keys.shape
    heads = decay.shape[0]
    dim = columns // heads
    state = jax.ShapeDtypeStruct((per, half // 2, 3 * dim + EXTRA, dim), F32)
    vmem = pl.BlockSpec(memory_space=pltpu.VMEM)
    return pl.pallas_call(
        functools.partial(states_kernel, half, per),
        out_shape=[state, state, jax.ShapeDtypeStruct((2, heads, rows), F32)],
        in_specs=[pl.BlockSpec(memory_space=pltpu.SMEM)] + [vmem] * 3,
        out_specs=[vmem] * 3,
        scratch_shapes=[pltpu.VMEM((3, heads, rows), F32)],
        cost_estimate=pl.CostEstimate(
            flops=16 * rows * dim * dim * half * per, bytes_accessed=8 * rows * columns, transcendentals=0
        ),
        name="local_states",
    )(place, keys, values, decay)


def join(earlier, later, dim):
    row_at = lax.broadcasted_iota(jnp.int32, later.shape, 1)
    column_at = lax.broadcasted_iota(jnp.int32, later.shape, 2)
    is_first = (row_at < dim) & (row_at <= column_at) | (row_at >= dim) & (row_at < 2 * dim)
    is_first = is_first | (row_at == 3 * dim)
    is_decay = (row_at == 3 * dim) | (row_at == 3 * dim + 1)
    factor = jnp.where(is_first, later[:, 3 * dim : 3 * dim + 1], later[:, 3 * dim + 1 : 3 * dim + 2])
    return factor * earlier + jnp.where(is_decay, 0.0, later)


def chip_kernel(dim, place_ref, own_ref, came_ref, *out_refs):
    is_first = place_ref[0] == 0
    for k, out_ref in enumerate(out_refs):
        own, came = own_ref[k], came_ref[k]
        out_ref[...] = join(jnp.where(is_first, own, came), jnp.where(is_first, came, own), dim)


def join_kernel(dim, place_ref, earlier_ref, later_ref, out_ref):
    out_ref[...] = join(earlier_ref[...], later_ref[...], dim)


def start_kernel(dim, k, place_ref, far_ref, near_ref, own_ref, came_ref, mine_ref, other_ref):
    is_first = place_ref[0] == 0
    before = join(far_ref[...], near_ref[...], dim)
    after = join(before, jnp.where(is_first, own_ref[k], came_ref[k]), dim)
    mine_ref[...] = jnp.where(is_first, before, after)
    other_ref[...] = jnp.where(is_first, after, before)


def combine(kernel, place, arrays, shape, outs):
    return pl.pallas_call(
        kernel,
        out_shape=[jax.ShapeDtypeStruct(shape, F32)] * outs,
        in_specs=[pl.BlockSpec(memory_space=pltpu.SMEM)] + [pl.BlockSpec(memory_space=pltpu.VMEM)] * len(arrays),
        out_specs=[pl.BlockSpec(memory_space=pltpu.VMEM)] * outs,
        cost_estimate=pl.CostEstimate(
            flops=0, bytes_accessed=8 * sum(a.size for a in arrays), transcendentals=0
        ),
    )(place, *arrays)


def solve_kernel(
    half, head_of, place_ref, regular_ref, q_ref, k_ref, v_ref, g_ref, rows_ref, mine_ref, other_ref, *rest
):
    mixed_ref, turned_ref = rest[-2:]
    rows, dim = q_ref.shape
    pieces = range(rows // SUB)
    place = [slice(c * SUB, (c + 1) * SUB) for c in pieces]
    step = pl.program_id(0)
    head = head_of(step, place_ref)
    ridge = regular_ref[head]
    row_at = lax.broadcasted_iota(jnp.int32, (SUB, SUB), 0)
    column_at = lax.broadcasted_iota(jnp.int32, (SUB, SUB), 1)
    lower = row_at >= column_at

    is_second = lax.rem(step, 2) == 1
    is_mine = step < half

    def state(start, size):
        at = pl.ds(start, size)
        return jnp.where(is_mine, mine_ref[0, at, :], other_ref[0, at, :])

    packed = state(0, dim)
    direct = (row_at > column_at) == is_second
    start = jnp.where(direct, packed, packed.T)
    diagonal = state(3 * dim, EXTRA)[2:3]
    gram = [jnp.where((row_at == column_at) & is_second, diagonal, start)]
    memory = [state(pl.multiple_of((1 + lax.rem(step, 2)) * dim, dim), dim)]
    start_trace = jnp.sum(jnp.where(row_at == column_at, gram[0], 0.0), axis=0, keepdims=True)
    start_trace = jnp.sum(start_trace, axis=1, keepdims=True)
    cumulative_row = rows_ref[0, pl.ds(head, 1), :]
    cumulative = [cumulative_row[:, at] for at in place]
    last = [row[:, SUB - 1 : SUB] for row in cumulative]
    whole, offset = [], jnp.zeros((1, 1), F32)
    for c in pieces:
        whole.append(cumulative[c] + offset)
        offset = offset + last[c]
    trace = jnp.exp(jnp.concatenate(whole, axis=1)) * start_trace + rows_ref[1, pl.ds(head, 1), :]
    span = 0.5 * trace
    center = ridge + span
    alphas, gammas = [1.0 / center], []
    for i in range(1, ITERS):
        factor = 0.5 if i == 1 else 0.25
        product = span * alphas[-1]
        alphas.append(1.0 / (center - factor * span * product))
        gammas.append(alphas[-1] * (factor * span * product))
    table = jnp.concatenate(alphas + gammas + [cumulative_row], axis=0).T

    def column(index):
        return [jnp.broadcast_to(table[at, index : index + 1], (SUB, SUB)) for at in place]

    rise = column(2 * ITERS - 1)
    weights = [
        jnp.where(lower, jnp.exp(jnp.where(lower, rise[c] - cumulative[c], 0.0)), 0.0) for c in pieces
    ]
    scale = [jnp.exp(r) for r in rise]

    keys = [k_ref[at, :] for at in place]
    values = [v_ref[at, :] for at in place]
    keys_turned = [key.astype(F32).T for key in keys]
    values_turned = [value.astype(F32).T for value in values]
    for c in pieces[:-1]:
        tail = jnp.exp(last[c] - cumulative[c])
        decay = jnp.exp(last[c])
        both = jnp.concatenate([keys_turned[c] * tail, values_turned[c] * tail], axis=0)
        grown = dot(wide(both), jnp.concatenate([keys[c], keys[c]], axis=0))
        gram.append(decay * gram[-1] + grown[0:dim])
        memory.append(decay * memory[-1] + grown[dim:])
    keys_turned = [key.astype(BF16) for key in keys_turned]
    values_turned = [value.astype(BF16) for value in values_turned]

    def pair(left, right):
        return jnp.concatenate([left, right], axis=0)

    residual = []
    for c in pieces:
        grad = g_ref[place[c], :]
        pulled = scale[c] * dot(jnp.concatenate([grad, grad], axis=1), wide(memory[c], 0))
        score = weights[c] * dot(grad, values_turned[c])
        pulled = pulled + dot(wide(score), pair(keys[c], keys[c]))
        residual.append(pair(q_ref[place[c], :].astype(F32), pulled))

    alpha = column(0)
    change = [pair(alpha[c], alpha[c]) * residual[c] for c in pieces]
    solution = list(change)
    rights = [jnp.concatenate([keys_turned[c], gram[c].astype(BF16)], axis=1) for c in pieces]
    for i in range(1, ITERS):
        alpha, gamma = column(i), column(ITERS + i - 1)
        first = [dot(change[c].astype(BF16), rights[c]) for c in pieces]
        second = [
            dot((first[c][:, 0:SUB] * pair(weights[c], weights[c])).astype(BF16), keys[c]) for c in pieces
        ]
        for c in pieces:
            applied = ridge * change[c] + (pair(scale[c], scale[c]) * first[c][:, SUB:] + second[c])
            residual[c] = residual[c] - applied
            change[c] = pair(alpha[c], alpha[c]) * residual[c] + pair(gamma[c], gamma[c]) * change[c]
            solution[c] = solution[c] + change[c]

    for c in pieces:
        turned_ref[0, :, place[c]] = solution[c][SUB:].T.astype(BF16).astype(F32)
    for c in pieces:
        high, low = split(solution[c][0:SUB])
        memory_high, memory_low = split(memory[c].T)
        right = jnp.concatenate([keys_turned[c], memory_high], axis=1)
        first = dot(jnp.concatenate([high, low], axis=1), pair(right, right))
        second = first[:, SUB:] + dot(high, memory_low)
        score = weights[c] * first[:, 0:SUB]
        output = scale[c] * second + dot(wide(score), pair(values[c], values[c]))
        mixed_ref[place[c], :] = output.astype(BF16)


def solve_heads(place, k, per, regular, queries, keys, values, grads, table, mine, other, mixed, after):
    rows, columns = keys.shape
    heads = regular.shape[0]
    dim = columns // heads
    half = 2 * mine.shape[0]
    count = 2 * half

    def head_of(step, place_ref):
        return lax.rem(place_ref[0] * half + step, count) * per + k

    def at_head(step, place_ref, regular_ref):
        return (0, head_of(step, place_ref))

    wide_spec = pl.BlockSpec((rows, dim), at_head)
    operands = [queries, keys, values, grads, table, mine, other]
    in_specs = [wide_spec] * 4 + [pl.BlockSpec(table.shape, lambda step, *_: (0, 0, 0))]
    pair = (1,) + mine.shape[1:]
    in_specs.append(pl.BlockSpec(pair, lambda step, *_: (jnp.minimum(step, half - 1) // 2, 0, 0)))
    in_specs.append(pl.BlockSpec(pair, lambda step, *_: (jnp.maximum(step - half, 0) // 2, 0, 0)))
    aliases = {}
    if mixed is not None:
        operands.append(mixed)
        in_specs.append(pl.BlockSpec(memory_space=pl.ANY))
        aliases = {2 + len(operands) - 1: 0}
    if after is not None:
        operands.append(after)
        in_specs.append(pl.BlockSpec(memory_space=pl.ANY))
    return pl.pallas_call(
        functools.partial(solve_kernel, half, head_of),
        out_shape=[
            jax.ShapeDtypeStruct((rows, columns), BF16),
            jax.ShapeDtypeStruct((count, dim, rows), F32),
        ],
        grid_spec=pltpu.PrefetchScalarGridSpec(
            num_scalar_prefetch=2,
            grid=(count,),
            in_specs=in_specs,
            out_specs=[wide_spec, pl.BlockSpec((1, dim, rows), lambda step, *_: (step, 0, 0))],
        ),
        input_output_aliases=aliases,
        cost_estimate=pl.CostEstimate(
            flops=count * 80 * rows * dim * dim, bytes_accessed=count * 14 * rows * dim, transcendentals=0
        ),
        name="solve_heads",
    )(place, regular, *operands)


def pick_kernel(core_ref, tokens_ref, out_ref):
    out_ref[0] = tokens_ref[...].astype(F32)


def pick_columns(core, tokens, blocks):
    rows, width = tokens.shape
    size = width // (2 * blocks)
    return pl.pallas_call(
        pick_kernel,
        out_shape=jax.ShapeDtypeStruct((blocks, rows, size), F32),
        grid_spec=pltpu.PrefetchScalarGridSpec(
            num_scalar_prefetch=1,
            grid=(blocks,),
            in_specs=[pl.BlockSpec((rows, size), lambda z, core_ref: (0, 2 * z + 1 - core_ref[0]))],
            out_specs=pl.BlockSpec((1, rows, size), lambda z, core_ref: (z, 0, 0)),
        ),
        cost_estimate=pl.CostEstimate(flops=0, bytes_accessed=3 * rows * width, transcendentals=0),
        name="pick_columns",
    )(core, tokens)


def narrow_kernel(in_ref, out_ref):
    out_ref[...] = in_ref[...].astype(BF16)


def narrow(blocks):
    spec = pl.BlockSpec((1,) + blocks.shape[1:], lambda z: (z, 0, 0))
    return pl.pallas_call(
        narrow_kernel,
        out_shape=jax.ShapeDtypeStruct(blocks.shape, BF16),
        grid=(blocks.shape[0],),
        in_specs=[spec],
        out_specs=spec,
        cost_estimate=pl.CostEstimate(flops=0, bytes_accessed=6 * blocks.size, transcendentals=0),
        name="narrow",
    )(blocks)


def gradient_kernel(order, place_ref, own_ref, far_ref, tokens_ref, other_ref, *rest):
    outs, left_ref = rest[:-1], rest[-1]
    core, group = place_ref[0], place_ref[1]
    count, dim, rows = own_ref.shape
    half = count // 2
    middle = dim // 2

    @pl.when(pl.program_id(0) == 0)
    def _():
        for i in range(half):
            near, away = (core * half + i) ^ group, ((1 - core) * half + i) ^ group
            left_ref[near, :, 0:rows] = own_ref[i].astype(BF16)
            left_ref[away, :, 0:rows] = own_ref[half + i].astype(BF16)
            left_ref[near, :, rows:] = far_ref[half + i].astype(BF16)
            left_ref[away, :, rows:] = far_ref[i].astype(BF16)

    left = left_ref[...].reshape(2 * half * dim, 2 * rows)
    result = dot(left, jnp.concatenate([tokens_ref[...], other_ref[0]], axis=0))
    for d in range(2 * half):
        for path in range(2):
            which, index = order[path][d]
            start = d * dim + path * middle
            outs[2 * path + which][index, 0] = result[start : start + middle]


def gradient_blocks(place, own, far, tokens, other, order):
    count, dim, rows = own.shape
    half = count // 2
    blocks, _, size = other.shape
    out = jax.ShapeDtypeStruct((half, blocks, dim // 2, size), F32)
    turned_spec = pl.BlockSpec((count, dim, rows), lambda z, p: (0, 0, 0))
    return pl.pallas_call(
        functools.partial(gradient_kernel, order),
        out_shape=[out] * 4,
        grid_spec=pltpu.PrefetchScalarGridSpec(
            num_scalar_prefetch=1,
            grid=(blocks,),
            in_specs=[turned_spec] * 2
            + [
                pl.BlockSpec((rows, size), lambda z, p: (0, 2 * (p[2] ^ z) + p[0])),
                pl.BlockSpec((1, rows, size), lambda z, p: (p[2] ^ z, 0, 0)),
            ],
            out_specs=[pl.BlockSpec((half, 1, dim // 2, size), lambda z, p: (0, z, 0, 0))] * 4,
            scratch_shapes=[pltpu.VMEM((2 * half, dim, 2 * rows), BF16)],
        ),
        cost_estimate=pl.CostEstimate(
            flops=8 * half * dim * rows * blocks * size,
            bytes_accessed=4 * (4 * half * dim * rows + blocks * rows * size + 2 * half * blocks * dim * size),
            transcendentals=0,
        ),
        name="gradient_blocks",
    )(place, own, far, tokens, other)


def sum_kernel(keep_ref, came_ref, keep_out, send_out):
    out_half = keep_out.shape[0]
    for i in range(out_half):
        send_out[i] = keep_ref[out_half + i] + came_ref[out_half + i]
    for i in range(out_half):
        keep_out[i] = keep_ref[i] + came_ref[i]


def sum_blocks(keep, came):
    shape = (keep.shape[0] // 2,) + keep.shape[1:]
    vmem = pl.BlockSpec(memory_space=pltpu.VMEM)
    return pl.pallas_call(
        sum_kernel,
        out_shape=[jax.ShapeDtypeStruct(shape, F32)] * 2,
        in_specs=[vmem] * 2,
        out_specs=[vmem] * 2,
        cost_estimate=pl.CostEstimate(flops=0, bytes_accessed=12 * keep.size, transcendentals=0),
        name="sum_blocks",
    )(keep, came)


def merge_kernel(count, *refs):
    sums, outs = refs[: 2 * count], refs[2 * count :]
    rows = sums[0].shape[2]
    for z, out in enumerate(outs):
        for i in range(count):
            out[i * rows : (i + 1) * rows, :] = sums[2 * i][0, z] + sums[2 * i + 1][0, z]


def merge_blocks(sums):
    _, chips, rows, size = sums[0].shape
    count = len(sums) // 2
    vmem = pl.BlockSpec(memory_space=pltpu.VMEM)
    return pl.pallas_call(
        functools.partial(merge_kernel, count),
        out_shape=[jax.ShapeDtypeStruct((count * rows, size), F32)] * chips,
        in_specs=[vmem] * len(sums),
        out_specs=[vmem] * chips,
        cost_estimate=pl.CostEstimate(
            flops=0, bytes_accessed=6 * sum(a.size for a in sums), transcendentals=0
        ),
        name="merge_blocks",
    )(*sums)


def bit_order(bits):
    table = []
    for d in range(1 << len(bits)):
        code = 0
        for bit in bits:
            code = 2 * code + ((d >> bit) & 1)
        table.append(divmod(code, 1 << (len(bits) - 1)))
    return table


def per_device(sizes, *arrays):
    return program(sizes, *arrays)


def program(sizes, tokens, w_query, keys, values, log_decay, regular, grad_out):
    groups, steps = sizes["dp"], sizes["seq"]
    chips = steps // 2
    heads = log_decay.shape[1]
    columns = keys.shape[2]
    dim = columns // heads
    per = heads // groups
    half = groups // 2
    tokens, keys, values, grads, decay = tokens[0], keys[0], values[0], grad_out[0], log_decay[0]
    here = lax.axis_index("seq")
    core = here % 2
    place = jnp.stack([core, lax.axis_index("dp"), here // 2]).astype(jnp.int32)
    partner = [(i, i ^ 1) for i in range(steps)]

    own, away, table = local_states(place, keys, values, decay, half, per)
    came = lax.ppermute(away, "seq", partner)
    shape = own.shape[1:]
    chip_states = combine(functools.partial(chip_kernel, dim), place, [own, came], shape, per)
    joined = functools.partial(join_kernel, dim)
    starts = []
    for k, chip_state in enumerate(chip_states):
        window, near, far = 0, None, None
        while window < chips - 1:
            if far is not None:
                (near,) = combine(joined, place, [far, near], shape, 1)
            sent = chip_state
            if near is not None:
                (sent,) = combine(joined, place, [near, chip_state], shape, 1)
            shift = 2 * (window + 1)
            pairs = [(i, i + shift) for i in range(steps - shift)]
            came_up = lax.ppermute(sent, "seq", pairs)
            near, far = (came_up, None) if near is None else (near, came_up)
            window = 2 * window + 1
        starting = functools.partial(start_kernel, dim, k)
        mine, others = combine(starting, place, [far, near, own, came], shape, 2)
        starts.append((mine, lax.ppermute(others, "seq", partner)))

    picked = pick_columns(place, tokens, chips)
    other = lax.ppermute(picked, "seq", partner)
    other = narrow(other)
    queries = jnp.dot(tokens, w_query, preferred_element_type=F32).astype(BF16)

    dp_bits = groups.bit_length() - 1
    paths = [list(range(dp_bits)), list(reversed(range(dp_bits)))]
    order = [bit_order(path) for path in paths]

    products, mixed = [], None
    for k, (mine, others) in enumerate(starts):
        after = products[-1][0] if k > 0 else None
        mixed, turned = solve_heads(
            place, k, per, regular, queries, keys, values, grads, table, mine, others, mixed, after
        )
        far = lax.ppermute(turned, "seq", partner)
        products.append(gradient_blocks(place, turned, far, tokens, other, order))

    finished = []
    for blocks in products:
        sums = []
        for index, path in enumerate(paths):
            keep, send = blocks[2 * index], blocks[2 * index + 1]
            for bit in path:
                pairs = [(i, i ^ (1 << bit)) for i in range(groups)]
                came = lax.ppermute(send, "dp", pairs)
                if bit == path[-1]:
                    sums += [keep, came]
                else:
                    keep, send = sum_blocks(keep, came)
        out, *others = merge_blocks(sums)
        for z, other_block in enumerate(others, 1):
            pairs = [(i, i ^ (2 * z)) for i in range(steps)]
            out = out + lax.ppermute(other_block, "seq", pairs)
        finished.append(out)
    return mixed[None], jnp.concatenate(finished, axis=0)


def solution(mesh):
    sizes = dict(mesh.shape)
    in_specs = (
        P("dp", "seq", None),
        P(),
        P("dp", "seq", None),
        P("dp", "seq", None),
        P("dp", None, "seq"),
        P(),
        P("dp", "seq", None),
    )
    out_specs = (P("dp", "seq", None), P("dp", "seq"))
    return jax.shard_map(
        functools.partial(per_device, sizes),
        mesh=mesh,
        in_specs=in_specs,
        out_specs=out_specs,
        check_vma=False,
    )
```

```python
import functools

import jax
import jax.numpy as jnp
from jax import lax
from jax.experimental import pallas as pl
from jax.experimental.pallas import tpu as pltpu
from jax.sharding import PartitionSpec as P

ITERS = 4
SUB = 128
EXTRA = 8


F32 = jnp.float32
BF16 = jnp.bfloat16


FULL = pltpu.CompilerParams(vmem_limit_bytes=67_043_328)


def whole(array):
    return pl.BlockSpec(array.shape, lambda *_: (0,) * len(array.shape))


def dot(left, right):
    return jnp.dot(left, right, preferred_element_type=F32)


def split(value):
    high = value.astype(BF16)
    low = (value - high.astype(F32)).astype(BF16)
    return high, low


def wide(value, axis=1):
    return jnp.concatenate(split(value), axis=axis)


def lane_shift(value, step):
    lanes = lax.broadcasted_iota(jnp.int32, value.shape, 1)
    return jnp.where(lanes >= step, pltpu.roll(value, step, 1), 0.0), lanes >= step


def cumulative_rows(value):
    step = 1
    while step < value.shape[1]:
        value = value + lane_shift(value, step)[0]
        step *= 2
    return value


def decayed_rows(value, cumulative):
    step = 1
    while step < value.shape[1]:
        earlier, inside = lane_shift(cumulative, step)
        factor = jnp.exp(jnp.where(inside, cumulative - earlier, 0.0))
        value = value + factor * lane_shift(value, step)[0]
        step *= 2
    return value


def decay_tables(decay_ref):
    rows = decay_ref.shape[1]
    offset = jnp.zeros((decay_ref.shape[0], 1), F32)
    local, full = [], []
    for c in range(rows // SUB):
        part = cumulative_rows(decay_ref[:, c * SUB : (c + 1) * SUB])
        local.append(part)
        full.append(part + offset)
        offset = offset + part[:, SUB - 1 : SUB]
    return local, jnp.exp(offset - jnp.concatenate(full, axis=1)), jnp.exp(offset)


def states_kernel(half, per, place_ref, keys_ref, values_ref, decay_ref, near_ref, away_ref, table_ref, work_ref):
    rows, dim = keys_ref.shape[0], SUB
    core = place_ref[0]
    row_at = lax.broadcasted_iota(jnp.int32, (dim, dim), 0)
    column_at = lax.broadcasted_iota(jnp.int32, (dim, dim), 1)
    local, tails, total = decay_tables(decay_ref)
    work_ref[0] = tails
    work_ref[2] = jnp.broadcast_to(total, tails.shape)
    for out, block in ((away_ref, 1 - core), (near_ref, core)):
        for k in range(per):
            for i in range(half):
                head = (block * half + i) * per + k
                column = pl.ds(pl.multiple_of(head * dim, dim), dim)
                key = keys_ref[:, column]
                tail = work_ref[0, pl.ds(head, 1), :]
                key_turned = key.astype(F32).T
                value_turned = values_ref[:, column].astype(F32).T
                work_ref[1, pl.ds(head, 1), :] = jnp.sum(key_turned * key_turned, axis=0, keepdims=True)
                high, low = split(jnp.concatenate([key_turned * tail, value_turned * tail], axis=0))
                state = dot(high, key) + dot(low, key)
                gram = state[0:dim]
                at, second = i // 2, i % 2
                out[k, at, (1 + second) * dim : (2 + second) * dim, :] = state[dim:]
                decay = work_ref[2, pl.ds(head, 1), :][:, 0:SUB]
                out[k, at, 3 * dim + second : 3 * dim + second + 1, :] = decay
                if second == 0:
                    first_gram = gram
                else:
                    out[k, at, 0:dim, :] = jnp.where(row_at <= column_at, first_gram, gram)
                    diagonal = jnp.sum(jnp.where(row_at == column_at, gram, 0.0), axis=0, keepdims=True)
                    out[k, at, 3 * dim + 2 : 3 * dim + 3, :] = diagonal
                    out[k, at, 3 * dim + 3 :, :] = jnp.zeros((EXTRA - 3, dim), F32)
    carry = jnp.zeros_like(total)
    for c in range(rows // SUB):
        lanes = slice(c * SUB, (c + 1) * SUB)
        part = decayed_rows(work_ref[1, :, lanes], local[c]) + jnp.exp(local[c]) * carry
        table_ref[0, :, lanes] = local[c]
        table_ref[1, :, lanes] = part
        carry = part[:, SUB - 1 : SUB]


def local_states(place, keys, values, decay, half, per):
    rows, columns = keys.shape
    heads = decay.shape[0]
    dim = columns // heads
    state = jax.ShapeDtypeStruct((per, half // 2, 3 * dim + EXTRA, dim), F32)
    table = jax.ShapeDtypeStruct((2, heads, rows), F32)
    return pl.pallas_call(
        functools.partial(states_kernel, half, per),
        out_shape=[state, state, table],
        in_specs=[pl.BlockSpec(memory_space=pltpu.SMEM)] + [whole(a) for a in (keys, values, decay)],
        out_specs=[whole(state), whole(state), whole(table)],
        scratch_shapes=[pltpu.VMEM((3, heads, rows), F32)],
        grid=(1,),
        compiler_params=FULL,
        cost_estimate=pl.CostEstimate(
            flops=16 * rows * dim * dim * half * per, bytes_accessed=8 * rows * columns, transcendentals=0
        ),
        name="local_states",
    )(place, keys, values, decay)


def join(earlier, later, dim):
    row_at = lax.broadcasted_iota(jnp.int32, later.shape, 1)
    column_at = lax.broadcasted_iota(jnp.int32, later.shape, 2)
    is_first = (row_at < dim) & (row_at <= column_at) | (row_at >= dim) & (row_at < 2 * dim)
    is_first = is_first | (row_at == 3 * dim)
    is_decay = (row_at == 3 * dim) | (row_at == 3 * dim + 1)
    factor = jnp.where(is_first, later[:, 3 * dim : 3 * dim + 1], later[:, 3 * dim + 1 : 3 * dim + 2])
    return factor * earlier + jnp.where(is_decay, 0.0, later)


def chip_kernel(dim, place_ref, own_ref, came_ref, *out_refs):
    is_first = place_ref[0] == 0
    for k, out_ref in enumerate(out_refs):
        own, came = own_ref[k], came_ref[k]
        out_ref[...] = join(jnp.where(is_first, own, came), jnp.where(is_first, came, own), dim)


def join_kernel(dim, place_ref, earlier_ref, later_ref, out_ref):
    out_ref[...] = join(earlier_ref[...], later_ref[...], dim)


def start_kernel(dim, k, place_ref, far_ref, near_ref, own_ref, came_ref, mine_ref, other_ref):
    is_first = place_ref[0] == 0
    before = join(far_ref[...], near_ref[...], dim)
    after = join(before, jnp.where(is_first, own_ref[k], came_ref[k]), dim)
    mine_ref[...] = jnp.where(is_first, before, after)
    other_ref[...] = jnp.where(is_first, after, before)


def combine(kernel, place, arrays, shape, outs):
    out = jax.ShapeDtypeStruct(shape, F32)
    return pl.pallas_call(
        kernel,
        out_shape=[out] * outs,
        in_specs=[pl.BlockSpec(memory_space=pltpu.SMEM)] + [whole(a) for a in arrays],
        out_specs=[whole(out)] * outs,
        grid=(1,),
        compiler_params=FULL,
        cost_estimate=pl.CostEstimate(
            flops=0, bytes_accessed=8 * sum(a.size for a in arrays), transcendentals=0
        ),
    )(place, *arrays)


def solve_kernel(
    half, head_of, place_ref, regular_ref, q_ref, k_ref, v_ref, g_ref, rows_ref, mine_ref, other_ref, *rest
):
    mixed_ref, turned_ref = rest[-2:]
    rows, dim = q_ref.shape
    pieces = range(rows // SUB)
    place = [slice(c * SUB, (c + 1) * SUB) for c in pieces]
    step = pl.program_id(0)
    head = head_of(step, place_ref)
    ridge = regular_ref[head]
    row_at = lax.broadcasted_iota(jnp.int32, (SUB, SUB), 0)
    column_at = lax.broadcasted_iota(jnp.int32, (SUB, SUB), 1)
    lower = row_at >= column_at

    is_second = lax.rem(step, 2) == 1
    is_mine = step < half

    def state(start, size):
        at = pl.ds(start, size)
        return jnp.where(is_mine, mine_ref[0, at, :], other_ref[0, at, :])

    packed = state(0, dim)
    direct = (row_at > column_at) == is_second
    start = jnp.where(direct, packed, packed.T)
    diagonal = state(3 * dim, EXTRA)[2:3]
    gram = [jnp.where((row_at == column_at) & is_second, diagonal, start)]
    memory = [state(pl.multiple_of((1 + lax.rem(step, 2)) * dim, dim), dim)]
    start_trace = jnp.sum(jnp.where(row_at == column_at, gram[0], 0.0), axis=0, keepdims=True)
    start_trace = jnp.sum(start_trace, axis=1, keepdims=True)
    cumulative_row = rows_ref[0, pl.ds(head, 1), :]
    cumulative = [cumulative_row[:, at] for at in place]
    last = [row[:, SUB - 1 : SUB] for row in cumulative]
    whole, offset = [], jnp.zeros((1, 1), F32)
    for c in pieces:
        whole.append(cumulative[c] + offset)
        offset = offset + last[c]
    trace = jnp.exp(jnp.concatenate(whole, axis=1)) * start_trace + rows_ref[1, pl.ds(head, 1), :]
    span = 0.5 * trace
    center = ridge + span
    alphas, gammas = [1.0 / center], []
    for i in range(1, ITERS):
        factor = 0.5 if i == 1 else 0.25
        product = span * alphas[-1]
        alphas.append(1.0 / (center - factor * span * product))
        gammas.append(alphas[-1] * (factor * span * product))
    table = jnp.concatenate(alphas + gammas + [cumulative_row], axis=0).T

    def column(index):
        return [jnp.broadcast_to(table[at, index : index + 1], (SUB, SUB)) for at in place]

    rise = column(2 * ITERS - 1)
    weights = [
        jnp.where(lower, jnp.exp(jnp.where(lower, rise[c] - cumulative[c], 0.0)), 0.0) for c in pieces
    ]
    scale = [jnp.exp(r) for r in rise]

    keys = [k_ref[at, :] for at in place]
    values = [v_ref[at, :] for at in place]
    keys_turned = [key.astype(F32).T for key in keys]
    values_turned = [value.astype(F32).T for value in values]
    for c in pieces[:-1]:
        tail = jnp.exp(last[c] - cumulative[c])
        decay = jnp.exp(last[c])
        both = jnp.concatenate([keys_turned[c] * tail, values_turned[c] * tail], axis=0)
        grown = dot(wide(both), jnp.concatenate([keys[c], keys[c]], axis=0))
        gram.append(decay * gram[-1] + grown[0:dim])
        memory.append(decay * memory[-1] + grown[dim:])
    keys_turned = [key.astype(BF16) for key in keys_turned]
    values_turned = [value.astype(BF16) for value in values_turned]

    def pair(left, right):
        return jnp.concatenate([left, right], axis=0)

    residual = []
    for c in pieces:
        grad = g_ref[place[c], :]
        pulled = scale[c] * dot(jnp.concatenate([grad, grad], axis=1), wide(memory[c], 0))
        score = weights[c] * dot(grad, values_turned[c])
        pulled = pulled + dot(wide(score), pair(keys[c], keys[c]))
        residual.append(pair(q_ref[place[c], :].astype(F32), pulled))

    alpha = column(0)
    change = [pair(alpha[c], alpha[c]) * residual[c] for c in pieces]
    solution = list(change)
    rights = [jnp.concatenate([keys_turned[c], gram[c].astype(BF16)], axis=1) for c in pieces]
    for i in range(1, ITERS):
        alpha, gamma = column(i), column(ITERS + i - 1)
        first = [dot(change[c].astype(BF16), rights[c]) for c in pieces]
        second = [
            dot((first[c][:, 0:SUB] * pair(weights[c], weights[c])).astype(BF16), keys[c]) for c in pieces
        ]
        for c in pieces:
            applied = ridge * change[c] + (pair(scale[c], scale[c]) * first[c][:, SUB:] + second[c])
            residual[c] = residual[c] - applied
            change[c] = pair(alpha[c], alpha[c]) * residual[c] + pair(gamma[c], gamma[c]) * change[c]
            solution[c] = solution[c] + change[c]

    for c in pieces:
        turned_ref[0, :, place[c]] = solution[c][SUB:].T.astype(BF16).astype(F32)
    for c in pieces:
        high, low = split(solution[c][0:SUB])
        memory_high, memory_low = split(memory[c].T)
        right = jnp.concatenate([keys_turned[c], memory_high], axis=1)
        first = dot(jnp.concatenate([high, low], axis=1), pair(right, right))
        second = first[:, SUB:] + dot(high, memory_low)
        score = weights[c] * first[:, 0:SUB]
        output = scale[c] * second + dot(wide(score), pair(values[c], values[c]))
        mixed_ref[place[c], :] = output.astype(BF16)


def solve_heads(place, k, per, regular, queries, keys, values, grads, table, mine, other, mixed, after):
    rows, columns = keys.shape
    heads = regular.shape[0]
    dim = columns // heads
    half = 2 * mine.shape[0]
    count = 2 * half

    def head_of(step, place_ref):
        return lax.rem(place_ref[0] * half + step, count) * per + k

    def at_head(step, place_ref, regular_ref):
        return (0, head_of(step, place_ref))

    wide_spec = pl.BlockSpec((rows, dim), at_head)
    operands = [queries, keys, values, grads, table, mine, other]
    in_specs = [wide_spec] * 4 + [pl.BlockSpec(table.shape, lambda step, *_: (0, 0, 0))]
    pair = (1,) + mine.shape[1:]
    in_specs.append(pl.BlockSpec(pair, lambda step, *_: (jnp.minimum(step, half - 1) // 2, 0, 0)))
    in_specs.append(pl.BlockSpec(pair, lambda step, *_: (jnp.maximum(step - half, 0) // 2, 0, 0)))
    aliases = {}
    if mixed is not None:
        operands.append(mixed)
        in_specs.append(pl.BlockSpec(memory_space=pl.ANY))
        aliases = {2 + len(operands) - 1: 0}
    if after is not None:
        operands.append(after)
        in_specs.append(pl.BlockSpec(memory_space=pl.ANY))
    return pl.pallas_call(
        functools.partial(solve_kernel, half, head_of),
        out_shape=[
            jax.ShapeDtypeStruct((rows, columns), BF16),
            jax.ShapeDtypeStruct((count, dim, rows), F32),
        ],
        grid_spec=pltpu.PrefetchScalarGridSpec(
            num_scalar_prefetch=2,
            grid=(count,),
            in_specs=in_specs,
            out_specs=[wide_spec, pl.BlockSpec((1, dim, rows), lambda step, *_: (step, 0, 0))],
        ),
        input_output_aliases=aliases,
        cost_estimate=pl.CostEstimate(
            flops=count * 80 * rows * dim * dim, bytes_accessed=count * 14 * rows * dim, transcendentals=0
        ),
        compiler_params=FULL,
        name="solve_heads",
    )(place, regular, *operands)


def pick_kernel(core_ref, tokens_ref, out_ref):
    out_ref[0] = tokens_ref[...].astype(F32)


def pick_columns(core, tokens, blocks):
    rows, width = tokens.shape
    size = width // (2 * blocks)
    return pl.pallas_call(
        pick_kernel,
        out_shape=jax.ShapeDtypeStruct((blocks, rows, size), F32),
        grid_spec=pltpu.PrefetchScalarGridSpec(
            num_scalar_prefetch=1,
            grid=(blocks,),
            in_specs=[pl.BlockSpec((rows, size), lambda z, core_ref: (0, 2 * z + 1 - core_ref[0]))],
            out_specs=pl.BlockSpec((1, rows, size), lambda z, core_ref: (z, 0, 0)),
        ),
        cost_estimate=pl.CostEstimate(flops=0, bytes_accessed=3 * rows * width, transcendentals=0),
        compiler_params=FULL,
        name="pick_columns",
    )(core, tokens)


def narrow_kernel(in_ref, out_ref):
    out_ref[...] = in_ref[...].astype(BF16)


def narrow(blocks):
    spec = pl.BlockSpec((1,) + blocks.shape[1:], lambda z: (z, 0, 0))
    return pl.pallas_call(
        narrow_kernel,
        out_shape=jax.ShapeDtypeStruct(blocks.shape, BF16),
        grid=(blocks.shape[0],),
        in_specs=[spec],
        out_specs=spec,
        cost_estimate=pl.CostEstimate(flops=0, bytes_accessed=6 * blocks.size, transcendentals=0),
        compiler_params=FULL,
        name="narrow",
    )(blocks)


def gradient_kernel(order, place_ref, own_ref, far_ref, tokens_ref, other_ref, *rest):
    outs, left_ref = rest[:-1], rest[-1]
    core, group = place_ref[0], place_ref[1]
    count, dim, rows = own_ref.shape
    half = count // 2
    middle = dim // 2

    @pl.when(pl.program_id(0) == 0)
    def _():
        for i in range(half):
            near, away = (core * half + i) ^ group, ((1 - core) * half + i) ^ group
            left_ref[near, :, 0:rows] = own_ref[i].astype(BF16)
            left_ref[away, :, 0:rows] = own_ref[half + i].astype(BF16)
            left_ref[near, :, rows:] = far_ref[half + i].astype(BF16)
            left_ref[away, :, rows:] = far_ref[i].astype(BF16)

    left = left_ref[...].reshape(2 * half * dim, 2 * rows)
    result = dot(left, jnp.concatenate([tokens_ref[...], other_ref[0]], axis=0))
    for d in range(2 * half):
        for path in range(2):
            which, index = order[path][d]
            start = d * dim + path * middle
            outs[2 * path + which][index, 0] = result[start : start + middle]


def gradient_blocks(place, own, far, tokens, other, order):
    count, dim, rows = own.shape
    half = count // 2
    blocks, _, size = other.shape
    out = jax.ShapeDtypeStruct((half, blocks, dim // 2, size), F32)
    turned_spec = pl.BlockSpec((count, dim, rows), lambda z, p: (0, 0, 0))
    return pl.pallas_call(
        functools.partial(gradient_kernel, order),
        out_shape=[out] * 4,
        grid_spec=pltpu.PrefetchScalarGridSpec(
            num_scalar_prefetch=1,
            grid=(blocks,),
            in_specs=[turned_spec] * 2
            + [
                pl.BlockSpec((rows, size), lambda z, p: (0, 2 * (p[2] ^ z) + p[0])),
                pl.BlockSpec((1, rows, size), lambda z, p: (p[2] ^ z, 0, 0)),
            ],
            out_specs=[pl.BlockSpec((half, 1, dim // 2, size), lambda z, p: (0, z, 0, 0))] * 4,
            scratch_shapes=[pltpu.VMEM((2 * half, dim, 2 * rows), BF16)],
        ),
        cost_estimate=pl.CostEstimate(
            flops=8 * half * dim * rows * blocks * size,
            bytes_accessed=4 * (4 * half * dim * rows + blocks * rows * size + 2 * half * blocks * dim * size),
            transcendentals=0,
        ),
        compiler_params=FULL,
        name="gradient_blocks",
    )(place, own, far, tokens, other)


def sum_kernel(keep_ref, came_ref, keep_out, send_out):
    out_half = keep_out.shape[0]
    for i in range(out_half):
        send_out[i] = keep_ref[out_half + i] + came_ref[out_half + i]
    for i in range(out_half):
        keep_out[i] = keep_ref[i] + came_ref[i]


def sum_blocks(keep, came):
    out = jax.ShapeDtypeStruct((keep.shape[0] // 2,) + keep.shape[1:], F32)
    return pl.pallas_call(
        sum_kernel,
        out_shape=[out] * 2,
        in_specs=[whole(keep)] * 2,
        out_specs=[whole(out)] * 2,
        grid=(1,),
        compiler_params=FULL,
        cost_estimate=pl.CostEstimate(flops=0, bytes_accessed=12 * keep.size, transcendentals=0),
        name="sum_blocks",
    )(keep, came)


def merge_kernel(count, *refs):
    sums, outs = refs[: 2 * count], refs[2 * count :]
    rows = sums[0].shape[2]
    for z, out in enumerate(outs):
        for i in range(count):
            out[i * rows : (i + 1) * rows, :] = sums[2 * i][0, z] + sums[2 * i + 1][0, z]


def merge_blocks(sums):
    _, chips, rows, size = sums[0].shape
    count = len(sums) // 2
    out = jax.ShapeDtypeStruct((count * rows, size), F32)
    return pl.pallas_call(
        functools.partial(merge_kernel, count),
        out_shape=[out] * chips,
        in_specs=[whole(a) for a in sums],
        out_specs=[whole(out)] * chips,
        grid=(1,),
        compiler_params=FULL,
        cost_estimate=pl.CostEstimate(
            flops=0, bytes_accessed=6 * sum(a.size for a in sums), transcendentals=0
        ),
        name="merge_blocks",
    )(*sums)


def bit_order(bits):
    table = []
    for d in range(1 << len(bits)):
        code = 0
        for bit in bits:
            code = 2 * code + ((d >> bit) & 1)
        table.append(divmod(code, 1 << (len(bits) - 1)))
    return table


def per_device(sizes, *arrays):
    return program(sizes, *arrays)


def program(sizes, tokens, w_query, keys, values, log_decay, regular, grad_out):
    groups, steps = sizes["dp"], sizes["seq"]
    chips = steps // 2
    heads = log_decay.shape[1]
    columns = keys.shape[2]
    dim = columns // heads
    per = heads // groups
    half = groups // 2
    tokens, keys, values, grads, decay = tokens[0], keys[0], values[0], grad_out[0], log_decay[0]
    here = lax.axis_index("seq")
    core = here % 2
    place = jnp.stack([core, lax.axis_index("dp"), here // 2]).astype(jnp.int32)
    partner = [(i, i ^ 1) for i in range(steps)]

    own, away, table = local_states(place, keys, values, decay, half, per)
    came = lax.ppermute(away, "seq", partner)
    shape = own.shape[1:]
    chip_states = combine(functools.partial(chip_kernel, dim), place, [own, came], shape, per)
    joined = functools.partial(join_kernel, dim)
    starts = []
    for k, chip_state in enumerate(chip_states):
        window, near, far = 0, None, None
        while window < chips - 1:
            if far is not None:
                (near,) = combine(joined, place, [far, near], shape, 1)
            sent = chip_state
            if near is not None:
                (sent,) = combine(joined, place, [near, chip_state], shape, 1)
            shift = 2 * (window + 1)
            pairs = [(i, i + shift) for i in range(steps - shift)]
            came_up = lax.ppermute(sent, "seq", pairs)
            near, far = (came_up, None) if near is None else (near, came_up)
            window = 2 * window + 1
        starting = functools.partial(start_kernel, dim, k)
        mine, others = combine(starting, place, [far, near, own, came], shape, 2)
        starts.append((mine, lax.ppermute(others, "seq", partner)))

    picked = pick_columns(place, tokens, chips)
    other = lax.ppermute(picked, "seq", partner)
    other = narrow(other)
    queries = jnp.dot(tokens, w_query, preferred_element_type=F32).astype(BF16)

    dp_bits = groups.bit_length() - 1
    paths = [list(range(dp_bits)), list(reversed(range(dp_bits)))]
    order = [bit_order(path) for path in paths]

    products, mixed = [], None
    for k, (mine, others) in enumerate(starts):
        after = products[-1][0] if k > 0 else None
        mixed, turned = solve_heads(
            place, k, per, regular, queries, keys, values, grads, table, mine, others, mixed, after
        )
        far = lax.ppermute(turned, "seq", partner)
        products.append(gradient_blocks(place, turned, far, tokens, other, order))

    finished = []
    for blocks in products:
        sums = []
        for index, path in enumerate(paths):
            keep, send = blocks[2 * index], blocks[2 * index + 1]
            for bit in path:
                pairs = [(i, i ^ (1 << bit)) for i in range(groups)]
                came = lax.ppermute(send, "dp", pairs)
                if bit == path[-1]:
                    sums += [keep, came]
                else:
                    keep, send = sum_blocks(keep, came)
        out, *others = merge_blocks(sums)
        for z, other_block in enumerate(others, 1):
            pairs = [(i, i ^ (2 * z)) for i in range(steps)]
            out = out + lax.ppermute(other_block, "seq", pairs)
        finished.append(out)
    return mixed[None], jnp.concatenate(finished, axis=0)


def solution(mesh):
    sizes = dict(mesh.shape)
    in_specs = (
        P("dp", "seq", None),
        P(),
        P("dp", "seq", None),
        P("dp", "seq", None),
        P("dp", None, "seq"),
        P(),
        P("dp", "seq", None),
    )
    out_specs = (P("dp", "seq", None), P("dp", "seq"))
    return jax.shard_map(
        functools.partial(per_device, sizes),
        mesh=mesh,
        in_specs=in_specs,
        out_specs=out_specs,
        check_vma=False,
    )
```

```python
import functools

import jax
import jax.numpy as jnp
from jax import lax
from jax.experimental import pallas as pl
from jax.experimental.pallas import tpu as pltpu
from jax.sharding import PartitionSpec as P

ITERS = 4
SUB = 128
EXTRA = 8


F32 = jnp.float32
BF16 = jnp.bfloat16


FULL = pltpu.CompilerParams(vmem_limit_bytes=67_043_328)


def whole(array):
    return pl.BlockSpec(array.shape, lambda *_: (0,) * len(array.shape))


def dot(left, right):
    return jnp.dot(left, right, preferred_element_type=F32)


def split(value):
    high = value.astype(BF16)
    low = (value - high.astype(F32)).astype(BF16)
    return high, low


def wide(value, axis=1):
    return jnp.concatenate(split(value), axis=axis)


def lane_shift(value, step):
    lanes = lax.broadcasted_iota(jnp.int32, value.shape, 1)
    return jnp.where(lanes >= step, pltpu.roll(value, step, 1), 0.0), lanes >= step


def cumulative_rows(value):
    step = 1
    while step < value.shape[1]:
        value = value + lane_shift(value, step)[0]
        step *= 2
    return value


def decayed_rows(value, cumulative):
    step = 1
    while step < value.shape[1]:
        earlier, inside = lane_shift(cumulative, step)
        factor = jnp.exp(jnp.where(inside, cumulative - earlier, 0.0))
        value = value + factor * lane_shift(value, step)[0]
        step *= 2
    return value


def decay_tables(decay_ref):
    rows = decay_ref.shape[1]
    offset = jnp.zeros((decay_ref.shape[0], 1), F32)
    local, full = [], []
    for c in range(rows // SUB):
        part = cumulative_rows(decay_ref[:, c * SUB : (c + 1) * SUB])
        local.append(part)
        full.append(part + offset)
        offset = offset + part[:, SUB - 1 : SUB]
    return local, jnp.exp(offset - jnp.concatenate(full, axis=1)), jnp.exp(offset)


def states_kernel(half, per, place_ref, keys_ref, values_ref, decay_ref, near_ref, away_ref, table_ref, work_ref):
    rows, dim = keys_ref.shape[0], SUB
    core = place_ref[0]
    row_at = lax.broadcasted_iota(jnp.int32, (dim, dim), 0)
    column_at = lax.broadcasted_iota(jnp.int32, (dim, dim), 1)
    local, tails, total = decay_tables(decay_ref)
    work_ref[0] = tails
    work_ref[2] = jnp.broadcast_to(total, tails.shape)
    for out, block in ((away_ref, 1 - core), (near_ref, core)):
        for k in range(per):
            for i in range(half):
                head = (block * half + i) * per + k
                column = pl.ds(pl.multiple_of(head * dim, dim), dim)
                key = keys_ref[:, column]
                tail = work_ref[0, pl.ds(head, 1), :]
                key_turned = key.astype(F32).T
                value_turned = values_ref[:, column].astype(F32).T
                work_ref[1, pl.ds(head, 1), :] = jnp.sum(key_turned * key_turned, axis=0, keepdims=True)
                high, low = split(jnp.concatenate([key_turned * tail, value_turned * tail], axis=0))
                state = dot(high, key) + dot(low, key)
                gram = state[0:dim]
                at, second = i // 2, i % 2
                out[k, at, (1 + second) * dim : (2 + second) * dim, :] = state[dim:]
                decay = work_ref[2, pl.ds(head, 1), :][:, 0:SUB]
                out[k, at, 3 * dim + second : 3 * dim + second + 1, :] = decay
                if second == 0:
                    first_gram = gram
                else:
                    out[k, at, 0:dim, :] = jnp.where(row_at <= column_at, first_gram, gram)
                    diagonal = jnp.sum(jnp.where(row_at == column_at, gram, 0.0), axis=0, keepdims=True)
                    out[k, at, 3 * dim + 2 : 3 * dim + 3, :] = diagonal
                    out[k, at, 3 * dim + 3 :, :] = jnp.zeros((EXTRA - 3, dim), F32)
    carry = jnp.zeros_like(total)
    for c in range(rows // SUB):
        lanes = slice(c * SUB, (c + 1) * SUB)
        part = decayed_rows(work_ref[1, :, lanes], local[c]) + jnp.exp(local[c]) * carry
        table_ref[0, :, lanes] = local[c]
        table_ref[1, :, lanes] = part
        carry = part[:, SUB - 1 : SUB]


def local_states(place, keys, values, decay, half, per):
    rows, columns = keys.shape
    heads = decay.shape[0]
    dim = columns // heads
    state = jax.ShapeDtypeStruct((per, half // 2, 3 * dim + EXTRA, dim), F32)
    table = jax.ShapeDtypeStruct((2, heads, rows), F32)
    return pl.pallas_call(
        functools.partial(states_kernel, half, per),
        out_shape=[state, state, table],
        in_specs=[pl.BlockSpec(memory_space=pltpu.SMEM)] + [whole(a) for a in (keys, values, decay)],
        out_specs=[whole(state), whole(state), whole(table)],
        scratch_shapes=[pltpu.VMEM((3, heads, rows), F32)],
        grid=(1,),
        compiler_params=FULL,
        cost_estimate=pl.CostEstimate(
            flops=16 * rows * dim * dim * half * per, bytes_accessed=8 * rows * columns, transcendentals=0
        ),
        name="local_states",
    )(place, keys, values, decay)


def join(earlier, later, dim):
    row_at = lax.broadcasted_iota(jnp.int32, later.shape, 1)
    column_at = lax.broadcasted_iota(jnp.int32, later.shape, 2)
    is_first = (row_at < dim) & (row_at <= column_at) | (row_at >= dim) & (row_at < 2 * dim)
    is_first = is_first | (row_at == 3 * dim)
    is_decay = (row_at == 3 * dim) | (row_at == 3 * dim + 1)
    factor = jnp.where(is_first, later[:, 3 * dim : 3 * dim + 1], later[:, 3 * dim + 1 : 3 * dim + 2])
    return factor * earlier + jnp.where(is_decay, 0.0, later)


def chip_kernel(dim, place_ref, own_ref, came_ref, *out_refs):
    is_first = place_ref[0] == 0
    for k, out_ref in enumerate(out_refs):
        own, came = own_ref[k], came_ref[k]
        out_ref[...] = join(jnp.where(is_first, own, came), jnp.where(is_first, came, own), dim)


def join_kernel(dim, place_ref, earlier_ref, later_ref, out_ref):
    out_ref[...] = join(earlier_ref[...], later_ref[...], dim)


def start_kernel(dim, k, place_ref, far_ref, near_ref, own_ref, came_ref, mine_ref, other_ref):
    is_first = place_ref[0] == 0
    before = join(far_ref[...], near_ref[...], dim)
    after = join(before, jnp.where(is_first, own_ref[k], came_ref[k]), dim)
    mine_ref[...] = jnp.where(is_first, before, after)
    other_ref[...] = jnp.where(is_first, after, before)


def combine(kernel, place, arrays, shape, outs):
    out = jax.ShapeDtypeStruct(shape, F32)
    return pl.pallas_call(
        kernel,
        out_shape=[out] * outs,
        in_specs=[pl.BlockSpec(memory_space=pltpu.SMEM)] + [whole(a) for a in arrays],
        out_specs=[whole(out)] * outs,
        grid=(1,),
        compiler_params=FULL,
        cost_estimate=pl.CostEstimate(
            flops=0, bytes_accessed=8 * sum(a.size for a in arrays), transcendentals=0
        ),
    )(place, *arrays)


def solve_kernel(with_query, with_gradient, bounds, head_of, place_ref, regular_ref, *refs):
    refs = list(refs)
    q_ref = refs.pop(0) if with_query else None
    g_ref = refs.pop(0) if with_gradient else None
    k_ref, v_ref, rows_ref = refs[:3]
    state_refs, refs = refs[3 : 3 + len(bounds)], refs[3 + len(bounds) :]
    turned_ref = refs.pop() if with_gradient else None
    mixed_ref = refs.pop() if with_query else None
    rows, dim = k_ref.shape
    pieces = range(rows // SUB)
    place = [slice(c * SUB, (c + 1) * SUB) for c in pieces]
    step = pl.program_id(0)
    head = head_of(step, place_ref)
    ridge = regular_ref[head]
    row_at = lax.broadcasted_iota(jnp.int32, (SUB, SUB), 0)
    column_at = lax.broadcasted_iota(jnp.int32, (SUB, SUB), 1)
    lower = row_at >= column_at

    is_second = lax.rem(step, 2) == 1

    def state(start, size):
        at = pl.ds(start, size)
        if len(state_refs) == 1:
            return state_refs[0][0, at, :]
        return jnp.where(step < bounds[1], state_refs[0][0, at, :], state_refs[1][0, at, :])

    packed = state(0, dim)
    direct = (row_at > column_at) == is_second
    start = jnp.where(direct, packed, packed.T)
    diagonal = state(3 * dim, EXTRA)[2:3]
    gram = [jnp.where((row_at == column_at) & is_second, diagonal, start)]
    memory = [state(pl.multiple_of((1 + lax.rem(step, 2)) * dim, dim), dim)]
    start_trace = jnp.sum(jnp.where(row_at == column_at, gram[0], 0.0), axis=0, keepdims=True)
    start_trace = jnp.sum(start_trace, axis=1, keepdims=True)
    cumulative_row = rows_ref[0, pl.ds(head, 1), :]
    cumulative = [cumulative_row[:, at] for at in place]
    last = [row[:, SUB - 1 : SUB] for row in cumulative]
    whole, offset = [], jnp.zeros((1, 1), F32)
    for c in pieces:
        whole.append(cumulative[c] + offset)
        offset = offset + last[c]
    trace = jnp.exp(jnp.concatenate(whole, axis=1)) * start_trace + rows_ref[1, pl.ds(head, 1), :]
    span = 0.5 * trace
    center = ridge + span
    alphas, gammas = [1.0 / center], []
    for i in range(1, ITERS):
        factor = 0.5 if i == 1 else 0.25
        product = span * alphas[-1]
        alphas.append(1.0 / (center - factor * span * product))
        gammas.append(alphas[-1] * (factor * span * product))
    table = jnp.concatenate(alphas + gammas + [cumulative_row], axis=0).T

    def column(index):
        return [jnp.broadcast_to(table[at, index : index + 1], (SUB, SUB)) for at in place]

    rise = column(2 * ITERS - 1)
    weights = [
        jnp.where(lower, jnp.exp(jnp.where(lower, rise[c] - cumulative[c], 0.0)), 0.0) for c in pieces
    ]
    scale = [jnp.exp(r) for r in rise]

    keys = [k_ref[at, :] for at in place]
    values = [v_ref[at, :] for at in place]
    keys_turned = [key.astype(F32).T for key in keys]
    values_turned = [value.astype(F32).T for value in values]
    for c in pieces[:-1]:
        tail = jnp.exp(last[c] - cumulative[c])
        decay = jnp.exp(last[c])
        both = jnp.concatenate([keys_turned[c] * tail, values_turned[c] * tail], axis=0)
        grown = dot(wide(both), jnp.concatenate([keys[c], keys[c]], axis=0))
        gram.append(decay * gram[-1] + grown[0:dim])
        memory.append(decay * memory[-1] + grown[dim:])
    keys_turned = [key.astype(BF16) for key in keys_turned]
    values_turned = [value.astype(BF16) for value in values_turned]

    def pair(left, right):
        return jnp.concatenate([left, right], axis=0)

    def each(value):
        return pair(value, value) if with_query and with_gradient else value

    residual = []
    for c in pieces:
        sides = []
        if with_query:
            sides.append(q_ref[place[c], :].astype(F32))
        if with_gradient:
            grad = g_ref[place[c], :]
            pulled = scale[c] * dot(jnp.concatenate([grad, grad], axis=1), wide(memory[c], 0))
            score = weights[c] * dot(grad, values_turned[c])
            sides.append(pulled + dot(wide(score), pair(keys[c], keys[c])))
        residual.append(jnp.concatenate(sides, axis=0) if len(sides) > 1 else sides[0])

    alpha = column(0)
    change = [each(alpha[c]) * residual[c] for c in pieces]
    solution = list(change)
    rights = [jnp.concatenate([keys_turned[c], gram[c].astype(BF16)], axis=1) for c in pieces]
    for i in range(1, ITERS):
        alpha, gamma = column(i), column(ITERS + i - 1)
        first = [dot(change[c].astype(BF16), rights[c]) for c in pieces]
        second = [
            dot((first[c][:, 0:SUB] * each(weights[c])).astype(BF16), keys[c]) for c in pieces
        ]
        for c in pieces:
            applied = ridge * change[c] + (each(scale[c]) * first[c][:, SUB:] + second[c])
            residual[c] = residual[c] - applied
            change[c] = each(alpha[c]) * residual[c] + each(gamma[c]) * change[c]
            solution[c] = solution[c] + change[c]

    if with_gradient:
        for c in pieces:
            turned_ref[0, :, place[c]] = solution[c][-SUB:].T.astype(BF16).astype(F32)
    for c in pieces if with_query else ():
        high, low = split(solution[c][0:SUB])
        memory_high, memory_low = split(memory[c].T)
        right = jnp.concatenate([keys_turned[c], memory_high], axis=1)
        first = dot(jnp.concatenate([high, low], axis=1), pair(right, right))
        second = first[:, SUB:] + dot(high, memory_low)
        score = weights[c] * first[:, 0:SUB]
        output = scale[c] * second + dot(wide(score), pair(values[c], values[c]))
        mixed_ref[place[c], :] = output.astype(BF16)


def solve_heads(place, k, base, per, regular, queries, grads, keys, values, table, states, mixed, after):
    rows, columns = keys.shape
    heads = regular.shape[0]
    dim = columns // heads
    half = 2 * states[0].shape[0]
    groups, count = heads // per, half * len(states)
    with_query, with_gradient = queries is not None, grads is not None
    bounds = [half * i for i in range(len(states))]

    def head_of(step, place_ref):
        return lax.rem(place_ref[0] * half + base + step, groups) * per + k

    def at_head(step, place_ref, regular_ref):
        return (0, head_of(step, place_ref))

    wide_spec = pl.BlockSpec((rows, dim), at_head)
    operands = [a for a in (queries, grads, keys, values) if a is not None]
    in_specs = [wide_spec] * len(operands)
    operands.append(table)
    in_specs.append(whole(table))
    for bound, state in zip(bounds, states):

        def at_pair(step, *_, bound=bound):
            return (jnp.clip(step - bound, 0, half - 1) // 2, 0, 0)

        operands.append(state)
        in_specs.append(pl.BlockSpec((1,) + state.shape[1:], at_pair))
    aliases = {}
    if with_query and mixed is not None:
        operands.append(mixed)
        in_specs.append(pl.BlockSpec(memory_space=pl.ANY))
        aliases = {2 + len(operands) - 1: 0}
    if after is not None:
        operands.append(after)
        in_specs.append(pl.BlockSpec(memory_space=pl.ANY))
    shapes, out_specs = [], []
    if with_query:
        shapes.append(jax.ShapeDtypeStruct((rows, columns), BF16))
        out_specs.append(wide_spec)
    if with_gradient:
        shapes.append(jax.ShapeDtypeStruct((count, dim, rows), F32))
        out_specs.append(pl.BlockSpec((1, dim, rows), lambda step, *_: (step, 0, 0)))
    return pl.pallas_call(
        functools.partial(solve_kernel, with_query, with_gradient, bounds, head_of),
        out_shape=shapes,
        grid_spec=pltpu.PrefetchScalarGridSpec(
            num_scalar_prefetch=2, grid=(count,), in_specs=in_specs, out_specs=out_specs
        ),
        input_output_aliases=aliases,
        cost_estimate=pl.CostEstimate(
            flops=count * 80 * rows * dim * dim, bytes_accessed=count * 14 * rows * dim, transcendentals=0
        ),
        compiler_params=FULL,
        name="solve_heads",
    )(place, regular, *operands)


def pick_kernel(core_ref, tokens_ref, out_ref):
    out_ref[0] = tokens_ref[...].astype(F32)


def pick_columns(core, tokens, blocks):
    rows, width = tokens.shape
    size = width // (2 * blocks)
    return pl.pallas_call(
        pick_kernel,
        out_shape=jax.ShapeDtypeStruct((blocks, rows, size), F32),
        grid_spec=pltpu.PrefetchScalarGridSpec(
            num_scalar_prefetch=1,
            grid=(blocks,),
            in_specs=[pl.BlockSpec((rows, size), lambda z, core_ref: (0, 2 * z + 1 - core_ref[0]))],
            out_specs=pl.BlockSpec((1, rows, size), lambda z, core_ref: (z, 0, 0)),
        ),
        cost_estimate=pl.CostEstimate(flops=0, bytes_accessed=3 * rows * width, transcendentals=0),
        compiler_params=FULL,
        name="pick_columns",
    )(core, tokens)


def narrow_kernel(in_ref, out_ref):
    out_ref[...] = in_ref[...].astype(BF16)


def narrow(blocks):
    spec = pl.BlockSpec((1,) + blocks.shape[1:], lambda z: (z, 0, 0))
    return pl.pallas_call(
        narrow_kernel,
        out_shape=jax.ShapeDtypeStruct(blocks.shape, BF16),
        grid=(blocks.shape[0],),
        in_specs=[spec],
        out_specs=spec,
        cost_estimate=pl.CostEstimate(flops=0, bytes_accessed=6 * blocks.size, transcendentals=0),
        compiler_params=FULL,
        name="narrow",
    )(blocks)


def gradient_kernel(order, place_ref, own_ref, far_ref, tokens_ref, other_ref, *rest):
    outs, left_ref = rest[:-1], rest[-1]
    core, group = place_ref[0], place_ref[1]
    count, dim, rows = own_ref.shape
    half = count // 2
    middle = dim // 2

    @pl.when(pl.program_id(0) == 0)
    def _():
        for i in range(half):
            near, away = (core * half + i) ^ group, ((1 - core) * half + i) ^ group
            left_ref[near, :, 0:rows] = own_ref[i].astype(BF16)
            left_ref[away, :, 0:rows] = own_ref[half + i].astype(BF16)
            left_ref[near, :, rows:] = far_ref[half + i].astype(BF16)
            left_ref[away, :, rows:] = far_ref[i].astype(BF16)

    left = left_ref[...].reshape(2 * half * dim, 2 * rows)
    result = dot(left, jnp.concatenate([tokens_ref[...], other_ref[0]], axis=0))
    for d in range(2 * half):
        for path in range(2):
            which, index = order[path][d]
            start = d * dim + path * middle
            outs[2 * path + which][index, 0] = result[start : start + middle]


def gradient_blocks(place, own, far, tokens, other, order):
    count, dim, rows = own.shape
    half = count // 2
    blocks, _, size = other.shape
    out = jax.ShapeDtypeStruct((half, blocks, dim // 2, size), F32)
    turned_spec = pl.BlockSpec((count, dim, rows), lambda z, p: (0, 0, 0))
    return pl.pallas_call(
        functools.partial(gradient_kernel, order),
        out_shape=[out] * 4,
        grid_spec=pltpu.PrefetchScalarGridSpec(
            num_scalar_prefetch=1,
            grid=(blocks,),
            in_specs=[turned_spec] * 2
            + [
                pl.BlockSpec((rows, size), lambda z, p: (0, 2 * (p[2] ^ z) + p[0])),
                pl.BlockSpec((1, rows, size), lambda z, p: (p[2] ^ z, 0, 0)),
            ],
            out_specs=[pl.BlockSpec((half, 1, dim // 2, size), lambda z, p: (0, z, 0, 0))] * 4,
            scratch_shapes=[pltpu.VMEM((2 * half, dim, 2 * rows), BF16)],
        ),
        cost_estimate=pl.CostEstimate(
            flops=8 * half * dim * rows * blocks * size,
            bytes_accessed=4 * (4 * half * dim * rows + blocks * rows * size + 2 * half * blocks * dim * size),
            transcendentals=0,
        ),
        compiler_params=FULL,
        name="gradient_blocks",
    )(place, own, far, tokens, other)


def sum_kernel(keep_ref, came_ref, keep_out, send_out):
    out_half = keep_out.shape[0]
    for i in range(out_half):
        send_out[i] = keep_ref[out_half + i] + came_ref[out_half + i]
    for i in range(out_half):
        keep_out[i] = keep_ref[i] + came_ref[i]


def sum_blocks(keep, came):
    out = jax.ShapeDtypeStruct((keep.shape[0] // 2,) + keep.shape[1:], F32)
    return pl.pallas_call(
        sum_kernel,
        out_shape=[out] * 2,
        in_specs=[whole(keep)] * 2,
        out_specs=[whole(out)] * 2,
        grid=(1,),
        compiler_params=FULL,
        cost_estimate=pl.CostEstimate(flops=0, bytes_accessed=12 * keep.size, transcendentals=0),
        name="sum_blocks",
    )(keep, came)


def merge_kernel(count, *refs):
    sums, outs = refs[: 2 * count], refs[2 * count :]
    rows = sums[0].shape[2]
    for z, out in enumerate(outs):
        for i in range(count):
            out[i * rows : (i + 1) * rows, :] = sums[2 * i][0, z] + sums[2 * i + 1][0, z]


def merge_blocks(sums):
    _, chips, rows, size = sums[0].shape
    count = len(sums) // 2
    out = jax.ShapeDtypeStruct((count * rows, size), F32)
    return pl.pallas_call(
        functools.partial(merge_kernel, count),
        out_shape=[out] * chips,
        in_specs=[whole(a) for a in sums],
        out_specs=[whole(out)] * chips,
        grid=(1,),
        compiler_params=FULL,
        cost_estimate=pl.CostEstimate(
            flops=0, bytes_accessed=6 * sum(a.size for a in sums), transcendentals=0
        ),
        name="merge_blocks",
    )(*sums)


def finish_kernel(count, *refs):
    out = refs[-1]
    rows = refs[0].shape[0]
    for k in range((len(refs) - 1) // count):
        total = refs[k * count][...]
        for ref in refs[k * count + 1 : (k + 1) * count]:
            total = total + ref[...]
        out[k * rows : (k + 1) * rows, :] = total


def finish(sets):
    arrays = [a for group in sets for a in group]
    rows, size = arrays[0].shape
    out = jax.ShapeDtypeStruct((rows * len(sets), size), F32)
    return pl.pallas_call(
        functools.partial(finish_kernel, len(sets[0])),
        out_shape=out,
        in_specs=[whole(a) for a in arrays],
        out_specs=whole(out),
        grid=(1,),
        compiler_params=FULL,
        cost_estimate=pl.CostEstimate(
            flops=0, bytes_accessed=5 * sum(a.size for a in arrays), transcendentals=0
        ),
        name="finish",
    )(*arrays)


def bit_order(bits):
    table = []
    for d in range(1 << len(bits)):
        code = 0
        for bit in bits:
            code = 2 * code + ((d >> bit) & 1)
        table.append(divmod(code, 1 << (len(bits) - 1)))
    return table


def per_device(sizes, *arrays):
    return program(sizes, *arrays)


def program(sizes, tokens, w_query, keys, values, log_decay, regular, grad_out):
    groups, steps = sizes["dp"], sizes["seq"]
    chips = steps // 2
    heads = log_decay.shape[1]
    columns = keys.shape[2]
    dim = columns // heads
    per = heads // groups
    half = groups // 2
    tokens, keys, values, grads, decay = tokens[0], keys[0], values[0], grad_out[0], log_decay[0]
    here = lax.axis_index("seq")
    core = here % 2
    place = jnp.stack([core, lax.axis_index("dp"), here // 2]).astype(jnp.int32)
    partner = [(i, i ^ 1) for i in range(steps)]

    own, away, table = local_states(place, keys, values, decay, half, per)
    came = lax.ppermute(away, "seq", partner)
    shape = own.shape[1:]
    chip_states = combine(functools.partial(chip_kernel, dim), place, [own, came], shape, per)
    joined = functools.partial(join_kernel, dim)
    starts = []
    for k, chip_state in enumerate(chip_states):
        window, near, far = 0, None, None
        while window < chips - 1:
            if far is not None:
                (near,) = combine(joined, place, [far, near], shape, 1)
            sent = chip_state
            if near is not None:
                (sent,) = combine(joined, place, [near, chip_state], shape, 1)
            shift = 2 * (window + 1)
            pairs = [(i, i + shift) for i in range(steps - shift)]
            came_up = lax.ppermute(sent, "seq", pairs)
            near, far = (came_up, None) if near is None else (near, came_up)
            window = 2 * window + 1
        starting = functools.partial(start_kernel, dim, k)
        mine, others = combine(starting, place, [far, near, own, came], shape, 2)
        starts.append((mine, lax.ppermute(others, "seq", partner)))

    picked = pick_columns(place, tokens, chips)
    other = lax.ppermute(picked, "seq", partner)
    other = narrow(other)
    queries = jnp.dot(tokens, w_query, preferred_element_type=F32).astype(BF16)

    dp_bits = groups.bit_length() - 1
    paths = [list(range(dp_bits)), list(reversed(range(dp_bits)))]
    order = [bit_order(path) for path in paths]

    products, mixed = [], None
    for k, states in enumerate(starts):
        after = products[-1][0] if k > 0 else None
        joint = k < per - 1
        results = solve_heads(
            place, k, 0, per, regular, queries if joint else None, grads, keys, values, table, states, mixed, after
        )
        turned = results[-1]
        if joint:
            mixed = results[0]
        far = lax.ppermute(turned, "seq", partner)
        products.append(gradient_blocks(place, turned, far, tokens, other, order))
    for side in range(2):
        after = products[-1][0] if side == 0 else None
        (mixed,) = solve_heads(
            place, per - 1, side * half, per, regular, queries, None, keys, values, table,
            [starts[-1][side]], mixed, after,
        )

    finished = []
    for blocks in products:
        sums = []
        for index, path in enumerate(paths):
            keep, send = blocks[2 * index], blocks[2 * index + 1]
            for bit in path:
                pairs = [(i, i ^ (1 << bit)) for i in range(groups)]
                came = lax.ppermute(send, "dp", pairs)
                if bit == path[-1]:
                    sums += [keep, came]
                else:
                    keep, send = sum_blocks(keep, came)
        out, *others = merge_blocks(sums)
        finished.append([out])
        for z, other_block in enumerate(others, 1):
            pairs = [(i, i ^ (2 * z)) for i in range(steps)]
            finished[-1].append(lax.ppermute(other_block, "seq", pairs))
    return mixed[None], finish(finished)


def solution(mesh):
    sizes = dict(mesh.shape)
    in_specs = (
        P("dp", "seq", None),
        P(),
        P("dp", "seq", None),
        P("dp", "seq", None),
        P("dp", None, "seq"),
        P(),
        P("dp", "seq", None),
    )
    out_specs = (P("dp", "seq", None), P("dp", "seq"))
    return jax.shard_map(
        functools.partial(per_device, sizes),
        mesh=mesh,
        in_specs=in_specs,
        out_specs=out_specs,
        check_vma=False,
    )
```

```python
import functools

import jax
import jax.numpy as jnp
from jax import lax
from jax.experimental import pallas as pl
from jax.experimental.pallas import tpu as pltpu
from jax.sharding import PartitionSpec as P

ITERS = 4
SUB = 128
EXTRA = 8


F32 = jnp.float32
BF16 = jnp.bfloat16


FULL = pltpu.CompilerParams(vmem_limit_bytes=67_043_328)


def whole(array):
    return pl.BlockSpec(array.shape, lambda *_: (0,) * len(array.shape))


def dot(left, right):
    return jnp.dot(left, right, preferred_element_type=F32)


def split(value):
    high = value.astype(BF16)
    low = (value - high.astype(F32)).astype(BF16)
    return high, low


def wide(value, axis=1):
    return jnp.concatenate(split(value), axis=axis)


def lane_shift(value, step):
    lanes = lax.broadcasted_iota(jnp.int32, value.shape, 1)
    return jnp.where(lanes >= step, pltpu.roll(value, step, 1), 0.0), lanes >= step


def cumulative_rows(value):
    step = 1
    while step < value.shape[1]:
        value = value + lane_shift(value, step)[0]
        step *= 2
    return value


def decayed_rows(value, cumulative):
    step = 1
    while step < value.shape[1]:
        earlier, inside = lane_shift(cumulative, step)
        factor = jnp.exp(jnp.where(inside, cumulative - earlier, 0.0))
        value = value + factor * lane_shift(value, step)[0]
        step *= 2
    return value


def decay_tables(decay_ref):
    rows = decay_ref.shape[1]
    offset = jnp.zeros((decay_ref.shape[0], 1), F32)
    local, full = [], []
    for c in range(rows // SUB):
        part = cumulative_rows(decay_ref[:, c * SUB : (c + 1) * SUB])
        local.append(part)
        full.append(part + offset)
        offset = offset + part[:, SUB - 1 : SUB]
    return local, jnp.exp(offset - jnp.concatenate(full, axis=1)), jnp.exp(offset)


def states_kernel(half, per, place_ref, keys_ref, values_ref, decay_ref, near_ref, away_ref, table_ref, work_ref):
    rows, dim = keys_ref.shape[0], SUB
    core = place_ref[0]
    row_at = lax.broadcasted_iota(jnp.int32, (dim, dim), 0)
    column_at = lax.broadcasted_iota(jnp.int32, (dim, dim), 1)
    local, tails, total = decay_tables(decay_ref)
    work_ref[0] = tails
    work_ref[2] = jnp.broadcast_to(total, tails.shape)
    for out, block in ((away_ref, 1 - core), (near_ref, core)):
        for k in range(per):
            for i in range(half):
                head = (block * half + i) * per + k
                column = pl.ds(pl.multiple_of(head * dim, dim), dim)
                key = keys_ref[:, column]
                tail = work_ref[0, pl.ds(head, 1), :]
                key_turned = key.astype(F32).T
                value_turned = values_ref[:, column].astype(F32).T
                work_ref[1, pl.ds(head, 1), :] = jnp.sum(key_turned * key_turned, axis=0, keepdims=True)
                high, low = split(jnp.concatenate([key_turned * tail, value_turned * tail], axis=0))
                state = dot(high, key) + dot(low, key)
                gram = state[0:dim]
                at, second = i // 2, i % 2
                out[k, at, (1 + second) * dim : (2 + second) * dim, :] = state[dim:]
                decay = work_ref[2, pl.ds(head, 1), :][:, 0:SUB]
                out[k, at, 3 * dim + second : 3 * dim + second + 1, :] = decay
                if second == 0:
                    first_gram = gram
                else:
                    out[k, at, 0:dim, :] = jnp.where(row_at <= column_at, first_gram, gram)
                    diagonal = jnp.sum(jnp.where(row_at == column_at, gram, 0.0), axis=0, keepdims=True)
                    out[k, at, 3 * dim + 2 : 3 * dim + 3, :] = diagonal
                    out[k, at, 3 * dim + 3 :, :] = jnp.zeros((EXTRA - 3, dim), F32)
    carry = jnp.zeros_like(total)
    for c in range(rows // SUB):
        lanes = slice(c * SUB, (c + 1) * SUB)
        part = decayed_rows(work_ref[1, :, lanes], local[c]) + jnp.exp(local[c]) * carry
        table_ref[0, :, lanes] = local[c]
        table_ref[1, :, lanes] = part
        carry = part[:, SUB - 1 : SUB]


def local_states(place, keys, values, decay, half, per):
    rows, columns = keys.shape
    heads = decay.shape[0]
    dim = columns // heads
    state = jax.ShapeDtypeStruct((per, half // 2, 3 * dim + EXTRA, dim), F32)
    table = jax.ShapeDtypeStruct((2, heads, rows), F32)
    return pl.pallas_call(
        functools.partial(states_kernel, half, per),
        out_shape=[state, state, table],
        in_specs=[pl.BlockSpec(memory_space=pltpu.SMEM)] + [whole(a) for a in (keys, values, decay)],
        out_specs=[whole(state), whole(state), whole(table)],
        scratch_shapes=[pltpu.VMEM((3, heads, rows), F32)],
        grid=(1,),
        compiler_params=FULL,
        cost_estimate=pl.CostEstimate(
            flops=16 * rows * dim * dim * half * per, bytes_accessed=8 * rows * columns, transcendentals=0
        ),
        name="local_states",
    )(place, keys, values, decay)


def join(earlier, later, dim):
    row_at = lax.broadcasted_iota(jnp.int32, later.shape, 1)
    column_at = lax.broadcasted_iota(jnp.int32, later.shape, 2)
    is_first = (row_at < dim) & (row_at <= column_at) | (row_at >= dim) & (row_at < 2 * dim)
    is_first = is_first | (row_at == 3 * dim)
    is_decay = (row_at == 3 * dim) | (row_at == 3 * dim + 1)
    factor = jnp.where(is_first, later[:, 3 * dim : 3 * dim + 1], later[:, 3 * dim + 1 : 3 * dim + 2])
    return factor * earlier + jnp.where(is_decay, 0.0, later)


def chip_kernel(dim, place_ref, own_ref, came_ref, *out_refs):
    is_first = place_ref[0] == 0
    for k, out_ref in enumerate(out_refs):
        own, came = own_ref[k], came_ref[k]
        out_ref[...] = join(jnp.where(is_first, own, came), jnp.where(is_first, came, own), dim)


def start_kernel(dim, k, place_ref, own_ref, came_ref, *refs):
    sent_refs, (mine_ref, other_ref) = refs[:-2], refs[-2:]
    is_first = place_ref[0] == 0
    before = sent_refs[-1][...]
    for ref in reversed(sent_refs[:-1]):
        before = join(before, ref[...], dim)
    after = join(before, jnp.where(is_first, own_ref[k], came_ref[k]), dim)
    mine_ref[...] = jnp.where(is_first, before, after)
    other_ref[...] = jnp.where(is_first, after, before)


def combine(kernel, place, arrays, shape, outs):
    out = jax.ShapeDtypeStruct(shape, F32)
    return pl.pallas_call(
        kernel,
        out_shape=[out] * outs,
        in_specs=[pl.BlockSpec(memory_space=pltpu.SMEM)] + [whole(a) for a in arrays],
        out_specs=[whole(out)] * outs,
        grid=(1,),
        compiler_params=FULL,
        cost_estimate=pl.CostEstimate(
            flops=0, bytes_accessed=8 * sum(a.size for a in arrays), transcendentals=0
        ),
    )(place, *arrays)


def solve_kernel(with_query, with_gradient, bounds, head_of, place_ref, regular_ref, *refs):
    refs = list(refs)
    q_ref = refs.pop(0) if with_query else None
    g_ref = refs.pop(0) if with_gradient else None
    k_ref, v_ref, rows_ref = refs[:3]
    state_refs, refs = refs[3 : 3 + len(bounds)], refs[3 + len(bounds) :]
    turned_ref = refs.pop() if with_gradient else None
    mixed_ref = refs.pop() if with_query else None
    rows, dim = k_ref.shape
    pieces = range(rows // SUB)
    place = [slice(c * SUB, (c + 1) * SUB) for c in pieces]
    step = pl.program_id(0)
    head = head_of(step, place_ref)
    ridge = regular_ref[head]
    row_at = lax.broadcasted_iota(jnp.int32, (SUB, SUB), 0)
    column_at = lax.broadcasted_iota(jnp.int32, (SUB, SUB), 1)
    lower = row_at >= column_at

    is_second = lax.rem(step, 2) == 1

    def state(start, size):
        at = pl.ds(start, size)
        if len(state_refs) == 1:
            return state_refs[0][0, at, :]
        return jnp.where(step < bounds[1], state_refs[0][0, at, :], state_refs[1][0, at, :])

    packed = state(0, dim)
    direct = (row_at > column_at) == is_second
    start = jnp.where(direct, packed, packed.T)
    diagonal = state(3 * dim, EXTRA)[2:3]
    gram = [jnp.where((row_at == column_at) & is_second, diagonal, start)]
    memory = [state(pl.multiple_of((1 + lax.rem(step, 2)) * dim, dim), dim)]
    start_trace = jnp.sum(jnp.where(row_at == column_at, gram[0], 0.0), axis=0, keepdims=True)
    start_trace = jnp.sum(start_trace, axis=1, keepdims=True)
    cumulative_row = rows_ref[0, pl.ds(head, 1), :]
    cumulative = [cumulative_row[:, at] for at in place]
    last = [row[:, SUB - 1 : SUB] for row in cumulative]
    whole, offset = [], jnp.zeros((1, 1), F32)
    for c in pieces:
        whole.append(cumulative[c] + offset)
        offset = offset + last[c]
    trace = jnp.exp(jnp.concatenate(whole, axis=1)) * start_trace + rows_ref[1, pl.ds(head, 1), :]
    span = 0.5 * trace
    center = ridge + span
    alphas, gammas = [1.0 / center], []
    for i in range(1, ITERS):
        factor = 0.5 if i == 1 else 0.25
        product = span * alphas[-1]
        alphas.append(1.0 / (center - factor * span * product))
        gammas.append(alphas[-1] * (factor * span * product))
    table = jnp.concatenate(alphas + gammas + [cumulative_row], axis=0).T

    def column(index):
        return [jnp.broadcast_to(table[at, index : index + 1], (SUB, SUB)) for at in place]

    rise = column(2 * ITERS - 1)
    weights = [
        jnp.where(lower, jnp.exp(jnp.where(lower, rise[c] - cumulative[c], 0.0)), 0.0) for c in pieces
    ]
    scale = [jnp.exp(r) for r in rise]

    keys = [k_ref[at, :] for at in place]
    values = [v_ref[at, :] for at in place]
    keys_turned = [key.astype(F32).T for key in keys]
    values_turned = [value.astype(F32).T for value in values]
    for c in pieces[:-1]:
        tail = jnp.exp(last[c] - cumulative[c])
        decay = jnp.exp(last[c])
        both = jnp.concatenate([keys_turned[c] * tail, values_turned[c] * tail], axis=0)
        grown = dot(wide(both), jnp.concatenate([keys[c], keys[c]], axis=0))
        gram.append(decay * gram[-1] + grown[0:dim])
        memory.append(decay * memory[-1] + grown[dim:])
    keys_turned = [key.astype(BF16) for key in keys_turned]
    values_turned = [value.astype(BF16) for value in values_turned]

    def pair(left, right):
        return jnp.concatenate([left, right], axis=0)

    def each(value):
        return pair(value, value) if with_query and with_gradient else value

    residual = []
    for c in pieces:
        sides = []
        if with_query:
            sides.append(q_ref[place[c], :].astype(F32))
        if with_gradient:
            grad = g_ref[place[c], :]
            pulled = scale[c] * dot(jnp.concatenate([grad, grad], axis=1), wide(memory[c], 0))
            score = weights[c] * dot(grad, values_turned[c])
            sides.append(pulled + dot(wide(score), pair(keys[c], keys[c])))
        residual.append(jnp.concatenate(sides, axis=0) if len(sides) > 1 else sides[0])

    alpha = column(0)
    change = [each(alpha[c]) * residual[c] for c in pieces]
    solution = list(change)
    rights = [jnp.concatenate([keys_turned[c], gram[c].astype(BF16)], axis=1) for c in pieces]
    for i in range(1, ITERS):
        alpha, gamma = column(i), column(ITERS + i - 1)
        first = [dot(change[c].astype(BF16), rights[c]) for c in pieces]
        second = [
            dot((first[c][:, 0:SUB] * each(weights[c])).astype(BF16), keys[c]) for c in pieces
        ]
        for c in pieces:
            applied = ridge * change[c] + (each(scale[c]) * first[c][:, SUB:] + second[c])
            residual[c] = residual[c] - applied
            change[c] = each(alpha[c]) * residual[c] + each(gamma[c]) * change[c]
            solution[c] = solution[c] + change[c]

    if with_gradient:
        for c in pieces:
            turned_ref[0, :, place[c]] = solution[c][-SUB:].T.astype(BF16).astype(F32)
    for c in pieces if with_query else ():
        high, low = split(solution[c][0:SUB])
        memory_high, memory_low = split(memory[c].T)
        right = jnp.concatenate([keys_turned[c], memory_high], axis=1)
        first = dot(jnp.concatenate([high, low], axis=1), pair(right, right))
        second = first[:, SUB:] + dot(high, memory_low)
        score = weights[c] * first[:, 0:SUB]
        output = scale[c] * second + dot(wide(score), pair(values[c], values[c]))
        mixed_ref[place[c], :] = output.astype(BF16)


def solve_heads(place, k, base, per, regular, queries, grads, keys, values, table, states, mixed, after):
    rows, columns = keys.shape
    heads = regular.shape[0]
    dim = columns // heads
    half = 2 * states[0].shape[0]
    groups, count = heads // per, half * len(states)
    with_query, with_gradient = queries is not None, grads is not None
    bounds = [half * i for i in range(len(states))]

    def head_of(step, place_ref):
        return lax.rem(place_ref[0] * half + base + step, groups) * per + k

    def at_head(step, place_ref, regular_ref):
        return (0, head_of(step, place_ref))

    wide_spec = pl.BlockSpec((rows, dim), at_head)
    operands = [a for a in (queries, grads, keys, values) if a is not None]
    in_specs = [wide_spec] * len(operands)
    operands.append(table)
    in_specs.append(whole(table))
    for bound, state in zip(bounds, states):

        def at_pair(step, *_, bound=bound):
            return (jnp.clip(step - bound, 0, half - 1) // 2, 0, 0)

        operands.append(state)
        in_specs.append(pl.BlockSpec((1,) + state.shape[1:], at_pair))
    aliases = {}
    if with_query and mixed is not None:
        operands.append(mixed)
        in_specs.append(pl.BlockSpec(memory_space=pl.ANY))
        aliases = {2 + len(operands) - 1: 0}
    if after is not None:
        operands.append(after)
        in_specs.append(pl.BlockSpec(memory_space=pl.ANY))
    shapes, out_specs = [], []
    if with_query:
        shapes.append(jax.ShapeDtypeStruct((rows, columns), BF16))
        out_specs.append(wide_spec)
    if with_gradient:
        shapes.append(jax.ShapeDtypeStruct((count, dim, rows), F32))
        out_specs.append(pl.BlockSpec((1, dim, rows), lambda step, *_: (step, 0, 0)))
    return pl.pallas_call(
        functools.partial(solve_kernel, with_query, with_gradient, bounds, head_of),
        out_shape=shapes,
        grid_spec=pltpu.PrefetchScalarGridSpec(
            num_scalar_prefetch=2, grid=(count,), in_specs=in_specs, out_specs=out_specs
        ),
        input_output_aliases=aliases,
        cost_estimate=pl.CostEstimate(
            flops=count * 80 * rows * dim * dim, bytes_accessed=count * 14 * rows * dim, transcendentals=0
        ),
        compiler_params=FULL,
        name="solve_heads",
    )(place, regular, *operands)


def pick_kernel(core_ref, tokens_ref, out_ref):
    out_ref[0] = tokens_ref[...].astype(F32)


def pick_columns(core, tokens, blocks):
    rows, width = tokens.shape
    size = width // (2 * blocks)
    return pl.pallas_call(
        pick_kernel,
        out_shape=jax.ShapeDtypeStruct((blocks, rows, size), F32),
        grid_spec=pltpu.PrefetchScalarGridSpec(
            num_scalar_prefetch=1,
            grid=(blocks,),
            in_specs=[pl.BlockSpec((rows, size), lambda z, core_ref: (0, 2 * z + 1 - core_ref[0]))],
            out_specs=pl.BlockSpec((1, rows, size), lambda z, core_ref: (z, 0, 0)),
        ),
        cost_estimate=pl.CostEstimate(flops=0, bytes_accessed=3 * rows * width, transcendentals=0),
        compiler_params=FULL,
        name="pick_columns",
    )(core, tokens)


def narrow_kernel(in_ref, out_ref):
    out_ref[...] = in_ref[...].astype(BF16)


def narrow(blocks):
    spec = pl.BlockSpec((1,) + blocks.shape[1:], lambda z: (z, 0, 0))
    return pl.pallas_call(
        narrow_kernel,
        out_shape=jax.ShapeDtypeStruct(blocks.shape, BF16),
        grid=(blocks.shape[0],),
        in_specs=[spec],
        out_specs=spec,
        cost_estimate=pl.CostEstimate(flops=0, bytes_accessed=6 * blocks.size, transcendentals=0),
        compiler_params=FULL,
        name="narrow",
    )(blocks)


def gradient_kernel(order, place_ref, own_ref, far_ref, tokens_ref, other_ref, *rest):
    outs, left_ref = rest[:-1], rest[-1]
    core, group = place_ref[0], place_ref[1]
    count, dim, rows = own_ref.shape
    half = count // 2
    middle = dim // 2

    @pl.when(pl.program_id(0) == 0)
    def _():
        for i in range(half):
            near, away = (core * half + i) ^ group, ((1 - core) * half + i) ^ group
            left_ref[near, :, 0:rows] = own_ref[i].astype(BF16)
            left_ref[away, :, 0:rows] = own_ref[half + i].astype(BF16)
            left_ref[near, :, rows:] = far_ref[half + i].astype(BF16)
            left_ref[away, :, rows:] = far_ref[i].astype(BF16)

    left = left_ref[...].reshape(2 * half * dim, 2 * rows)
    result = dot(left, jnp.concatenate([tokens_ref[...], other_ref[0]], axis=0))
    for d in range(2 * half):
        for path in range(2):
            which, index = order[path][d]
            start = d * dim + path * middle
            outs[2 * path + which][index, 0] = result[start : start + middle]


def gradient_blocks(place, own, far, tokens, other, order):
    count, dim, rows = own.shape
    half = count // 2
    blocks, _, size = other.shape
    out = jax.ShapeDtypeStruct((half, blocks, dim // 2, size), F32)
    turned_spec = pl.BlockSpec((count, dim, rows), lambda z, p: (0, 0, 0))
    return pl.pallas_call(
        functools.partial(gradient_kernel, order),
        out_shape=[out] * 4,
        grid_spec=pltpu.PrefetchScalarGridSpec(
            num_scalar_prefetch=1,
            grid=(blocks,),
            in_specs=[turned_spec] * 2
            + [
                pl.BlockSpec((rows, size), lambda z, p: (0, 2 * (p[2] ^ z) + p[0])),
                pl.BlockSpec((1, rows, size), lambda z, p: (p[2] ^ z, 0, 0)),
            ],
            out_specs=[pl.BlockSpec((half, 1, dim // 2, size), lambda z, p: (0, z, 0, 0))] * 4,
            scratch_shapes=[pltpu.VMEM((2 * half, dim, 2 * rows), BF16)],
        ),
        cost_estimate=pl.CostEstimate(
            flops=8 * half * dim * rows * blocks * size,
            bytes_accessed=4 * (4 * half * dim * rows + blocks * rows * size + 2 * half * blocks * dim * size),
            transcendentals=0,
        ),
        compiler_params=FULL,
        name="gradient_blocks",
    )(place, own, far, tokens, other)


def sum_kernel(*refs):
    total = refs[0][...]
    for ref in refs[1:-1]:
        total = total + ref[...]
    refs[-1][...] = total


def sum_blocks(arrays, length):
    out = jax.ShapeDtypeStruct((length,) + arrays[0].shape[1:], F32)
    spec = pl.BlockSpec(out.shape, lambda _: (1, 0, 0, 0))
    return pl.pallas_call(
        sum_kernel,
        out_shape=out,
        in_specs=[spec] * len(arrays),
        out_specs=whole(out),
        grid=(1,),
        compiler_params=FULL,
        cost_estimate=pl.CostEstimate(flops=0, bytes_accessed=12 * out.size // length, transcendentals=0),
        name="sum_blocks",
    )(*arrays)


def merge_kernel(counts, *refs):
    sums, outs = refs[: sum(counts)], refs[sum(counts) :]
    rows = sums[0].shape[2]
    at = 0
    for i, count in enumerate(counts):
        for z, out in enumerate(outs):
            total = sums[at][0, z]
            for ref in sums[at + 1 : at + count]:
                total = total + ref[0, z]
            out[i * rows : (i + 1) * rows, :] = total
        at += count


def merge_blocks(sums):
    counts = [len(arrays) for arrays in sums]
    arrays = [a for group in sums for a in group]
    _, chips, rows, size = arrays[0].shape
    out = jax.ShapeDtypeStruct((len(counts) * rows, size), F32)
    return pl.pallas_call(
        functools.partial(merge_kernel, counts),
        out_shape=[out] * chips,
        in_specs=[pl.BlockSpec((1, chips, rows, size), lambda _: (0, 0, 0, 0))] * len(arrays),
        out_specs=[whole(out)] * chips,
        grid=(1,),
        compiler_params=FULL,
        cost_estimate=pl.CostEstimate(
            flops=0, bytes_accessed=4 * (len(arrays) + 2) * chips * rows * size, transcendentals=0
        ),
        name="merge_blocks",
    )(*arrays)


def finish_kernel(count, *refs):
    out = refs[-1]
    rows = refs[0].shape[0]
    for k in range((len(refs) - 1) // count):
        total = refs[k * count][...]
        for ref in refs[k * count + 1 : (k + 1) * count]:
            total = total + ref[...]
        out[k * rows : (k + 1) * rows, :] = total


def finish(sets):
    arrays = [a for group in sets for a in group]
    rows, size = arrays[0].shape
    out = jax.ShapeDtypeStruct((rows * len(sets), size), F32)
    return pl.pallas_call(
        functools.partial(finish_kernel, len(sets[0])),
        out_shape=out,
        in_specs=[whole(a) for a in arrays],
        out_specs=whole(out),
        grid=(1,),
        compiler_params=FULL,
        cost_estimate=pl.CostEstimate(
            flops=0, bytes_accessed=5 * sum(a.size for a in arrays), transcendentals=0
        ),
        name="finish",
    )(*arrays)


def bit_order(bits):
    table = []
    for d in range(1 << len(bits)):
        code = 0
        for bit in bits:
            code = 2 * code + ((d >> bit) & 1)
        table.append(divmod(code, 1 << (len(bits) - 1)))
    return table


def per_device(sizes, *arrays):
    return program(sizes, *arrays)


def program(sizes, tokens, w_query, keys, values, log_decay, regular, grad_out):
    groups, steps = sizes["dp"], sizes["seq"]
    chips = steps // 2
    heads = log_decay.shape[1]
    columns = keys.shape[2]
    dim = columns // heads
    per = heads // groups
    half = groups // 2
    tokens, keys, values, grads, decay = tokens[0], keys[0], values[0], grad_out[0], log_decay[0]
    here = lax.axis_index("seq")
    core = here % 2
    place = jnp.stack([core, lax.axis_index("dp"), here // 2]).astype(jnp.int32)
    partner = [(i, i ^ 1) for i in range(steps)]

    own, away, table = local_states(place, keys, values, decay, half, per)
    came = lax.ppermute(away, "seq", partner)
    shape = own.shape[1:]
    chip_states = combine(functools.partial(chip_kernel, dim), place, [own, came], shape, per)
    starts = []
    for k, chip_state in enumerate(chip_states):
        sent = []
        for z in range(1, chips):
            pairs = [(i, i + 2 * z) for i in range(steps - 2 * z)]
            sent.append(lax.ppermute(chip_state, "seq", pairs))
        starting = functools.partial(start_kernel, dim, k)
        mine, others = combine(starting, place, [own, came, *sent], shape, 2)
        starts.append((mine, lax.ppermute(others, "seq", partner)))

    picked = pick_columns(place, tokens, chips)
    other = lax.ppermute(picked, "seq", partner)
    other = narrow(other)
    queries = jnp.dot(tokens, w_query, preferred_element_type=F32).astype(BF16)

    dp_bits = groups.bit_length() - 1
    paths = [list(range(dp_bits)), list(reversed(range(dp_bits)))]
    order = [bit_order(path) for path in paths]

    products, mixed = [], None
    for k, states in enumerate(starts):
        after = products[-1][0] if k > 0 else None
        joint = k < per - 1
        results = solve_heads(
            place, k, 0, per, regular, queries if joint else None, grads, keys, values, table, states, mixed, after
        )
        turned = results[-1]
        if joint:
            mixed = results[0]
        far = lax.ppermute(turned, "seq", partner)
        products.append(gradient_blocks(place, turned, far, tokens, other, order))
    for side in range(2):
        after = products[-1][0] if side == 0 else None
        (mixed,) = solve_heads(
            place, per - 1, side * half, per, regular, queries, None, keys, values, table,
            [starts[-1][side]], mixed, after,
        )

    finished = []
    for blocks in products:
        sums = []
        for index, path in enumerate(paths):
            held, send = [blocks[2 * index]], blocks[2 * index + 1]
            for bit in path:
                pairs = [(i, i ^ (1 << bit)) for i in range(groups)]
                held.append(lax.ppermute(send, "dp", pairs))
                if bit != path[-1]:
                    send = sum_blocks(held, held[-1].shape[0] // 2)
            sums.append(held)
        out, *others = merge_blocks(sums)
        finished.append([out])
        for z, other_block in enumerate(others, 1):
            pairs = [(i, i ^ (2 * z)) for i in range(steps)]
            finished[-1].append(lax.ppermute(other_block, "seq", pairs))
    return mixed[None], finish(finished)


def solution(mesh):
    sizes = dict(mesh.shape)
    in_specs = (
        P("dp", "seq", None),
        P(),
        P("dp", "seq", None),
        P("dp", "seq", None),
        P("dp", None, "seq"),
        P(),
        P("dp", "seq", None),
    )
    out_specs = (P("dp", "seq", None), P("dp", "seq"))
    return jax.shard_map(
        functools.partial(per_device, sizes),
        mesh=mesh,
        in_specs=in_specs,
        out_specs=out_specs,
        check_vma=False,
    )
```

```python
import functools

import jax
import jax.numpy as jnp
from jax import lax
from jax.experimental import pallas as pl
from jax.experimental.pallas import tpu as pltpu
from jax.sharding import PartitionSpec as P

ITERS = 4
SUB = 128
EXTRA = 8


F32 = jnp.float32
BF16 = jnp.bfloat16


FULL = pltpu.CompilerParams(vmem_limit_bytes=67_043_328)


def whole(array):
    return pl.BlockSpec(array.shape, lambda *_: (0,) * len(array.shape))


def dot(left, right):
    return jnp.dot(left, right, preferred_element_type=F32)


def split(value):
    high = value.astype(BF16)
    low = (value - high.astype(F32)).astype(BF16)
    return high, low


def wide(value, axis=1):
    return jnp.concatenate(split(value), axis=axis)


def lane_shift(value, step):
    lanes = lax.broadcasted_iota(jnp.int32, value.shape, 1)
    return jnp.where(lanes >= step, pltpu.roll(value, step, 1), 0.0), lanes >= step


def cumulative_rows(value):
    step = 1
    while step < value.shape[1]:
        value = value + lane_shift(value, step)[0]
        step *= 2
    return value


def decayed_rows(value, cumulative):
    step = 1
    while step < value.shape[1]:
        earlier, inside = lane_shift(cumulative, step)
        factor = jnp.exp(jnp.where(inside, cumulative - earlier, 0.0))
        value = value + factor * lane_shift(value, step)[0]
        step *= 2
    return value


def decay_tables(decay_ref):
    rows = decay_ref.shape[1]
    offset = jnp.zeros((decay_ref.shape[0], 1), F32)
    local, full = [], []
    for c in range(rows // SUB):
        part = cumulative_rows(decay_ref[:, c * SUB : (c + 1) * SUB])
        local.append(part)
        full.append(part + offset)
        offset = offset + part[:, SUB - 1 : SUB]
    return local, jnp.exp(offset - jnp.concatenate(full, axis=1)), jnp.exp(offset)


def states_kernel(half, per, place_ref, keys_ref, values_ref, decay_ref, near_ref, away_ref, table_ref, work_ref):
    rows, dim = keys_ref.shape[0], SUB
    core = place_ref[0]
    row_at = lax.broadcasted_iota(jnp.int32, (dim, dim), 0)
    column_at = lax.broadcasted_iota(jnp.int32, (dim, dim), 1)
    local, tails, total = decay_tables(decay_ref)
    work_ref[0] = tails
    work_ref[2] = jnp.broadcast_to(total, tails.shape)
    for out, block in ((away_ref, 1 - core), (near_ref, core)):
        for k in range(per):
            for i in range(half):
                head = (block * half + i) * per + k
                column = pl.ds(pl.multiple_of(head * dim, dim), dim)
                key = keys_ref[:, column]
                tail = work_ref[0, pl.ds(head, 1), :]
                key_turned = key.astype(F32).T
                value_turned = values_ref[:, column].astype(F32).T
                work_ref[1, pl.ds(head, 1), :] = jnp.sum(key_turned * key_turned, axis=0, keepdims=True)
                high, low = split(jnp.concatenate([key_turned * tail, value_turned * tail], axis=0))
                state = dot(high, key) + dot(low, key)
                gram = state[0:dim]
                at, second = i // 2, i % 2
                out[k, at, (1 + second) * dim : (2 + second) * dim, :] = state[dim:]
                decay = work_ref[2, pl.ds(head, 1), :][:, 0:SUB]
                out[k, at, 3 * dim + second : 3 * dim + second + 1, :] = decay
                if second == 0:
                    first_gram = gram
                else:
                    out[k, at, 0:dim, :] = jnp.where(row_at <= column_at, first_gram, gram)
                    diagonal = jnp.sum(jnp.where(row_at == column_at, gram, 0.0), axis=0, keepdims=True)
                    out[k, at, 3 * dim + 2 : 3 * dim + 3, :] = diagonal
                    out[k, at, 3 * dim + 3 :, :] = jnp.zeros((EXTRA - 3, dim), F32)
    carry = jnp.zeros_like(total)
    for c in range(rows // SUB):
        lanes = slice(c * SUB, (c + 1) * SUB)
        part = decayed_rows(work_ref[1, :, lanes], local[c]) + jnp.exp(local[c]) * carry
        table_ref[0, :, lanes] = local[c]
        table_ref[1, :, lanes] = part
        carry = part[:, SUB - 1 : SUB]


def local_states(place, keys, values, decay, half, per):
    rows, columns = keys.shape
    heads = decay.shape[0]
    dim = columns // heads
    state = jax.ShapeDtypeStruct((per, half // 2, 3 * dim + EXTRA, dim), F32)
    table = jax.ShapeDtypeStruct((2, heads, rows), F32)
    return pl.pallas_call(
        functools.partial(states_kernel, half, per),
        out_shape=[state, state, table],
        in_specs=[pl.BlockSpec(memory_space=pltpu.SMEM)] + [whole(a) for a in (keys, values, decay)],
        out_specs=[whole(state), whole(state), whole(table)],
        scratch_shapes=[pltpu.VMEM((3, heads, rows), F32)],
        grid=(1,),
        compiler_params=FULL,
        cost_estimate=pl.CostEstimate(
            flops=16 * rows * dim * dim * half * per, bytes_accessed=8 * rows * columns, transcendentals=0
        ),
        name="local_states",
    )(place, keys, values, decay)


def join(earlier, later, dim):
    row_at = lax.broadcasted_iota(jnp.int32, later.shape, 1)
    column_at = lax.broadcasted_iota(jnp.int32, later.shape, 2)
    is_first = (row_at < dim) & (row_at <= column_at) | (row_at >= dim) & (row_at < 2 * dim)
    is_first = is_first | (row_at == 3 * dim)
    is_decay = (row_at == 3 * dim) | (row_at == 3 * dim + 1)
    factor = jnp.where(is_first, later[:, 3 * dim : 3 * dim + 1], later[:, 3 * dim + 1 : 3 * dim + 2])
    return factor * earlier + jnp.where(is_decay, 0.0, later)


def chip_kernel(dim, place_ref, own_ref, came_ref, *out_refs):
    is_first = place_ref[0] == 0
    for k, out_ref in enumerate(out_refs):
        own, came = own_ref[k], came_ref[k]
        out_ref[...] = join(jnp.where(is_first, own, came), jnp.where(is_first, came, own), dim)


def start_kernel(dim, k, place_ref, own_ref, came_ref, *refs):
    sent_refs, (mine_ref, other_ref) = refs[:-2], refs[-2:]
    is_first = place_ref[0] == 0
    before = sent_refs[-1][...]
    for ref in reversed(sent_refs[:-1]):
        before = join(before, ref[...], dim)
    after = join(before, jnp.where(is_first, own_ref[k], came_ref[k]), dim)
    mine_ref[...] = jnp.where(is_first, before, after)
    other_ref[...] = jnp.where(is_first, after, before)


def combine(kernel, place, arrays, shape, outs):
    out = jax.ShapeDtypeStruct(shape, F32)
    return pl.pallas_call(
        kernel,
        out_shape=[out] * outs,
        in_specs=[pl.BlockSpec(memory_space=pltpu.SMEM)] + [whole(a) for a in arrays],
        out_specs=[whole(out)] * outs,
        grid=(1,),
        compiler_params=FULL,
        cost_estimate=pl.CostEstimate(
            flops=0, bytes_accessed=8 * sum(a.size for a in arrays), transcendentals=0
        ),
    )(place, *arrays)


def solve_kernel(with_query, with_gradient, bounds, head_of, place_ref, regular_ref, *refs):
    refs = list(refs)
    q_ref = refs.pop(0) if with_query else None
    g_ref = refs.pop(0) if with_gradient else None
    k_ref, v_ref, rows_ref = refs[:3]
    state_refs, refs = refs[3 : 3 + len(bounds)], refs[3 + len(bounds) :]
    turned_ref = refs.pop() if with_gradient else None
    mixed_ref = refs.pop() if with_query else None
    rows, dim = k_ref.shape
    pieces = range(rows // SUB)
    place = [slice(c * SUB, (c + 1) * SUB) for c in pieces]
    step = pl.program_id(0)
    head = head_of(step, place_ref)
    ridge = regular_ref[head]
    row_at = lax.broadcasted_iota(jnp.int32, (SUB, SUB), 0)
    column_at = lax.broadcasted_iota(jnp.int32, (SUB, SUB), 1)
    lower = row_at >= column_at

    is_second = lax.rem(step, 2) == 1

    def state(start, size):
        at = pl.ds(start, size)
        if len(state_refs) == 1:
            return state_refs[0][0, at, :]
        return jnp.where(step < bounds[1], state_refs[0][0, at, :], state_refs[1][0, at, :])

    packed = state(0, dim)
    direct = (row_at > column_at) == is_second
    start = jnp.where(direct, packed, packed.T)
    diagonal = state(3 * dim, EXTRA)[2:3]
    gram = [jnp.where((row_at == column_at) & is_second, diagonal, start)]
    memory = [state(pl.multiple_of((1 + lax.rem(step, 2)) * dim, dim), dim)]
    start_trace = jnp.sum(jnp.where(row_at == column_at, gram[0], 0.0), axis=0, keepdims=True)
    start_trace = jnp.sum(start_trace, axis=1, keepdims=True)
    cumulative_row = rows_ref[0, pl.ds(head, 1), :]
    cumulative = [cumulative_row[:, at] for at in place]
    last = [row[:, SUB - 1 : SUB] for row in cumulative]
    whole, offset = [], jnp.zeros((1, 1), F32)
    for c in pieces:
        whole.append(cumulative[c] + offset)
        offset = offset + last[c]
    trace = jnp.exp(jnp.concatenate(whole, axis=1)) * start_trace + rows_ref[1, pl.ds(head, 1), :]
    span = 0.5 * trace
    center = ridge + span
    alphas, gammas = [1.0 / center], []
    for i in range(1, ITERS):
        factor = 0.5 if i == 1 else 0.25
        product = span * alphas[-1]
        alphas.append(1.0 / (center - factor * span * product))
        gammas.append(alphas[-1] * (factor * span * product))
    table = jnp.concatenate(alphas + gammas + [cumulative_row], axis=0).T

    def column(index):
        return [jnp.broadcast_to(table[at, index : index + 1], (SUB, SUB)) for at in place]

    rise = column(2 * ITERS - 1)
    weights = [
        jnp.where(lower, jnp.exp(jnp.where(lower, rise[c] - cumulative[c], 0.0)), 0.0) for c in pieces
    ]
    scale = [jnp.exp(r) for r in rise]

    keys = [k_ref[at, :] for at in place]
    values = [v_ref[at, :] for at in place]
    keys_turned = [key.astype(F32).T for key in keys]
    values_turned = [value.astype(F32).T for value in values]
    for c in pieces[:-1]:
        tail = jnp.exp(last[c] - cumulative[c])
        decay = jnp.exp(last[c])
        both = jnp.concatenate([keys_turned[c] * tail, values_turned[c] * tail], axis=0)
        grown = dot(wide(both), jnp.concatenate([keys[c], keys[c]], axis=0))
        gram.append(decay * gram[-1] + grown[0:dim])
        memory.append(decay * memory[-1] + grown[dim:])
    keys_turned = [key.astype(BF16) for key in keys_turned]
    values_turned = [value.astype(BF16) for value in values_turned]

    def pair(left, right):
        return jnp.concatenate([left, right], axis=0)

    def each(value):
        return pair(value, value) if with_query and with_gradient else value

    residual = []
    for c in pieces:
        sides = []
        if with_query:
            sides.append(q_ref[place[c], :].astype(F32))
        if with_gradient:
            grad = g_ref[place[c], :]
            pulled = scale[c] * dot(jnp.concatenate([grad, grad], axis=1), wide(memory[c], 0))
            score = weights[c] * dot(grad, values_turned[c])
            sides.append(pulled + dot(wide(score), pair(keys[c], keys[c])))
        residual.append(jnp.concatenate(sides, axis=0) if len(sides) > 1 else sides[0])

    alpha = column(0)
    change = [each(alpha[c]) * residual[c] for c in pieces]
    solution = list(change)
    rights = [jnp.concatenate([keys_turned[c], gram[c].astype(BF16)], axis=1) for c in pieces]
    for i in range(1, ITERS):
        alpha, gamma = column(i), column(ITERS + i - 1)
        first = [dot(change[c].astype(BF16), rights[c]) for c in pieces]
        second = [
            dot((first[c][:, 0:SUB] * each(weights[c])).astype(BF16), keys[c]) for c in pieces
        ]
        for c in pieces:
            applied = ridge * change[c] + (each(scale[c]) * first[c][:, SUB:] + second[c])
            residual[c] = residual[c] - applied
            change[c] = each(alpha[c]) * residual[c] + each(gamma[c]) * change[c]
            solution[c] = solution[c] + change[c]

    if with_gradient:
        for c in pieces:
            turned_ref[0, :, place[c]] = solution[c][-SUB:].T.astype(BF16).astype(F32)
    for c in pieces if with_query else ():
        high, low = split(solution[c][0:SUB])
        memory_high, memory_low = split(memory[c].T)
        right = jnp.concatenate([keys_turned[c], memory_high], axis=1)
        first = dot(jnp.concatenate([high, low], axis=1), pair(right, right))
        second = first[:, SUB:] + dot(high, memory_low)
        score = weights[c] * first[:, 0:SUB]
        output = scale[c] * second + dot(wide(score), pair(values[c], values[c]))
        mixed_ref[place[c], :] = output.astype(BF16)


def solve_heads(place, k, base, per, regular, queries, grads, keys, values, table, states, mixed, after):
    rows, columns = keys.shape
    heads = regular.shape[0]
    dim = columns // heads
    half = 2 * states[0].shape[0]
    groups, count = heads // per, half * len(states)
    with_query, with_gradient = queries is not None, grads is not None
    bounds = [half * i for i in range(len(states))]

    def head_of(step, place_ref):
        return lax.rem(place_ref[0] * half + base + step, groups) * per + k

    def at_head(step, place_ref, regular_ref):
        return (0, head_of(step, place_ref))

    wide_spec = pl.BlockSpec((rows, dim), at_head)
    operands = [a for a in (queries, grads, keys, values) if a is not None]
    in_specs = [wide_spec] * len(operands)
    operands.append(table)
    in_specs.append(whole(table))
    for bound, state in zip(bounds, states):

        def at_pair(step, *_, bound=bound):
            return (jnp.clip(step - bound, 0, half - 1) // 2, 0, 0)

        operands.append(state)
        in_specs.append(pl.BlockSpec((1,) + state.shape[1:], at_pair))
    aliases = {}
    if with_query and mixed is not None:
        operands.append(mixed)
        in_specs.append(pl.BlockSpec(memory_space=pl.ANY))
        aliases = {2 + len(operands) - 1: 0}
    if after is not None:
        operands.append(after)
        in_specs.append(pl.BlockSpec(memory_space=pl.ANY))
    shapes, out_specs = [], []
    if with_query:
        shapes.append(jax.ShapeDtypeStruct((rows, columns), BF16))
        out_specs.append(wide_spec)
    if with_gradient:
        shapes.append(jax.ShapeDtypeStruct((count, dim, rows), F32))
        out_specs.append(pl.BlockSpec((1, dim, rows), lambda step, *_: (step, 0, 0)))
    return pl.pallas_call(
        functools.partial(solve_kernel, with_query, with_gradient, bounds, head_of),
        out_shape=shapes,
        grid_spec=pltpu.PrefetchScalarGridSpec(
            num_scalar_prefetch=2, grid=(count,), in_specs=in_specs, out_specs=out_specs
        ),
        input_output_aliases=aliases,
        cost_estimate=pl.CostEstimate(
            flops=count * 80 * rows * dim * dim, bytes_accessed=count * 14 * rows * dim, transcendentals=0
        ),
        compiler_params=FULL,
        name="solve_heads",
    )(place, regular, *operands)


def pick_kernel(core_ref, tokens_ref, out_ref):
    out_ref[0] = tokens_ref[...].astype(F32)


def pick_columns(core, tokens, blocks):
    rows, width = tokens.shape
    size = width // (2 * blocks)
    return pl.pallas_call(
        pick_kernel,
        out_shape=jax.ShapeDtypeStruct((blocks, rows, size), F32),
        grid_spec=pltpu.PrefetchScalarGridSpec(
            num_scalar_prefetch=1,
            grid=(blocks,),
            in_specs=[pl.BlockSpec((rows, size), lambda z, core_ref: (0, 2 * z + 1 - core_ref[0]))],
            out_specs=pl.BlockSpec((1, rows, size), lambda z, core_ref: (z, 0, 0)),
        ),
        cost_estimate=pl.CostEstimate(flops=0, bytes_accessed=3 * rows * width, transcendentals=0),
        compiler_params=FULL,
        name="pick_columns",
    )(core, tokens)


def gradient_kernel(order, place_ref, own_ref, far_ref, tokens_ref, other_ref, *rest):
    outs, left_ref = rest[:-1], rest[-1]
    core, group = place_ref[0], place_ref[1]
    count, dim, rows = own_ref.shape
    half = count // 2
    middle = dim // 2

    @pl.when(pl.program_id(0) == 0)
    def _():
        for i in range(half):
            near, away = (core * half + i) ^ group, ((1 - core) * half + i) ^ group
            left_ref[near, :, 0:rows] = own_ref[i].astype(BF16)
            left_ref[away, :, 0:rows] = own_ref[half + i].astype(BF16)
            left_ref[near, :, rows:] = far_ref[half + i].astype(BF16)
            left_ref[away, :, rows:] = far_ref[i].astype(BF16)

    left = left_ref[...].reshape(2 * half * dim, 2 * rows)
    result = dot(left, jnp.concatenate([tokens_ref[...], other_ref[0].astype(BF16)], axis=0))
    for d in range(2 * half):
        for path in range(2):
            which, index = order[path][d]
            start = d * dim + path * middle
            outs[2 * path + which][index, 0] = result[start : start + middle]


def gradient_blocks(place, own, far, tokens, other, order):
    count, dim, rows = own.shape
    half = count // 2
    blocks, _, size = other.shape
    out = jax.ShapeDtypeStruct((half, blocks, dim // 2, size), F32)
    turned_spec = pl.BlockSpec((count, dim, rows), lambda z, p: (0, 0, 0))
    return pl.pallas_call(
        functools.partial(gradient_kernel, order),
        out_shape=[out] * 4,
        grid_spec=pltpu.PrefetchScalarGridSpec(
            num_scalar_prefetch=1,
            grid=(blocks,),
            in_specs=[turned_spec] * 2
            + [
                pl.BlockSpec((rows, size), lambda z, p: (0, 2 * (p[2] ^ z) + p[0])),
                pl.BlockSpec((1, rows, size), lambda z, p: (p[2] ^ z, 0, 0)),
            ],
            out_specs=[pl.BlockSpec((half, 1, dim // 2, size), lambda z, p: (0, z, 0, 0))] * 4,
            scratch_shapes=[pltpu.VMEM((2 * half, dim, 2 * rows), BF16)],
        ),
        cost_estimate=pl.CostEstimate(
            flops=8 * half * dim * rows * blocks * size,
            bytes_accessed=4 * (4 * half * dim * rows + blocks * rows * size + 2 * half * blocks * dim * size),
            transcendentals=0,
        ),
        compiler_params=FULL,
        name="gradient_blocks",
    )(place, own, far, tokens, other)


def sum_kernel(*refs):
    total = refs[0][...]
    for ref in refs[1:-1]:
        total = total + ref[...]
    refs[-1][...] = total


def sum_blocks(arrays, length):
    out = jax.ShapeDtypeStruct((length,) + arrays[0].shape[1:], F32)
    spec = pl.BlockSpec(out.shape, lambda _: (1, 0, 0, 0))
    return pl.pallas_call(
        sum_kernel,
        out_shape=out,
        in_specs=[spec] * len(arrays),
        out_specs=whole(out),
        grid=(1,),
        compiler_params=FULL,
        cost_estimate=pl.CostEstimate(flops=0, bytes_accessed=12 * out.size // length, transcendentals=0),
        name="sum_blocks",
    )(*arrays)


def merge_kernel(counts, *refs):
    sums, outs = refs[: sum(counts)], refs[sum(counts) :]
    rows = sums[0].shape[2]
    at = 0
    for i, count in enumerate(counts):
        for z, out in enumerate(outs):
            total = sums[at][0, z]
            for ref in sums[at + 1 : at + count]:
                total = total + ref[0, z]
            out[i * rows : (i + 1) * rows, :] = total
        at += count


def merge_blocks(sums):
    counts = [len(arrays) for arrays in sums]
    arrays = [a for group in sums for a in group]
    _, chips, rows, size = arrays[0].shape
    out = jax.ShapeDtypeStruct((len(counts) * rows, size), F32)
    return pl.pallas_call(
        functools.partial(merge_kernel, counts),
        out_shape=[out] * chips,
        in_specs=[pl.BlockSpec((1, chips, rows, size), lambda _: (0, 0, 0, 0))] * len(arrays),
        out_specs=[whole(out)] * chips,
        grid=(1,),
        compiler_params=FULL,
        cost_estimate=pl.CostEstimate(
            flops=0, bytes_accessed=4 * (len(arrays) + 2) * chips * rows * size, transcendentals=0
        ),
        name="merge_blocks",
    )(*arrays)


def finish_kernel(count, *refs):
    out = refs[-1]
    rows = refs[0].shape[0]
    for k in range((len(refs) - 1) // count):
        total = refs[k * count][...]
        for ref in refs[k * count + 1 : (k + 1) * count]:
            total = total + ref[...]
        out[k * rows : (k + 1) * rows, :] = total


def finish(sets):
    arrays = [a for group in sets for a in group]
    rows, size = arrays[0].shape
    out = jax.ShapeDtypeStruct((rows * len(sets), size), F32)
    return pl.pallas_call(
        functools.partial(finish_kernel, len(sets[0])),
        out_shape=out,
        in_specs=[whole(a) for a in arrays],
        out_specs=whole(out),
        grid=(1,),
        compiler_params=FULL,
        cost_estimate=pl.CostEstimate(
            flops=0, bytes_accessed=5 * sum(a.size for a in arrays), transcendentals=0
        ),
        name="finish",
    )(*arrays)


def bit_order(bits):
    table = []
    for d in range(1 << len(bits)):
        code = 0
        for bit in bits:
            code = 2 * code + ((d >> bit) & 1)
        table.append(divmod(code, 1 << (len(bits) - 1)))
    return table


def per_device(sizes, *arrays):
    return program(sizes, *arrays)


def program(sizes, tokens, w_query, keys, values, log_decay, regular, grad_out):
    groups, steps = sizes["dp"], sizes["seq"]
    chips = steps // 2
    heads = log_decay.shape[1]
    columns = keys.shape[2]
    dim = columns // heads
    per = heads // groups
    half = groups // 2
    tokens, keys, values, grads, decay = tokens[0], keys[0], values[0], grad_out[0], log_decay[0]
    here = lax.axis_index("seq")
    core = here % 2
    place = jnp.stack([core, lax.axis_index("dp"), here // 2]).astype(jnp.int32)
    partner = [(i, i ^ 1) for i in range(steps)]

    own, away, table = local_states(place, keys, values, decay, half, per)
    came = lax.ppermute(away, "seq", partner)
    shape = own.shape[1:]
    chip_states = combine(functools.partial(chip_kernel, dim), place, [own, came], shape, per)
    starts = []
    for k, chip_state in enumerate(chip_states):
        sent = []
        for z in range(1, chips):
            pairs = [(i, i + 2 * z) for i in range(steps - 2 * z)]
            sent.append(lax.ppermute(chip_state, "seq", pairs))
        starting = functools.partial(start_kernel, dim, k)
        mine, others = combine(starting, place, [own, came, *sent], shape, 2)
        starts.append((mine, lax.ppermute(others, "seq", partner)))

    picked = pick_columns(place, tokens, chips)
    other = lax.ppermute(picked, "seq", partner)
    queries = jnp.dot(tokens, w_query, preferred_element_type=F32).astype(BF16)

    dp_bits = groups.bit_length() - 1
    paths = [list(range(dp_bits)), list(reversed(range(dp_bits)))]
    order = [bit_order(path) for path in paths]

    products, mixed = [], None
    for k, states in enumerate(starts):
        after = products[-1][0] if k > 0 else None
        joint = k < per - 1
        results = solve_heads(
            place, k, 0, per, regular, queries if joint else None, grads, keys, values, table, states, mixed, after
        )
        turned = results[-1]
        if joint:
            mixed = results[0]
        far = lax.ppermute(turned, "seq", partner)
        products.append(gradient_blocks(place, turned, far, tokens, other, order))
    for side in range(2):
        after = products[-1][0] if side == 0 else None
        (mixed,) = solve_heads(
            place, per - 1, side * half, per, regular, queries, None, keys, values, table,
            [starts[-1][side]], mixed, after,
        )

    finished = []
    for blocks in products:
        sums = []
        for index, path in enumerate(paths):
            held, send = [blocks[2 * index]], blocks[2 * index + 1]
            for bit in path:
                pairs = [(i, i ^ (1 << bit)) for i in range(groups)]
                held.append(lax.ppermute(send, "dp", pairs))
                if bit != path[-1]:
                    send = sum_blocks(held, held[-1].shape[0] // 2)
            sums.append(held)
        out, *others = merge_blocks(sums)
        finished.append([out])
        for z, other_block in enumerate(others, 1):
            pairs = [(i, i ^ (2 * z)) for i in range(steps)]
            finished[-1].append(lax.ppermute(other_block, "seq", pairs))
    return mixed[None], finish(finished)


def solution(mesh):
    sizes = dict(mesh.shape)
    in_specs = (
        P("dp", "seq", None),
        P(),
        P("dp", "seq", None),
        P("dp", "seq", None),
        P("dp", None, "seq"),
        P(),
        P("dp", "seq", None),
    )
    out_specs = (P("dp", "seq", None), P("dp", "seq"))
    return jax.shard_map(
        functools.partial(per_device, sizes),
        mesh=mesh,
        in_specs=in_specs,
        out_specs=out_specs,
        check_vma=False,
    )
```

```python
import functools

import jax
import jax.numpy as jnp
from jax import lax
from jax.experimental import pallas as pl
from jax.experimental.pallas import tpu as pltpu
from jax.sharding import PartitionSpec as P

ITERS = 4
SUB = 128
EXTRA = 8


F32 = jnp.float32
BF16 = jnp.bfloat16


FULL = pltpu.CompilerParams(vmem_limit_bytes=67_043_328)


def whole(array):
    return pl.BlockSpec(array.shape, lambda *_: (0,) * len(array.shape))


def dot(left, right):
    return jnp.dot(left, right, preferred_element_type=F32)


def split(value):
    high = value.astype(BF16)
    low = (value - high.astype(F32)).astype(BF16)
    return high, low


def wide(value, axis=1):
    return jnp.concatenate(split(value), axis=axis)


def lane_shift(value, step):
    lanes = lax.broadcasted_iota(jnp.int32, value.shape, 1)
    return jnp.where(lanes >= step, pltpu.roll(value, step, 1), 0.0), lanes >= step


def cumulative_rows(value):
    step = 1
    while step < value.shape[1]:
        value = value + lane_shift(value, step)[0]
        step *= 2
    return value


def decayed_rows(value, cumulative):
    step = 1
    while step < value.shape[1]:
        earlier, inside = lane_shift(cumulative, step)
        factor = jnp.exp(jnp.where(inside, cumulative - earlier, 0.0))
        value = value + factor * lane_shift(value, step)[0]
        step *= 2
    return value


def decay_tables(decay_ref):
    rows = decay_ref.shape[1]
    offset = jnp.zeros((decay_ref.shape[0], 1), F32)
    local, full = [], []
    for c in range(rows // SUB):
        part = cumulative_rows(decay_ref[:, c * SUB : (c + 1) * SUB])
        local.append(part)
        full.append(part + offset)
        offset = offset + part[:, SUB - 1 : SUB]
    return local, jnp.exp(offset - jnp.concatenate(full, axis=1)), jnp.exp(offset)


def states_kernel(half, per, place_ref, keys_ref, values_ref, decay_ref, near_ref, away_ref, table_ref, work_ref):
    rows, dim = keys_ref.shape[0], SUB
    core = place_ref[0]
    row_at = lax.broadcasted_iota(jnp.int32, (dim, dim), 0)
    column_at = lax.broadcasted_iota(jnp.int32, (dim, dim), 1)
    local, tails, total = decay_tables(decay_ref)
    work_ref[0] = tails
    work_ref[2] = jnp.broadcast_to(total, tails.shape)
    for out, block in ((away_ref, 1 - core), (near_ref, core)):
        for k in range(per):
            for i in range(half):
                head = (block * half + i) * per + k
                column = pl.ds(pl.multiple_of(head * dim, dim), dim)
                key = keys_ref[:, column]
                tail = work_ref[0, pl.ds(head, 1), :]
                key_turned = key.astype(F32).T
                value_turned = values_ref[:, column].astype(F32).T
                work_ref[1, pl.ds(head, 1), :] = jnp.sum(key_turned * key_turned, axis=0, keepdims=True)
                high, low = split(jnp.concatenate([key_turned * tail, value_turned * tail], axis=0))
                state = dot(high, key) + dot(low, key)
                gram = state[0:dim]
                at, second = i // 2, i % 2
                out[k, at, (1 + second) * dim : (2 + second) * dim, :] = state[dim:]
                decay = work_ref[2, pl.ds(head, 1), :][:, 0:SUB]
                out[k, at, 3 * dim + second : 3 * dim + second + 1, :] = decay
                if second == 0:
                    first_gram = gram
                else:
                    out[k, at, 0:dim, :] = jnp.where(row_at <= column_at, first_gram, gram)
                    diagonal = jnp.sum(jnp.where(row_at == column_at, gram, 0.0), axis=0, keepdims=True)
                    out[k, at, 3 * dim + 2 : 3 * dim + 3, :] = diagonal
                    out[k, at, 3 * dim + 3 :, :] = jnp.zeros((EXTRA - 3, dim), F32)
    carry = jnp.zeros_like(total)
    for c in range(rows // SUB):
        lanes = slice(c * SUB, (c + 1) * SUB)
        part = decayed_rows(work_ref[1, :, lanes], local[c]) + jnp.exp(local[c]) * carry
        table_ref[0, :, lanes] = local[c]
        table_ref[1, :, lanes] = part
        carry = part[:, SUB - 1 : SUB]


def local_states(place, keys, values, decay, half, per):
    rows, columns = keys.shape
    heads = decay.shape[0]
    dim = columns // heads
    state = jax.ShapeDtypeStruct((per, half // 2, 3 * dim + EXTRA, dim), F32)
    table = jax.ShapeDtypeStruct((2, heads, rows), F32)
    return pl.pallas_call(
        functools.partial(states_kernel, half, per),
        out_shape=[state, state, table],
        in_specs=[pl.BlockSpec(memory_space=pltpu.SMEM)] + [whole(a) for a in (keys, values, decay)],
        out_specs=[whole(state), whole(state), whole(table)],
        scratch_shapes=[pltpu.VMEM((3, heads, rows), F32)],
        grid=(1,),
        compiler_params=FULL,
        cost_estimate=pl.CostEstimate(
            flops=16 * rows * dim * dim * half * per, bytes_accessed=8 * rows * columns, transcendentals=0
        ),
        name="local_states",
    )(place, keys, values, decay)


def join(earlier, later, dim):
    row_at = lax.broadcasted_iota(jnp.int32, later.shape, 1)
    column_at = lax.broadcasted_iota(jnp.int32, later.shape, 2)
    is_first = (row_at < dim) & (row_at <= column_at) | (row_at >= dim) & (row_at < 2 * dim)
    is_first = is_first | (row_at == 3 * dim)
    is_decay = (row_at == 3 * dim) | (row_at == 3 * dim + 1)
    factor = jnp.where(is_first, later[:, 3 * dim : 3 * dim + 1], later[:, 3 * dim + 1 : 3 * dim + 2])
    return factor * earlier + jnp.where(is_decay, 0.0, later)


def chip_kernel(dim, place_ref, own_ref, came_ref, *out_refs):
    is_first = place_ref[0] == 0
    for k, out_ref in enumerate(out_refs):
        own, came = own_ref[k], came_ref[k]
        out_ref[...] = join(jnp.where(is_first, own, came), jnp.where(is_first, came, own), dim)


def start_kernel(dim, k, place_ref, own_ref, came_ref, *refs):
    sent_refs, (mine_ref, other_ref) = refs[:-2], refs[-2:]
    is_first = place_ref[0] == 0
    before = sent_refs[-1][...]
    for ref in reversed(sent_refs[:-1]):
        before = join(before, ref[...], dim)
    after = join(before, jnp.where(is_first, own_ref[k], came_ref[k]), dim)
    mine_ref[...] = jnp.where(is_first, before, after)
    other_ref[...] = jnp.where(is_first, after, before)


def combine(kernel, place, arrays, shape, outs):
    out = jax.ShapeDtypeStruct(shape, F32)
    return pl.pallas_call(
        kernel,
        out_shape=[out] * outs,
        in_specs=[pl.BlockSpec(memory_space=pltpu.SMEM)] + [whole(a) for a in arrays],
        out_specs=[whole(out)] * outs,
        grid=(1,),
        compiler_params=FULL,
        cost_estimate=pl.CostEstimate(
            flops=0, bytes_accessed=8 * sum(a.size for a in arrays), transcendentals=0
        ),
    )(place, *arrays)


def solve_kernel(with_query, with_gradient, bounds, head_of, place_ref, regular_ref, *refs):
    refs = list(refs)
    q_ref = refs.pop(0) if with_query else None
    g_ref = refs.pop(0) if with_gradient else None
    k_ref, v_ref, rows_ref = refs[:3]
    state_refs, refs = refs[3 : 3 + len(bounds)], refs[3 + len(bounds) :]
    turned_ref = refs.pop() if with_gradient else None
    mixed_ref = refs.pop() if with_query else None
    rows, dim = k_ref.shape
    pieces = range(rows // SUB)
    place = [slice(c * SUB, (c + 1) * SUB) for c in pieces]
    step = pl.program_id(0)
    head = head_of(step, place_ref)
    ridge = regular_ref[head]
    row_at = lax.broadcasted_iota(jnp.int32, (SUB, SUB), 0)
    column_at = lax.broadcasted_iota(jnp.int32, (SUB, SUB), 1)
    lower = row_at >= column_at

    is_second = lax.rem(step, 2) == 1

    def state(start, size):
        at = pl.ds(start, size)
        if len(state_refs) == 1:
            return state_refs[0][0, at, :]
        return jnp.where(step < bounds[1], state_refs[0][0, at, :], state_refs[1][0, at, :])

    packed = state(0, dim)
    direct = (row_at > column_at) == is_second
    start = jnp.where(direct, packed, packed.T)
    diagonal = state(3 * dim, EXTRA)[2:3]
    gram = [jnp.where((row_at == column_at) & is_second, diagonal, start)]
    memory = [state(pl.multiple_of((1 + lax.rem(step, 2)) * dim, dim), dim)]
    start_trace = jnp.sum(jnp.where(row_at == column_at, gram[0], 0.0), axis=0, keepdims=True)
    start_trace = jnp.sum(start_trace, axis=1, keepdims=True)
    cumulative_row = rows_ref[0, pl.ds(head, 1), :]
    cumulative = [cumulative_row[:, at] for at in place]
    last = [row[:, SUB - 1 : SUB] for row in cumulative]
    whole, offset = [], jnp.zeros((1, 1), F32)
    for c in pieces:
        whole.append(cumulative[c] + offset)
        offset = offset + last[c]
    trace = jnp.exp(jnp.concatenate(whole, axis=1)) * start_trace + rows_ref[1, pl.ds(head, 1), :]
    span = 0.5 * trace
    center = ridge + span
    alphas, gammas = [1.0 / center], []
    for i in range(1, ITERS):
        factor = 0.5 if i == 1 else 0.25
        product = span * alphas[-1]
        alphas.append(1.0 / (center - factor * span * product))
        gammas.append(alphas[-1] * (factor * span * product))
    table = jnp.concatenate(alphas + gammas + [cumulative_row], axis=0).T

    def column(index):
        return [jnp.broadcast_to(table[at, index : index + 1], (SUB, SUB)) for at in place]

    rise = column(2 * ITERS - 1)
    weights = [
        jnp.where(lower, jnp.exp(jnp.where(lower, rise[c] - cumulative[c], 0.0)), 0.0) for c in pieces
    ]
    scale = [jnp.exp(r) for r in rise]

    keys = [k_ref[at, :] for at in place]
    values = [v_ref[at, :] for at in place]
    keys_turned = [key.astype(F32).T for key in keys]
    values_turned = [value.astype(F32).T for value in values]
    for c in pieces[:-1]:
        tail = jnp.exp(last[c] - cumulative[c])
        decay = jnp.exp(last[c])
        both = jnp.concatenate([keys_turned[c] * tail, values_turned[c] * tail], axis=0)
        grown = dot(wide(both), jnp.concatenate([keys[c], keys[c]], axis=0))
        gram.append(decay * gram[-1] + grown[0:dim])
        memory.append(decay * memory[-1] + grown[dim:])
    keys_turned = [key.astype(BF16) for key in keys_turned]
    values_turned = [value.astype(BF16) for value in values_turned]

    def pair(left, right):
        return jnp.concatenate([left, right], axis=0)

    def each(value):
        return pair(value, value) if with_query and with_gradient else value

    residual = []
    for c in pieces:
        sides = []
        if with_query:
            sides.append(q_ref[place[c], :].astype(F32))
        if with_gradient:
            grad = g_ref[place[c], :]
            pulled = scale[c] * dot(jnp.concatenate([grad, grad], axis=1), wide(memory[c], 0))
            score = weights[c] * dot(grad, values_turned[c])
            sides.append(pulled + dot(wide(score), pair(keys[c], keys[c])))
        residual.append(jnp.concatenate(sides, axis=0) if len(sides) > 1 else sides[0])

    alpha = column(0)
    change = [each(alpha[c]) * residual[c] for c in pieces]
    solution = list(change)
    rights = [jnp.concatenate([keys_turned[c], gram[c].astype(BF16)], axis=1) for c in pieces]
    for i in range(1, ITERS):
        alpha, gamma = column(i), column(ITERS + i - 1)
        first = [dot(change[c].astype(BF16), rights[c]) for c in pieces]
        second = [
            dot((first[c][:, 0:SUB] * each(weights[c])).astype(BF16), keys[c]) for c in pieces
        ]
        for c in pieces:
            applied = ridge * change[c] + (each(scale[c]) * first[c][:, SUB:] + second[c])
            residual[c] = residual[c] - applied
            change[c] = each(alpha[c]) * residual[c] + each(gamma[c]) * change[c]
            solution[c] = solution[c] + change[c]

    if with_gradient:
        for c in pieces:
            turned_ref[0, :, place[c]] = solution[c][-SUB:].T.astype(BF16).astype(F32)
    for c in pieces if with_query else ():
        high, low = split(solution[c][0:SUB])
        memory_high, memory_low = split(memory[c].T)
        right = jnp.concatenate([keys_turned[c], memory_high], axis=1)
        first = dot(jnp.concatenate([high, low], axis=1), pair(right, right))
        second = first[:, SUB:] + dot(high, memory_low)
        score = weights[c] * first[:, 0:SUB]
        output = scale[c] * second + dot(wide(score), pair(values[c], values[c]))
        mixed_ref[place[c], :] = output.astype(BF16)


def solve_heads(place, k, base, per, regular, queries, grads, keys, values, table, states, mixed, after):
    rows, columns = keys.shape
    heads = regular.shape[0]
    dim = columns // heads
    half = 2 * states[0].shape[0]
    groups, count = heads // per, half * len(states)
    with_query, with_gradient = queries is not None, grads is not None
    bounds = [half * i for i in range(len(states))]

    def head_of(step, place_ref):
        return lax.rem(place_ref[0] * half + base + step, groups) * per + k

    def at_head(step, place_ref, regular_ref):
        return (0, head_of(step, place_ref))

    wide_spec = pl.BlockSpec((rows, dim), at_head)
    operands = [a for a in (queries, grads, keys, values) if a is not None]
    in_specs = [wide_spec] * len(operands)
    operands.append(table)
    in_specs.append(whole(table))
    for bound, state in zip(bounds, states):

        def at_pair(step, *_, bound=bound):
            return (jnp.clip(step - bound, 0, half - 1) // 2, 0, 0)

        operands.append(state)
        in_specs.append(pl.BlockSpec((1,) + state.shape[1:], at_pair))
    aliases = {}
    if with_query and mixed is not None:
        operands.append(mixed)
        in_specs.append(pl.BlockSpec(memory_space=pl.ANY))
        aliases = {2 + len(operands) - 1: 0}
    if after is not None:
        operands.append(after)
        in_specs.append(pl.BlockSpec(memory_space=pl.ANY))
    shapes, out_specs = [], []
    if with_query:
        shapes.append(jax.ShapeDtypeStruct((rows, columns), BF16))
        out_specs.append(wide_spec)
    if with_gradient:
        shapes.append(jax.ShapeDtypeStruct((count, dim, rows), F32))
        out_specs.append(pl.BlockSpec((1, dim, rows), lambda step, *_: (step, 0, 0)))
    return pl.pallas_call(
        functools.partial(solve_kernel, with_query, with_gradient, bounds, head_of),
        out_shape=shapes,
        grid_spec=pltpu.PrefetchScalarGridSpec(
            num_scalar_prefetch=2, grid=(count,), in_specs=in_specs, out_specs=out_specs
        ),
        input_output_aliases=aliases,
        cost_estimate=pl.CostEstimate(
            flops=count * 80 * rows * dim * dim, bytes_accessed=count * 14 * rows * dim, transcendentals=0
        ),
        compiler_params=FULL,
        name="solve_heads",
    )(place, regular, *operands)


def pick_kernel(core_ref, tokens_ref, out_ref):
    out_ref[0] = tokens_ref[...].astype(F32)


def pick_columns(core, tokens, blocks):
    rows, width = tokens.shape
    size = width // (2 * blocks)
    return pl.pallas_call(
        pick_kernel,
        out_shape=jax.ShapeDtypeStruct((blocks, rows, size), F32),
        grid_spec=pltpu.PrefetchScalarGridSpec(
            num_scalar_prefetch=1,
            grid=(blocks,),
            in_specs=[pl.BlockSpec((rows, size), lambda z, core_ref: (0, 2 * z + 1 - core_ref[0]))],
            out_specs=pl.BlockSpec((1, rows, size), lambda z, core_ref: (z, 0, 0)),
        ),
        cost_estimate=pl.CostEstimate(flops=0, bytes_accessed=3 * rows * width, transcendentals=0),
        compiler_params=FULL,
        name="pick_columns",
    )(core, tokens)


def gradient_kernel(order, place_ref, own_ref, far_ref, tokens_ref, other_ref, *rest):
    outs, left_ref = rest[:-1], rest[-1]
    core, group = place_ref[0], place_ref[1]
    count, dim, rows = own_ref.shape
    half = count // 2
    middle = dim // 2

    @pl.when(pl.program_id(0) == 0)
    def _():
        for i in range(half):
            near, away = (core * half + i) ^ group, ((1 - core) * half + i) ^ group
            left_ref[near, :, 0:rows] = own_ref[i].astype(BF16)
            left_ref[away, :, 0:rows] = own_ref[half + i].astype(BF16)
            left_ref[near, :, rows:] = far_ref[half + i].astype(BF16)
            left_ref[away, :, rows:] = far_ref[i].astype(BF16)

    left = left_ref[...].reshape(2 * half * dim, 2 * rows)
    result = dot(left, jnp.concatenate([tokens_ref[...], other_ref[0].astype(BF16)], axis=0))
    for d in range(2 * half):
        for path in range(2):
            which, index = order[path][d]
            start = d * dim + path * middle
            outs[2 * path + which][index, 0] = result[start : start + middle]


def gradient_blocks(place, own, far, tokens, other, order):
    count, dim, rows = own.shape
    half = count // 2
    blocks, _, size = other.shape
    out = jax.ShapeDtypeStruct((half, blocks, dim // 2, size), F32)
    turned_spec = pl.BlockSpec((count, dim, rows), lambda z, p: (0, 0, 0))
    return pl.pallas_call(
        functools.partial(gradient_kernel, order),
        out_shape=[out] * 4,
        grid_spec=pltpu.PrefetchScalarGridSpec(
            num_scalar_prefetch=1,
            grid=(blocks,),
            in_specs=[turned_spec] * 2
            + [
                pl.BlockSpec((rows, size), lambda z, p: (0, 2 * (p[2] ^ z) + p[0])),
                pl.BlockSpec((1, rows, size), lambda z, p: (p[2] ^ z, 0, 0)),
            ],
            out_specs=[pl.BlockSpec((half, 1, dim // 2, size), lambda z, p: (0, z, 0, 0))] * 4,
            scratch_shapes=[pltpu.VMEM((2 * half, dim, 2 * rows), BF16)],
        ),
        cost_estimate=pl.CostEstimate(
            flops=8 * half * dim * rows * blocks * size,
            bytes_accessed=4 * (4 * half * dim * rows + blocks * rows * size + 2 * half * blocks * dim * size),
            transcendentals=0,
        ),
        compiler_params=FULL,
        name="gradient_blocks",
    )(place, own, far, tokens, other)


def sum_kernel(counts, *refs):
    arrays, outs = refs[: sum(counts)], refs[sum(counts) :]
    at = 0
    for count, out in zip(counts, outs):
        total = arrays[at][...]
        for ref in arrays[at + 1 : at + count]:
            total = total + ref[...]
        out[...] = total
        at += count


def sum_blocks(sums, length):
    counts = [len(arrays) for arrays in sums]
    arrays = [a for group in sums for a in group]
    out = jax.ShapeDtypeStruct((length,) + arrays[0].shape[1:], F32)
    return pl.pallas_call(
        functools.partial(sum_kernel, counts),
        out_shape=[out] * len(sums),
        in_specs=[pl.BlockSpec(out.shape, lambda _: (1, 0, 0, 0))] * len(arrays),
        out_specs=[whole(out)] * len(sums),
        grid=(1,),
        compiler_params=FULL,
        cost_estimate=pl.CostEstimate(
            flops=0, bytes_accessed=4 * (len(arrays) + 2) * out.size, transcendentals=0
        ),
        name="sum_blocks",
    )(*arrays)


def merge_kernel(counts, *refs):
    sums, outs = refs[: sum(counts)], refs[sum(counts) :]
    rows = sums[0].shape[2]
    at = 0
    for i, count in enumerate(counts):
        for z, out in enumerate(outs):
            total = sums[at][0, z]
            for ref in sums[at + 1 : at + count]:
                total = total + ref[0, z]
            out[i * rows : (i + 1) * rows, :] = total
        at += count


def merge_blocks(sums):
    counts = [len(arrays) for arrays in sums]
    arrays = [a for group in sums for a in group]
    _, chips, rows, size = arrays[0].shape
    out = jax.ShapeDtypeStruct((len(counts) * rows, size), F32)
    return pl.pallas_call(
        functools.partial(merge_kernel, counts),
        out_shape=[out] * chips,
        in_specs=[pl.BlockSpec((1, chips, rows, size), lambda _: (0, 0, 0, 0))] * len(arrays),
        out_specs=[whole(out)] * chips,
        grid=(1,),
        compiler_params=FULL,
        cost_estimate=pl.CostEstimate(
            flops=0, bytes_accessed=4 * (len(arrays) + 2) * chips * rows * size, transcendentals=0
        ),
        name="merge_blocks",
    )(*arrays)


def finish_kernel(count, *refs):
    out = refs[-1]
    rows = refs[0].shape[0]
    for k in range((len(refs) - 1) // count):
        total = refs[k * count][...]
        for ref in refs[k * count + 1 : (k + 1) * count]:
            total = total + ref[...]
        out[k * rows : (k + 1) * rows, :] = total


def finish(sets):
    arrays = [a for group in sets for a in group]
    rows, size = arrays[0].shape
    out = jax.ShapeDtypeStruct((rows * len(sets), size), F32)
    return pl.pallas_call(
        functools.partial(finish_kernel, len(sets[0])),
        out_shape=out,
        in_specs=[whole(a) for a in arrays],
        out_specs=whole(out),
        grid=(1,),
        compiler_params=FULL,
        cost_estimate=pl.CostEstimate(
            flops=0, bytes_accessed=5 * sum(a.size for a in arrays), transcendentals=0
        ),
        name="finish",
    )(*arrays)


def bit_order(bits):
    table = []
    for d in range(1 << len(bits)):
        code = 0
        for bit in bits:
            code = 2 * code + ((d >> bit) & 1)
        table.append(divmod(code, 1 << (len(bits) - 1)))
    return table


def per_device(sizes, *arrays):
    return program(sizes, *arrays)


def program(sizes, tokens, w_query, keys, values, log_decay, regular, grad_out):
    groups, steps = sizes["dp"], sizes["seq"]
    chips = steps // 2
    heads = log_decay.shape[1]
    columns = keys.shape[2]
    dim = columns // heads
    per = heads // groups
    half = groups // 2
    tokens, keys, values, grads, decay = tokens[0], keys[0], values[0], grad_out[0], log_decay[0]
    here = lax.axis_index("seq")
    core = here % 2
    place = jnp.stack([core, lax.axis_index("dp"), here // 2]).astype(jnp.int32)
    partner = [(i, i ^ 1) for i in range(steps)]

    own, away, table = local_states(place, keys, values, decay, half, per)
    came = lax.ppermute(away, "seq", partner)
    shape = own.shape[1:]
    chip_states = combine(functools.partial(chip_kernel, dim), place, [own, came], shape, per)
    starts = []
    for k, chip_state in enumerate(chip_states):
        sent = []
        for z in range(1, chips):
            pairs = [(i, i + 2 * z) for i in range(steps - 2 * z)]
            sent.append(lax.ppermute(chip_state, "seq", pairs))
        starting = functools.partial(start_kernel, dim, k)
        mine, others = combine(starting, place, [own, came, *sent], shape, 2)
        starts.append((mine, lax.ppermute(others, "seq", partner)))

    picked = pick_columns(place, tokens, chips)
    other = lax.ppermute(picked, "seq", partner)
    queries = jnp.dot(tokens, w_query, preferred_element_type=F32).astype(BF16)

    dp_bits = groups.bit_length() - 1
    paths = [list(range(dp_bits)), list(reversed(range(dp_bits)))]
    order = [bit_order(path) for path in paths]

    products, mixed = [], None
    for k, states in enumerate(starts):
        after = products[-1][0] if k > 0 else None
        joint = k < per - 1
        results = solve_heads(
            place, k, 0, per, regular, queries if joint else None, grads, keys, values, table, states, mixed, after
        )
        turned = results[-1]
        if joint:
            mixed = results[0]
        far = lax.ppermute(turned, "seq", partner)
        products.append(gradient_blocks(place, turned, far, tokens, other, order))
    for side in range(2):
        after = products[-1][0] if side == 0 else None
        (mixed,) = solve_heads(
            place, per - 1, side * half, per, regular, queries, None, keys, values, table,
            [starts[-1][side]], mixed, after,
        )

    finished = []
    for blocks in products:
        sums, sends = [[blocks[0]], [blocks[2]]], [blocks[1], blocks[3]]
        for stage in range(dp_bits):
            for index, path in enumerate(paths):
                pairs = [(i, i ^ (1 << path[stage])) for i in range(groups)]
                sums[index].append(lax.ppermute(sends[index], "dp", pairs))
            if stage < dp_bits - 1:
                sends = sum_blocks(sums, sends[0].shape[0] // 2)
        out, *others = merge_blocks(sums)
        finished.append([out])
        for z, other_block in enumerate(others, 1):
            pairs = [(i, i ^ (2 * z)) for i in range(steps)]
            finished[-1].append(lax.ppermute(other_block, "seq", pairs))
    return mixed[None], finish(finished)


def solution(mesh):
    sizes = dict(mesh.shape)
    in_specs = (
        P("dp", "seq", None),
        P(),
        P("dp", "seq", None),
        P("dp", "seq", None),
        P("dp", None, "seq"),
        P(),
        P("dp", "seq", None),
    )
    out_specs = (P("dp", "seq", None), P("dp", "seq"))
    return jax.shard_map(
        functools.partial(per_device, sizes),
        mesh=mesh,
        in_specs=in_specs,
        out_specs=out_specs,
        check_vma=False,
    )
```

```python
import functools

import jax
import jax.numpy as jnp
from jax import lax
from jax.experimental import pallas as pl
from jax.experimental.pallas import tpu as pltpu
from jax.sharding import PartitionSpec as P

ITERS = 4
SUB = 128
EXTRA = 8


F32 = jnp.float32
BF16 = jnp.bfloat16


FULL = pltpu.CompilerParams(vmem_limit_bytes=67_043_328)


def whole(array):
    return pl.BlockSpec(array.shape, lambda *_: (0,) * len(array.shape))


def dot(left, right):
    return jnp.dot(left, right, preferred_element_type=F32)


def split(value):
    high = value.astype(BF16)
    low = (value - high.astype(F32)).astype(BF16)
    return high, low


def wide(value, axis=1):
    return jnp.concatenate(split(value), axis=axis)


def lane_shift(value, step):
    lanes = lax.broadcasted_iota(jnp.int32, value.shape, 1)
    return jnp.where(lanes >= step, pltpu.roll(value, step, 1), 0.0), lanes >= step


def cumulative_rows(value):
    step = 1
    while step < value.shape[1]:
        value = value + lane_shift(value, step)[0]
        step *= 2
    return value


def decayed_rows(value, cumulative):
    step = 1
    while step < value.shape[1]:
        earlier, inside = lane_shift(cumulative, step)
        factor = jnp.exp(jnp.where(inside, cumulative - earlier, 0.0))
        value = value + factor * lane_shift(value, step)[0]
        step *= 2
    return value


def decay_tables(decay_ref):
    rows = decay_ref.shape[1]
    offset = jnp.zeros((decay_ref.shape[0], 1), F32)
    local, full = [], []
    for c in range(rows // SUB):
        part = cumulative_rows(decay_ref[:, c * SUB : (c + 1) * SUB])
        local.append(part)
        full.append(part + offset)
        offset = offset + part[:, SUB - 1 : SUB]
    return local, jnp.exp(offset - jnp.concatenate(full, axis=1)), jnp.exp(offset)


def states_kernel(half, per, keys_hbm, values_hbm, decay_ref, near_ref, away_ref, table_ref, work_ref, held_ref, done):
    rows, dim = keys_hbm.shape[0], SUB
    core = lax.axis_index("seq") % 2
    copies = []
    for slot in range(2 * half):
        block = 1 - core if slot < half else core
        group = block * half + slot % half
        column = pl.ds(pl.multiple_of(group * per * dim, per * dim), per * dim)
        for which, source in enumerate((keys_hbm, values_hbm)):
            target = held_ref.at[which, slot]
            copies.append(pltpu.make_async_copy(source.at[:, column], target, done.at[which, slot]))
            copies[-1].start()
    row_at = lax.broadcasted_iota(jnp.int32, (dim, dim), 0)
    column_at = lax.broadcasted_iota(jnp.int32, (dim, dim), 1)
    local, tails, total = decay_tables(decay_ref)
    work_ref[0] = tails
    work_ref[2] = jnp.broadcast_to(total, tails.shape)
    first_gram = {}
    for slot in range(2 * half):
        out, block = (away_ref, 1 - core) if slot < half else (near_ref, core)
        i = slot % half
        copies[2 * slot].wait()
        copies[2 * slot + 1].wait()
        for k in range(per):
            head = (block * half + i) * per + k
            column = slice(k * dim, (k + 1) * dim)
            key = held_ref[0, slot, :, column]
            tail = work_ref[0, pl.ds(head, 1), :]
            key_turned = key.astype(F32).T
            value_turned = held_ref[1, slot, :, column].astype(F32).T
            work_ref[1, pl.ds(head, 1), :] = jnp.sum(key_turned * key_turned, axis=0, keepdims=True)
            high, low = split(jnp.concatenate([key_turned * tail, value_turned * tail], axis=0))
            state = dot(high, key) + dot(low, key)
            gram = state[0:dim]
            at, second = i // 2, i % 2
            out[k, at, (1 + second) * dim : (2 + second) * dim, :] = state[dim:]
            decay = work_ref[2, pl.ds(head, 1), :][:, 0:SUB]
            out[k, at, 3 * dim + second : 3 * dim + second + 1, :] = decay
            if second == 0:
                first_gram[k] = gram
            else:
                out[k, at, 0:dim, :] = jnp.where(row_at <= column_at, first_gram[k], gram)
                diagonal = jnp.sum(jnp.where(row_at == column_at, gram, 0.0), axis=0, keepdims=True)
                out[k, at, 3 * dim + 2 : 3 * dim + 3, :] = diagonal
                out[k, at, 3 * dim + 3 :, :] = jnp.zeros((EXTRA - 3, dim), F32)
    carry = jnp.zeros_like(total)
    for c in range(rows // SUB):
        lanes = slice(c * SUB, (c + 1) * SUB)
        part = decayed_rows(work_ref[1, :, lanes], local[c]) + jnp.exp(local[c]) * carry
        table_ref[0, :, lanes] = local[c]
        table_ref[1, :, lanes] = part
        carry = part[:, SUB - 1 : SUB]


def local_states(keys, values, decay, half, per):
    rows, columns = keys.shape
    heads = decay.shape[0]
    dim = columns // heads
    state = jax.ShapeDtypeStruct((per, half // 2, 3 * dim + EXTRA, dim), F32)
    table = jax.ShapeDtypeStruct((2, heads, rows), F32)
    return pl.pallas_call(
        functools.partial(states_kernel, half, per),
        out_shape=[state, state, table],
        in_specs=[pl.BlockSpec(memory_space=pl.ANY)] * 2 + [whole(decay)],
        out_specs=[whole(state), whole(state), whole(table)],
        scratch_shapes=[
            pltpu.VMEM((3, heads, rows), F32),
            pltpu.VMEM((2, 2 * half, rows, per * dim), keys.dtype),
            pltpu.SemaphoreType.DMA((2, 2 * half)),
        ],
        grid=(1,),
        compiler_params=FULL,
        cost_estimate=pl.CostEstimate(
            flops=16 * rows * dim * dim * half * per, bytes_accessed=8 * rows * columns, transcendentals=0
        ),
        name="local_states",
    )(keys, values, decay)


def join(earlier, later, dim):
    row_at = lax.broadcasted_iota(jnp.int32, later.shape, 1)
    column_at = lax.broadcasted_iota(jnp.int32, later.shape, 2)
    is_first = (row_at < dim) & (row_at <= column_at) | (row_at >= dim) & (row_at < 2 * dim)
    is_first = is_first | (row_at == 3 * dim)
    is_decay = (row_at == 3 * dim) | (row_at == 3 * dim + 1)
    factor = jnp.where(is_first, later[:, 3 * dim : 3 * dim + 1], later[:, 3 * dim + 1 : 3 * dim + 2])
    return factor * earlier + jnp.where(is_decay, 0.0, later)


def chip_kernel(dim, own_ref, came_ref, *out_refs):
    is_first = lax.axis_index("seq") % 2 == 0
    for k, out_ref in enumerate(out_refs):
        own, came = own_ref[k], came_ref[k]
        out_ref[...] = join(jnp.where(is_first, own, came), jnp.where(is_first, came, own), dim)


def start_kernel(dim, k, own_ref, came_ref, *refs):
    sent_refs, (mine_ref, other_ref) = refs[:-2], refs[-2:]
    is_first = lax.axis_index("seq") % 2 == 0
    before = sent_refs[-1][...]
    for ref in reversed(sent_refs[:-1]):
        before = join(before, ref[...], dim)
    after = join(before, jnp.where(is_first, own_ref[k], came_ref[k]), dim)
    mine_ref[...] = jnp.where(is_first, before, after)
    other_ref[...] = jnp.where(is_first, after, before)


def combine(kernel, arrays, shape, outs):
    out = jax.ShapeDtypeStruct(shape, F32)
    return pl.pallas_call(
        kernel,
        out_shape=[out] * outs,
        in_specs=[whole(a) for a in arrays],
        out_specs=[whole(out)] * outs,
        grid=(1,),
        compiler_params=FULL,
        cost_estimate=pl.CostEstimate(
            flops=0, bytes_accessed=8 * sum(a.size for a in arrays), transcendentals=0
        ),
    )(*arrays)


def solve_kernel(with_query, with_gradient, bounds, head_of, place_ref, regular_ref, *refs):
    refs = list(refs)
    q_ref = refs.pop(0) if with_query else None
    g_ref = refs.pop(0) if with_gradient else None
    k_ref, v_ref, rows_ref = refs[:3]
    state_refs, refs = refs[3 : 3 + len(bounds)], refs[3 + len(bounds) :]
    turned_ref = refs.pop() if with_gradient else None
    mixed_ref = refs.pop() if with_query else None
    rows, dim = k_ref.shape
    pieces = range(rows // SUB)
    place = [slice(c * SUB, (c + 1) * SUB) for c in pieces]
    step = pl.program_id(0)
    head = head_of(step, place_ref)
    ridge = regular_ref[head]
    row_at = lax.broadcasted_iota(jnp.int32, (SUB, SUB), 0)
    column_at = lax.broadcasted_iota(jnp.int32, (SUB, SUB), 1)
    lower = row_at >= column_at

    is_second = lax.rem(step, 2) == 1

    def state(start, size):
        at = pl.ds(start, size)
        if len(state_refs) == 1:
            return state_refs[0][0, at, :]
        return jnp.where(step < bounds[1], state_refs[0][0, at, :], state_refs[1][0, at, :])

    packed = state(0, dim)
    direct = (row_at > column_at) == is_second
    start = jnp.where(direct, packed, packed.T)
    diagonal = state(3 * dim, EXTRA)[2:3]
    gram = [jnp.where((row_at == column_at) & is_second, diagonal, start)]
    memory = [state(pl.multiple_of((1 + lax.rem(step, 2)) * dim, dim), dim)]
    start_trace = jnp.sum(jnp.where(row_at == column_at, gram[0], 0.0), axis=0, keepdims=True)
    start_trace = jnp.sum(start_trace, axis=1, keepdims=True)
    cumulative_row = rows_ref[0, pl.ds(head, 1), :]
    cumulative = [cumulative_row[:, at] for at in place]
    last = [row[:, SUB - 1 : SUB] for row in cumulative]
    whole, offset = [], jnp.zeros((1, 1), F32)
    for c in pieces:
        whole.append(cumulative[c] + offset)
        offset = offset + last[c]
    trace = jnp.exp(jnp.concatenate(whole, axis=1)) * start_trace + rows_ref[1, pl.ds(head, 1), :]
    span = 0.5 * trace
    center = ridge + span
    alphas, gammas = [1.0 / center], []
    for i in range(1, ITERS):
        factor = 0.5 if i == 1 else 0.25
        product = span * alphas[-1]
        alphas.append(1.0 / (center - factor * span * product))
        gammas.append(alphas[-1] * (factor * span * product))
    table = jnp.concatenate(alphas + gammas + [cumulative_row], axis=0).T

    def column(index):
        return [jnp.broadcast_to(table[at, index : index + 1], (SUB, SUB)) for at in place]

    rise = column(2 * ITERS - 1)
    weights = [
        jnp.where(lower, jnp.exp(jnp.where(lower, rise[c] - cumulative[c], 0.0)), 0.0) for c in pieces
    ]
    scale = [jnp.exp(r) for r in rise]

    keys = [k_ref[at, :] for at in place]
    values = [v_ref[at, :] for at in place]
    keys_turned = [key.astype(F32).T for key in keys]
    values_turned = [value.astype(F32).T for value in values]
    for c in pieces[:-1]:
        tail = jnp.exp(last[c] - cumulative[c])
        decay = jnp.exp(last[c])
        both = jnp.concatenate([keys_turned[c] * tail, values_turned[c] * tail], axis=0)
        grown = dot(wide(both), jnp.concatenate([keys[c], keys[c]], axis=0))
        gram.append(decay * gram[-1] + grown[0:dim])
        memory.append(decay * memory[-1] + grown[dim:])
    keys_turned = [key.astype(BF16) for key in keys_turned]
    values_turned = [value.astype(BF16) for value in values_turned]

    def pair(left, right):
        return jnp.concatenate([left, right], axis=0)

    def each(value):
        return pair(value, value) if with_query and with_gradient else value

    residual = []
    for c in pieces:
        sides = []
        if with_query:
            sides.append(q_ref[place[c], :].astype(F32))
        if with_gradient:
            grad = g_ref[place[c], :]
            pulled = scale[c] * dot(jnp.concatenate([grad, grad], axis=1), wide(memory[c], 0))
            score = weights[c] * dot(grad, values_turned[c])
            sides.append(pulled + dot(wide(score), pair(keys[c], keys[c])))
        residual.append(jnp.concatenate(sides, axis=0) if len(sides) > 1 else sides[0])

    alpha = column(0)
    change = [each(alpha[c]) * residual[c] for c in pieces]
    solution = list(change)
    rights = [jnp.concatenate([keys_turned[c], gram[c].astype(BF16)], axis=1) for c in pieces]
    for i in range(1, ITERS):
        alpha, gamma = column(i), column(ITERS + i - 1)
        first = [dot(change[c].astype(BF16), rights[c]) for c in pieces]
        second = [
            dot((first[c][:, 0:SUB] * each(weights[c])).astype(BF16), keys[c]) for c in pieces
        ]
        for c in pieces:
            applied = ridge * change[c] + (each(scale[c]) * first[c][:, SUB:] + second[c])
            residual[c] = residual[c] - applied
            change[c] = each(alpha[c]) * residual[c] + each(gamma[c]) * change[c]
            solution[c] = solution[c] + change[c]

    if with_gradient:
        for c in pieces:
            turned_ref[0, :, place[c]] = solution[c][-SUB:].T.astype(BF16).astype(F32)
    for c in pieces if with_query else ():
        high, low = split(solution[c][0:SUB])
        memory_high, memory_low = split(memory[c].T)
        right = jnp.concatenate([keys_turned[c], memory_high], axis=1)
        first = dot(jnp.concatenate([high, low], axis=1), pair(right, right))
        second = first[:, SUB:] + dot(high, memory_low)
        score = weights[c] * first[:, 0:SUB]
        output = scale[c] * second + dot(wide(score), pair(values[c], values[c]))
        mixed_ref[place[c], :] = output.astype(BF16)


def solve_heads(place, k, base, per, regular, queries, grads, keys, values, table, states, mixed, after):
    rows, columns = keys.shape
    heads = regular.shape[0]
    dim = columns // heads
    half = 2 * states[0].shape[0]
    groups, count = heads // per, half * len(states)
    with_query, with_gradient = queries is not None, grads is not None
    bounds = [half * i for i in range(len(states))]

    def head_of(step, place_ref):
        return lax.rem(place_ref[0] * half + base + step, groups) * per + k

    def at_head(step, place_ref, regular_ref):
        return (0, head_of(step, place_ref))

    wide_spec = pl.BlockSpec((rows, dim), at_head)
    operands = [a for a in (queries, grads, keys, values) if a is not None]
    in_specs = [wide_spec] * len(operands)
    operands.append(table)
    in_specs.append(whole(table))
    for bound, state in zip(bounds, states):

        def at_pair(step, *_, bound=bound):
            return (jnp.clip(step - bound, 0, half - 1) // 2, 0, 0)

        operands.append(state)
        in_specs.append(pl.BlockSpec((1,) + state.shape[1:], at_pair))
    aliases = {}
    if with_query and mixed is not None:
        operands.append(mixed)
        in_specs.append(pl.BlockSpec(memory_space=pl.ANY))
        aliases = {2 + len(operands) - 1: 0}
    if after is not None:
        operands.append(after)
        in_specs.append(pl.BlockSpec(memory_space=pl.ANY))
    shapes, out_specs = [], []
    if with_query:
        shapes.append(jax.ShapeDtypeStruct((rows, columns), BF16))
        out_specs.append(wide_spec)
    if with_gradient:
        shapes.append(jax.ShapeDtypeStruct((count, dim, rows), F32))
        out_specs.append(pl.BlockSpec((1, dim, rows), lambda step, *_: (step, 0, 0)))
    return pl.pallas_call(
        functools.partial(solve_kernel, with_query, with_gradient, bounds, head_of),
        out_shape=shapes,
        grid_spec=pltpu.PrefetchScalarGridSpec(
            num_scalar_prefetch=2, grid=(count,), in_specs=in_specs, out_specs=out_specs
        ),
        input_output_aliases=aliases,
        cost_estimate=pl.CostEstimate(
            flops=count * 80 * rows * dim * dim, bytes_accessed=count * 14 * rows * dim, transcendentals=0
        ),
        compiler_params=FULL,
        name="solve_heads",
    )(place, regular, *operands)


def pick_kernel(core_ref, tokens_ref, out_ref):
    out_ref[0] = tokens_ref[...].astype(F32)


def pick_columns(core, tokens, blocks):
    rows, width = tokens.shape
    size = width // (2 * blocks)
    return pl.pallas_call(
        pick_kernel,
        out_shape=jax.ShapeDtypeStruct((blocks, rows, size), F32),
        grid_spec=pltpu.PrefetchScalarGridSpec(
            num_scalar_prefetch=1,
            grid=(blocks,),
            in_specs=[pl.BlockSpec((rows, size), lambda z, core_ref: (0, 2 * z + 1 - core_ref[0]))],
            out_specs=pl.BlockSpec((1, rows, size), lambda z, core_ref: (z, 0, 0)),
        ),
        cost_estimate=pl.CostEstimate(flops=0, bytes_accessed=3 * rows * width, transcendentals=0),
        compiler_params=FULL,
        name="pick_columns",
    )(core, tokens)


def gradient_kernel(order, place_ref, own_ref, far_ref, tokens_ref, other_ref, *rest):
    outs, left_ref = rest[:-1], rest[-1]
    core, group = place_ref[0], place_ref[1]
    count, dim, rows = own_ref.shape
    half = count // 2
    middle = dim // 2

    @pl.when(pl.program_id(0) == 0)
    def _():
        for i in range(half):
            near, away = (core * half + i) ^ group, ((1 - core) * half + i) ^ group
            left_ref[near, :, 0:rows] = own_ref[i].astype(BF16)
            left_ref[away, :, 0:rows] = own_ref[half + i].astype(BF16)
            left_ref[near, :, rows:] = far_ref[half + i].astype(BF16)
            left_ref[away, :, rows:] = far_ref[i].astype(BF16)

    left = left_ref[...].reshape(2 * half * dim, 2 * rows)
    result = dot(left, jnp.concatenate([tokens_ref[...], other_ref[0].astype(BF16)], axis=0))
    for d in range(2 * half):
        for path in range(2):
            which, index = order[path][d]
            start = d * dim + path * middle
            outs[2 * path + which][index, 0] = result[start : start + middle]


def gradient_blocks(place, own, far, tokens, other, order):
    count, dim, rows = own.shape
    half = count // 2
    blocks, _, size = other.shape
    out = jax.ShapeDtypeStruct((half, blocks, dim // 2, size), F32)
    turned_spec = pl.BlockSpec((count, dim, rows), lambda z, p: (0, 0, 0))
    return pl.pallas_call(
        functools.partial(gradient_kernel, order),
        out_shape=[out] * 4,
        grid_spec=pltpu.PrefetchScalarGridSpec(
            num_scalar_prefetch=1,
            grid=(blocks,),
            in_specs=[turned_spec] * 2
            + [
                pl.BlockSpec((rows, size), lambda z, p: (0, 2 * (p[2] ^ z) + p[0])),
                pl.BlockSpec((1, rows, size), lambda z, p: (p[2] ^ z, 0, 0)),
            ],
            out_specs=[pl.BlockSpec((half, 1, dim // 2, size), lambda z, p: (0, z, 0, 0))] * 4,
            scratch_shapes=[pltpu.VMEM((2 * half, dim, 2 * rows), BF16)],
        ),
        cost_estimate=pl.CostEstimate(
            flops=8 * half * dim * rows * blocks * size,
            bytes_accessed=4 * (4 * half * dim * rows + blocks * rows * size + 2 * half * blocks * dim * size),
            transcendentals=0,
        ),
        compiler_params=FULL,
        name="gradient_blocks",
    )(place, own, far, tokens, other)


def sum_kernel(counts, *refs):
    arrays, outs = refs[: sum(counts)], refs[sum(counts) :]
    at = 0
    for count, out in zip(counts, outs):
        total = arrays[at][...]
        for ref in arrays[at + 1 : at + count]:
            total = total + ref[...]
        out[...] = total
        at += count


def sum_blocks(sums, length):
    counts = [len(arrays) for arrays in sums]
    arrays = [a for group in sums for a in group]
    out = jax.ShapeDtypeStruct((length,) + arrays[0].shape[1:], F32)
    return pl.pallas_call(
        functools.partial(sum_kernel, counts),
        out_shape=[out] * len(sums),
        in_specs=[pl.BlockSpec(out.shape, lambda _: (1, 0, 0, 0))] * len(arrays),
        out_specs=[whole(out)] * len(sums),
        grid=(1,),
        compiler_params=FULL,
        cost_estimate=pl.CostEstimate(
            flops=0, bytes_accessed=4 * (len(arrays) + 2) * out.size, transcendentals=0
        ),
        name="sum_blocks",
    )(*arrays)


def merge_kernel(counts, *refs):
    sums, outs = refs[: sum(counts)], refs[sum(counts) :]
    rows = sums[0].shape[2]
    at = 0
    for i, count in enumerate(counts):
        for z, out in enumerate(outs):
            total = sums[at][0, z]
            for ref in sums[at + 1 : at + count]:
                total = total + ref[0, z]
            out[i * rows : (i + 1) * rows, :] = total
        at += count


def merge_blocks(sums):
    counts = [len(arrays) for arrays in sums]
    arrays = [a for group in sums for a in group]
    _, chips, rows, size = arrays[0].shape
    out = jax.ShapeDtypeStruct((len(counts) * rows, size), F32)
    return pl.pallas_call(
        functools.partial(merge_kernel, counts),
        out_shape=[out] * chips,
        in_specs=[pl.BlockSpec((1, chips, rows, size), lambda _: (0, 0, 0, 0))] * len(arrays),
        out_specs=[whole(out)] * chips,
        grid=(1,),
        compiler_params=FULL,
        cost_estimate=pl.CostEstimate(
            flops=0, bytes_accessed=4 * (len(arrays) + 2) * chips * rows * size, transcendentals=0
        ),
        name="merge_blocks",
    )(*arrays)


def finish_kernel(count, *refs):
    out = refs[-1]
    rows = refs[0].shape[0]
    for k in range((len(refs) - 1) // count):
        total = refs[k * count][...]
        for ref in refs[k * count + 1 : (k + 1) * count]:
            total = total + ref[...]
        out[k * rows : (k + 1) * rows, :] = total


def finish(sets):
    arrays = [a for group in sets for a in group]
    rows, size = arrays[0].shape
    out = jax.ShapeDtypeStruct((rows * len(sets), size), F32)
    return pl.pallas_call(
        functools.partial(finish_kernel, len(sets[0])),
        out_shape=out,
        in_specs=[whole(a) for a in arrays],
        out_specs=whole(out),
        grid=(1,),
        compiler_params=FULL,
        cost_estimate=pl.CostEstimate(
            flops=0, bytes_accessed=5 * sum(a.size for a in arrays), transcendentals=0
        ),
        name="finish",
    )(*arrays)


def bit_order(bits):
    table = []
    for d in range(1 << len(bits)):
        code = 0
        for bit in bits:
            code = 2 * code + ((d >> bit) & 1)
        table.append(divmod(code, 1 << (len(bits) - 1)))
    return table


def per_device(sizes, *arrays):
    return program(sizes, *arrays)


def program(sizes, tokens, w_query, keys, values, log_decay, regular, grad_out):
    groups, steps = sizes["dp"], sizes["seq"]
    chips = steps // 2
    heads = log_decay.shape[1]
    columns = keys.shape[2]
    dim = columns // heads
    per = heads // groups
    half = groups // 2
    tokens, keys, values, grads, decay = tokens[0], keys[0], values[0], grad_out[0], log_decay[0]
    here = lax.axis_index("seq")
    core = here % 2
    place = jnp.stack([core, lax.axis_index("dp"), here // 2]).astype(jnp.int32)
    partner = [(i, i ^ 1) for i in range(steps)]

    own, away, table = local_states(keys, values, decay, half, per)
    came = lax.ppermute(away, "seq", partner)
    shape = own.shape[1:]
    chip_states = combine(functools.partial(chip_kernel, dim), [own, came], shape, per)
    starts = []
    for k, chip_state in enumerate(chip_states):
        sent = []
        for z in range(1, chips):
            pairs = [(i, i + 2 * z) for i in range(steps - 2 * z)]
            sent.append(lax.ppermute(chip_state, "seq", pairs))
        starting = functools.partial(start_kernel, dim, k)
        mine, others = combine(starting, [own, came, *sent], shape, 2)
        starts.append((mine, lax.ppermute(others, "seq", partner)))

    picked = pick_columns(place, tokens, chips)
    other = lax.ppermute(picked, "seq", partner)
    queries = jnp.dot(tokens, w_query, preferred_element_type=F32).astype(BF16)

    dp_bits = groups.bit_length() - 1
    paths = [list(range(dp_bits)), list(reversed(range(dp_bits)))]
    order = [bit_order(path) for path in paths]

    products, mixed = [], None
    for k, states in enumerate(starts):
        after = products[-1][0] if k > 0 else None
        joint = k < per - 1
        results = solve_heads(
            place, k, 0, per, regular, queries if joint else None, grads, keys, values, table, states, mixed, after
        )
        turned = results[-1]
        if joint:
            mixed = results[0]
        far = lax.ppermute(turned, "seq", partner)
        products.append(gradient_blocks(place, turned, far, tokens, other, order))
    for side in range(2):
        after = products[-1][0] if side == 0 else None
        (mixed,) = solve_heads(
            place, per - 1, side * half, per, regular, queries, None, keys, values, table,
            [starts[-1][side]], mixed, after,
        )

    finished = []
    for blocks in products:
        sums, sends = [[blocks[0]], [blocks[2]]], [blocks[1], blocks[3]]
        for stage in range(dp_bits):
            for index, path in enumerate(paths):
                pairs = [(i, i ^ (1 << path[stage])) for i in range(groups)]
                sums[index].append(lax.ppermute(sends[index], "dp", pairs))
            if stage < dp_bits - 1:
                sends = sum_blocks(sums, sends[0].shape[0] // 2)
        out, *others = merge_blocks(sums)
        finished.append([out])
        for z, other_block in enumerate(others, 1):
            pairs = [(i, i ^ (2 * z)) for i in range(steps)]
            finished[-1].append(lax.ppermute(other_block, "seq", pairs))
    return mixed[None], finish(finished)


def solution(mesh):
    sizes = dict(mesh.shape)
    in_specs = (
        P("dp", "seq", None),
        P(),
        P("dp", "seq", None),
        P("dp", "seq", None),
        P("dp", None, "seq"),
        P(),
        P("dp", "seq", None),
    )
    out_specs = (P("dp", "seq", None), P("dp", "seq"))
    return jax.shard_map(
        functools.partial(per_device, sizes),
        mesh=mesh,
        in_specs=in_specs,
        out_specs=out_specs,
        check_vma=False,
    )
```

```python
import functools

import jax
import jax.numpy as jnp
from jax import lax
from jax.experimental import pallas as pl
from jax.experimental.pallas import tpu as pltpu
from jax.sharding import PartitionSpec as P

ITERS = 4
SUB = 128
EXTRA = 8


F32 = jnp.float32
BF16 = jnp.bfloat16


FULL = pltpu.CompilerParams(vmem_limit_bytes=67_043_328)


def whole(array):
    return pl.BlockSpec(array.shape, lambda *_: (0,) * len(array.shape))


def dot(left, right):
    return jnp.dot(left, right, preferred_element_type=F32)


def split(value):
    high = value.astype(BF16)
    low = (value - high.astype(F32)).astype(BF16)
    return high, low


def wide(value, axis=1):
    return jnp.concatenate(split(value), axis=axis)


def lane_shift(value, step):
    lanes = lax.broadcasted_iota(jnp.int32, value.shape, 1)
    return jnp.where(lanes >= step, pltpu.roll(value, step, 1), 0.0), lanes >= step


def cumulative_rows(value):
    step = 1
    while step < value.shape[1]:
        value = value + lane_shift(value, step)[0]
        step *= 2
    return value


def decayed_rows(value, cumulative):
    step = 1
    while step < value.shape[1]:
        earlier, inside = lane_shift(cumulative, step)
        factor = jnp.exp(jnp.where(inside, cumulative - earlier, 0.0))
        value = value + factor * lane_shift(value, step)[0]
        step *= 2
    return value


def decay_tables(decay_ref):
    rows = decay_ref.shape[1]
    offset = jnp.zeros((decay_ref.shape[0], 1), F32)
    local, full = [], []
    for c in range(rows // SUB):
        part = cumulative_rows(decay_ref[:, c * SUB : (c + 1) * SUB])
        local.append(part)
        full.append(part + offset)
        offset = offset + part[:, SUB - 1 : SUB]
    return local, jnp.exp(offset - jnp.concatenate(full, axis=1)), jnp.exp(offset)


def states_kernel(half, per, keys_ref, values_ref, decay_ref, near_ref, away_ref, table_ref, work_ref):
    rows, dim = keys_ref.shape[0], SUB
    core = lax.axis_index("seq") % 2
    row_at = lax.broadcasted_iota(jnp.int32, (dim, dim), 0)
    column_at = lax.broadcasted_iota(jnp.int32, (dim, dim), 1)
    local, tails, total = decay_tables(decay_ref)
    work_ref[0] = tails
    work_ref[2] = jnp.broadcast_to(total, tails.shape)
    first_gram = {}
    for slot in range(2 * half):
        out, block = (away_ref, 1 - core) if slot < half else (near_ref, core)
        i = slot % half
        for k in range(per):
            head = (block * half + i) * per + k
            column = pl.ds(pl.multiple_of(head * dim, dim), dim)
            key = keys_ref[:, column]
            tail = work_ref[0, pl.ds(head, 1), :]
            key_turned = key.astype(F32).T
            value_turned = values_ref[:, column].astype(F32).T
            work_ref[1, pl.ds(head, 1), :] = jnp.sum(key_turned * key_turned, axis=0, keepdims=True)
            high, low = split(jnp.concatenate([key_turned * tail, value_turned * tail], axis=0))
            state = dot(high, key) + dot(low, key)
            gram = state[0:dim]
            at, second = i // 2, i % 2
            out[k, at, (1 + second) * dim : (2 + second) * dim, :] = state[dim:]
            decay = work_ref[2, pl.ds(head, 1), :][:, 0:SUB]
            out[k, at, 3 * dim + second : 3 * dim + second + 1, :] = decay
            if second == 0:
                first_gram[k] = gram
            else:
                out[k, at, 0:dim, :] = jnp.where(row_at <= column_at, first_gram[k], gram)
                diagonal = jnp.sum(jnp.where(row_at == column_at, gram, 0.0), axis=0, keepdims=True)
                out[k, at, 3 * dim + 2 : 3 * dim + 3, :] = diagonal
                out[k, at, 3 * dim + 3 :, :] = jnp.zeros((EXTRA - 3, dim), F32)
    carry = jnp.zeros_like(total)
    for c in range(rows // SUB):
        lanes = slice(c * SUB, (c + 1) * SUB)
        part = decayed_rows(work_ref[1, :, lanes], local[c]) + jnp.exp(local[c]) * carry
        table_ref[0, :, lanes] = local[c]
        table_ref[1, :, lanes] = part
        carry = part[:, SUB - 1 : SUB]


def local_states(keys, values, decay, half, per):
    rows, columns = keys.shape
    heads = decay.shape[0]
    dim = columns // heads
    state = jax.ShapeDtypeStruct((per, half // 2, 3 * dim + EXTRA, dim), F32)
    table = jax.ShapeDtypeStruct((2, heads, rows), F32)
    return pl.pallas_call(
        functools.partial(states_kernel, half, per),
        out_shape=[state, state, table],
        in_specs=[whole(a) for a in (keys, values, decay)],
        out_specs=[whole(state), whole(state), whole(table)],
        scratch_shapes=[pltpu.VMEM((3, heads, rows), F32)],
        grid=(1,),
        compiler_params=FULL,
        cost_estimate=pl.CostEstimate(
            flops=16 * rows * dim * dim * half * per, bytes_accessed=8 * rows * columns, transcendentals=0
        ),
        name="local_states",
    )(keys, values, decay)


def join(earlier, later, dim):
    row_at = lax.broadcasted_iota(jnp.int32, later.shape, 1)
    column_at = lax.broadcasted_iota(jnp.int32, later.shape, 2)
    is_first = (row_at < dim) & (row_at <= column_at) | (row_at >= dim) & (row_at < 2 * dim)
    is_first = is_first | (row_at == 3 * dim)
    is_decay = (row_at == 3 * dim) | (row_at == 3 * dim + 1)
    factor = jnp.where(is_first, later[:, 3 * dim : 3 * dim + 1], later[:, 3 * dim + 1 : 3 * dim + 2])
    return factor * earlier + jnp.where(is_decay, 0.0, later)


def chip_kernel(dim, own_ref, came_ref, *out_refs):
    is_first = lax.axis_index("seq") % 2 == 0
    for k, out_ref in enumerate(out_refs):
        own, came = own_ref[k], came_ref[k]
        out_ref[...] = join(jnp.where(is_first, own, came), jnp.where(is_first, came, own), dim)


def start_kernel(dim, k, own_ref, came_ref, *refs):
    sent_refs, (mine_ref, other_ref) = refs[:-2], refs[-2:]
    is_first = lax.axis_index("seq") % 2 == 0
    before = sent_refs[-1][...]
    for ref in reversed(sent_refs[:-1]):
        before = join(before, ref[...], dim)
    after = join(before, jnp.where(is_first, own_ref[k], came_ref[k]), dim)
    mine_ref[...] = jnp.where(is_first, before, after)
    other_ref[...] = jnp.where(is_first, after, before)


def combine(kernel, arrays, shape, outs):
    out = jax.ShapeDtypeStruct(shape, F32)
    return pl.pallas_call(
        kernel,
        out_shape=[out] * outs,
        in_specs=[whole(a) for a in arrays],
        out_specs=[whole(out)] * outs,
        grid=(1,),
        compiler_params=FULL,
        cost_estimate=pl.CostEstimate(
            flops=0, bytes_accessed=8 * sum(a.size for a in arrays), transcendentals=0
        ),
    )(*arrays)


def solve_kernel(with_query, with_gradient, bounds, head_of, place_ref, regular_ref, *refs):
    refs = list(refs)
    q_ref = refs.pop(0) if with_query else None
    g_ref = refs.pop(0) if with_gradient else None
    k_ref, v_ref, rows_ref = refs[:3]
    state_refs, refs = refs[3 : 3 + len(bounds)], refs[3 + len(bounds) :]
    turned_ref = refs.pop() if with_gradient else None
    mixed_ref = refs.pop() if with_query else None
    rows, dim = k_ref.shape
    pieces = range(rows // SUB)
    place = [slice(c * SUB, (c + 1) * SUB) for c in pieces]
    step = pl.program_id(0)
    head = head_of(step, place_ref)
    ridge = regular_ref[head]
    row_at = lax.broadcasted_iota(jnp.int32, (SUB, SUB), 0)
    column_at = lax.broadcasted_iota(jnp.int32, (SUB, SUB), 1)
    lower = row_at >= column_at

    is_second = lax.rem(step, 2) == 1

    def state(start, size):
        at = pl.ds(start, size)
        if len(state_refs) == 1:
            return state_refs[0][0, at, :]
        return jnp.where(step < bounds[1], state_refs[0][0, at, :], state_refs[1][0, at, :])

    packed = state(0, dim)
    direct = (row_at > column_at) == is_second
    start = jnp.where(direct, packed, packed.T)
    diagonal = state(3 * dim, EXTRA)[2:3]
    gram = [jnp.where((row_at == column_at) & is_second, diagonal, start)]
    memory = [state(pl.multiple_of((1 + lax.rem(step, 2)) * dim, dim), dim)]
    start_trace = jnp.sum(jnp.where(row_at == column_at, gram[0], 0.0), axis=0, keepdims=True)
    start_trace = jnp.sum(start_trace, axis=1, keepdims=True)
    cumulative_row = rows_ref[0, pl.ds(head, 1), :]
    cumulative = [cumulative_row[:, at] for at in place]
    last = [row[:, SUB - 1 : SUB] for row in cumulative]
    whole, offset = [], jnp.zeros((1, 1), F32)
    for c in pieces:
        whole.append(cumulative[c] + offset)
        offset = offset + last[c]
    trace = jnp.exp(jnp.concatenate(whole, axis=1)) * start_trace + rows_ref[1, pl.ds(head, 1), :]
    span = 0.5 * trace
    center = ridge + span
    alphas, gammas = [1.0 / center], []
    for i in range(1, ITERS):
        factor = 0.5 if i == 1 else 0.25
        product = span * alphas[-1]
        alphas.append(1.0 / (center - factor * span * product))
        gammas.append(alphas[-1] * (factor * span * product))
    table = jnp.concatenate(alphas + gammas + [cumulative_row], axis=0).T

    def column(index):
        return [jnp.broadcast_to(table[at, index : index + 1], (SUB, SUB)) for at in place]

    rise = column(2 * ITERS - 1)
    weights = [
        jnp.where(lower, jnp.exp(jnp.where(lower, rise[c] - cumulative[c], 0.0)), 0.0) for c in pieces
    ]
    scale = [jnp.exp(r) for r in rise]

    keys = [k_ref[at, :] for at in place]
    values = [v_ref[at, :] for at in place]
    keys_turned = [key.astype(F32).T for key in keys]
    values_turned = [value.astype(F32).T for value in values]
    for c in pieces[:-1]:
        tail = jnp.exp(last[c] - cumulative[c])
        decay = jnp.exp(last[c])
        both = jnp.concatenate([keys_turned[c] * tail, values_turned[c] * tail], axis=0)
        grown = dot(wide(both), jnp.concatenate([keys[c], keys[c]], axis=0))
        gram.append(decay * gram[-1] + grown[0:dim])
        memory.append(decay * memory[-1] + grown[dim:])
    keys_turned = [key.astype(BF16) for key in keys_turned]
    values_turned = [value.astype(BF16) for value in values_turned]

    def pair(left, right):
        return jnp.concatenate([left, right], axis=0)

    def each(value):
        return pair(value, value) if with_query and with_gradient else value

    residual = []
    for c in pieces:
        sides = []
        if with_query:
            sides.append(q_ref[place[c], :].astype(F32))
        if with_gradient:
            grad = g_ref[place[c], :]
            pulled = scale[c] * dot(jnp.concatenate([grad, grad], axis=1), wide(memory[c], 0))
            score = weights[c] * dot(grad, values_turned[c])
            sides.append(pulled + dot(wide(score), pair(keys[c], keys[c])))
        residual.append(jnp.concatenate(sides, axis=0) if len(sides) > 1 else sides[0])

    alpha = column(0)
    change = [each(alpha[c]) * residual[c] for c in pieces]
    solution = list(change)
    rights = [jnp.concatenate([keys_turned[c], gram[c].astype(BF16)], axis=1) for c in pieces]
    for i in range(1, ITERS):
        alpha, gamma = column(i), column(ITERS + i - 1)
        first = [dot(change[c].astype(BF16), rights[c]) for c in pieces]
        second = [
            dot((first[c][:, 0:SUB] * each(weights[c])).astype(BF16), keys[c]) for c in pieces
        ]
        for c in pieces:
            applied = ridge * change[c] + (each(scale[c]) * first[c][:, SUB:] + second[c])
            residual[c] = residual[c] - applied
            change[c] = each(alpha[c]) * residual[c] + each(gamma[c]) * change[c]
            solution[c] = solution[c] + change[c]

    if with_gradient:
        for c in pieces:
            turned_ref[0, :, place[c]] = solution[c][-SUB:].T.astype(BF16).astype(F32)
    for c in pieces if with_query else ():
        high, low = split(solution[c][0:SUB])
        memory_high, memory_low = split(memory[c].T)
        right = jnp.concatenate([keys_turned[c], memory_high], axis=1)
        first = dot(jnp.concatenate([high, low], axis=1), pair(right, right))
        second = first[:, SUB:] + dot(high, memory_low)
        score = weights[c] * first[:, 0:SUB]
        output = scale[c] * second + dot(wide(score), pair(values[c], values[c]))
        mixed_ref[place[c], :] = output.astype(BF16)


def solve_heads(place, k, base, per, regular, queries, grads, keys, values, table, states, mixed, after):
    rows, columns = keys.shape
    heads = regular.shape[0]
    dim = columns // heads
    half = 2 * states[0].shape[0]
    groups, count = heads // per, half * len(states)
    with_query, with_gradient = queries is not None, grads is not None
    bounds = [half * i for i in range(len(states))]

    def head_of(step, place_ref):
        return lax.rem(place_ref[0] * half + base + step, groups) * per + k

    def at_head(step, place_ref, regular_ref):
        return (0, head_of(step, place_ref))

    wide_spec = pl.BlockSpec((rows, dim), at_head)
    operands = [a for a in (queries, grads, keys, values) if a is not None]
    in_specs = [wide_spec] * len(operands)
    operands.append(table)
    in_specs.append(whole(table))
    for bound, state in zip(bounds, states):

        def at_pair(step, *_, bound=bound):
            return (jnp.clip(step - bound, 0, half - 1) // 2, 0, 0)

        operands.append(state)
        in_specs.append(pl.BlockSpec((1,) + state.shape[1:], at_pair))
    aliases = {}
    if with_query and mixed is not None:
        operands.append(mixed)
        in_specs.append(pl.BlockSpec(memory_space=pl.ANY))
        aliases = {2 + len(operands) - 1: 0}
    if after is not None:
        operands.append(after)
        in_specs.append(pl.BlockSpec(memory_space=pl.ANY))
    shapes, out_specs = [], []
    if with_query:
        shapes.append(jax.ShapeDtypeStruct((rows, columns), BF16))
        out_specs.append(wide_spec)
    if with_gradient:
        shapes.append(jax.ShapeDtypeStruct((count, dim, rows), F32))
        out_specs.append(pl.BlockSpec((1, dim, rows), lambda step, *_: (step, 0, 0)))
    return pl.pallas_call(
        functools.partial(solve_kernel, with_query, with_gradient, bounds, head_of),
        out_shape=shapes,
        grid_spec=pltpu.PrefetchScalarGridSpec(
            num_scalar_prefetch=2, grid=(count,), in_specs=in_specs, out_specs=out_specs
        ),
        input_output_aliases=aliases,
        cost_estimate=pl.CostEstimate(
            flops=count * 80 * rows * dim * dim, bytes_accessed=count * 14 * rows * dim, transcendentals=0
        ),
        compiler_params=FULL,
        name="solve_heads",
    )(place, regular, *operands)


def pick_kernel(core_ref, tokens_ref, out_ref):
    out_ref[0] = tokens_ref[...].astype(F32)


def pick_columns(core, tokens, blocks):
    rows, width = tokens.shape
    size = width // (2 * blocks)
    return pl.pallas_call(
        pick_kernel,
        out_shape=jax.ShapeDtypeStruct((blocks, rows, size), F32),
        grid_spec=pltpu.PrefetchScalarGridSpec(
            num_scalar_prefetch=1,
            grid=(blocks,),
            in_specs=[pl.BlockSpec((rows, size), lambda z, core_ref: (0, 2 * z + 1 - core_ref[0]))],
            out_specs=pl.BlockSpec((1, rows, size), lambda z, core_ref: (z, 0, 0)),
        ),
        cost_estimate=pl.CostEstimate(flops=0, bytes_accessed=3 * rows * width, transcendentals=0),
        compiler_params=FULL,
        name="pick_columns",
    )(core, tokens)


def gradient_kernel(order, place_ref, own_ref, far_ref, tokens_ref, other_ref, *rest):
    outs, left_ref = rest[:-1], rest[-1]
    core, group = place_ref[0], place_ref[1]
    count, dim, rows = own_ref.shape
    half = count // 2
    middle = dim // 2

    @pl.when(pl.program_id(0) == 0)
    def _():
        for i in range(half):
            near, away = (core * half + i) ^ group, ((1 - core) * half + i) ^ group
            left_ref[near, :, 0:rows] = own_ref[i].astype(BF16)
            left_ref[away, :, 0:rows] = own_ref[half + i].astype(BF16)
            left_ref[near, :, rows:] = far_ref[half + i].astype(BF16)
            left_ref[away, :, rows:] = far_ref[i].astype(BF16)

    left = left_ref[...].reshape(2 * half * dim, 2 * rows)
    result = dot(left, jnp.concatenate([tokens_ref[...], other_ref[0].astype(BF16)], axis=0))
    for d in range(2 * half):
        for path in range(2):
            which, index = order[path][d]
            start = d * dim + path * middle
            outs[2 * path + which][index, 0] = result[start : start + middle]


def gradient_blocks(place, own, far, tokens, other, order):
    count, dim, rows = own.shape
    half = count // 2
    blocks, _, size = other.shape
    out = jax.ShapeDtypeStruct((half, blocks, dim // 2, size), F32)
    turned_spec = pl.BlockSpec((count, dim, rows), lambda z, p: (0, 0, 0))
    return pl.pallas_call(
        functools.partial(gradient_kernel, order),
        out_shape=[out] * 4,
        grid_spec=pltpu.PrefetchScalarGridSpec(
            num_scalar_prefetch=1,
            grid=(blocks,),
            in_specs=[turned_spec] * 2
            + [
                pl.BlockSpec((rows, size), lambda z, p: (0, 2 * (p[2] ^ z) + p[0])),
                pl.BlockSpec((1, rows, size), lambda z, p: (p[2] ^ z, 0, 0)),
            ],
            out_specs=[pl.BlockSpec((half, 1, dim // 2, size), lambda z, p: (0, z, 0, 0))] * 4,
            scratch_shapes=[pltpu.VMEM((2 * half, dim, 2 * rows), BF16)],
        ),
        cost_estimate=pl.CostEstimate(
            flops=8 * half * dim * rows * blocks * size,
            bytes_accessed=4 * (4 * half * dim * rows + blocks * rows * size + 2 * half * blocks * dim * size),
            transcendentals=0,
        ),
        compiler_params=FULL,
        name="gradient_blocks",
    )(place, own, far, tokens, other)


def sum_kernel(counts, *refs):
    arrays, outs = refs[: sum(counts)], refs[sum(counts) :]
    at = 0
    for count, out in zip(counts, outs):
        total = arrays[at][...]
        for ref in arrays[at + 1 : at + count]:
            total = total + ref[...]
        out[...] = total
        at += count


def sum_blocks(sums, length):
    counts = [len(arrays) for arrays in sums]
    arrays = [a for group in sums for a in group]
    out = jax.ShapeDtypeStruct((length,) + arrays[0].shape[1:], F32)
    return pl.pallas_call(
        functools.partial(sum_kernel, counts),
        out_shape=[out] * len(sums),
        in_specs=[pl.BlockSpec(out.shape, lambda _: (1, 0, 0, 0))] * len(arrays),
        out_specs=[whole(out)] * len(sums),
        grid=(1,),
        compiler_params=FULL,
        cost_estimate=pl.CostEstimate(
            flops=0, bytes_accessed=4 * (len(arrays) + 2) * out.size, transcendentals=0
        ),
        name="sum_blocks",
    )(*arrays)


def merge_kernel(counts, *refs):
    sums, outs = refs[: sum(counts)], refs[sum(counts) :]
    rows = sums[0].shape[2]
    at = 0
    for i, count in enumerate(counts):
        for z, out in enumerate(outs):
            total = sums[at][0, z]
            for ref in sums[at + 1 : at + count]:
                total = total + ref[0, z]
            out[i * rows : (i + 1) * rows, :] = total
        at += count


def merge_blocks(sums):
    counts = [len(arrays) for arrays in sums]
    arrays = [a for group in sums for a in group]
    _, chips, rows, size = arrays[0].shape
    out = jax.ShapeDtypeStruct((len(counts) * rows, size), F32)
    return pl.pallas_call(
        functools.partial(merge_kernel, counts),
        out_shape=[out] * chips,
        in_specs=[pl.BlockSpec((1, chips, rows, size), lambda _: (0, 0, 0, 0))] * len(arrays),
        out_specs=[whole(out)] * chips,
        grid=(1,),
        compiler_params=FULL,
        cost_estimate=pl.CostEstimate(
            flops=0, bytes_accessed=4 * (len(arrays) + 2) * chips * rows * size, transcendentals=0
        ),
        name="merge_blocks",
    )(*arrays)


def finish_kernel(count, *refs):
    out = refs[-1]
    rows = refs[0].shape[0]
    for k in range((len(refs) - 1) // count):
        total = refs[k * count][...]
        for ref in refs[k * count + 1 : (k + 1) * count]:
            total = total + ref[...]
        out[k * rows : (k + 1) * rows, :] = total


def finish(sets):
    arrays = [a for group in sets for a in group]
    rows, size = arrays[0].shape
    out = jax.ShapeDtypeStruct((rows * len(sets), size), F32)
    return pl.pallas_call(
        functools.partial(finish_kernel, len(sets[0])),
        out_shape=out,
        in_specs=[whole(a) for a in arrays],
        out_specs=whole(out),
        grid=(1,),
        compiler_params=FULL,
        cost_estimate=pl.CostEstimate(
            flops=0, bytes_accessed=5 * sum(a.size for a in arrays), transcendentals=0
        ),
        name="finish",
    )(*arrays)


def bit_order(bits):
    table = []
    for d in range(1 << len(bits)):
        code = 0
        for bit in bits:
            code = 2 * code + ((d >> bit) & 1)
        table.append(divmod(code, 1 << (len(bits) - 1)))
    return table


def per_device(sizes, *arrays):
    return program(sizes, *arrays)


def program(sizes, tokens, w_query, keys, values, log_decay, regular, grad_out):
    groups, steps = sizes["dp"], sizes["seq"]
    chips = steps // 2
    heads = log_decay.shape[1]
    columns = keys.shape[2]
    dim = columns // heads
    per = heads // groups
    half = groups // 2
    tokens, keys, values, grads, decay = tokens[0], keys[0], values[0], grad_out[0], log_decay[0]
    here = lax.axis_index("seq")
    core = here % 2
    place = jnp.stack([core, lax.axis_index("dp"), here // 2]).astype(jnp.int32)
    partner = [(i, i ^ 1) for i in range(steps)]

    own, away, table = local_states(keys, values, decay, half, per)
    came = lax.ppermute(away, "seq", partner)
    shape = own.shape[1:]
    chip_states = combine(functools.partial(chip_kernel, dim), [own, came], shape, per)
    starts = []
    for k, chip_state in enumerate(chip_states):
        sent = []
        for z in range(1, chips):
            pairs = [(i, i + 2 * z) for i in range(steps - 2 * z)]
            sent.append(lax.ppermute(chip_state, "seq", pairs))
        starting = functools.partial(start_kernel, dim, k)
        mine, others = combine(starting, [own, came, *sent], shape, 2)
        starts.append((mine, lax.ppermute(others, "seq", partner)))

    picked = pick_columns(place, tokens, chips)
    other = lax.ppermute(picked, "seq", partner)
    queries = jnp.dot(tokens, w_query, preferred_element_type=F32).astype(BF16)

    dp_bits = groups.bit_length() - 1
    paths = [list(range(dp_bits)), list(reversed(range(dp_bits)))]
    order = [bit_order(path) for path in paths]

    products, mixed = [], None
    for k, states in enumerate(starts):
        after = products[-1][0] if k > 0 else None
        joint = k < per - 1
        results = solve_heads(
            place, k, 0, per, regular, queries if joint else None, grads, keys, values, table, states, mixed, after
        )
        turned = results[-1]
        if joint:
            mixed = results[0]
        far = lax.ppermute(turned, "seq", partner)
        products.append(gradient_blocks(place, turned, far, tokens, other, order))
    for side in range(2):
        after = products[-1][0] if side == 0 else None
        (mixed,) = solve_heads(
            place, per - 1, side * half, per, regular, queries, None, keys, values, table,
            [starts[-1][side]], mixed, after,
        )

    finished = []
    for blocks in products:
        sums, sends = [[blocks[0]], [blocks[2]]], [blocks[1], blocks[3]]
        for stage in range(dp_bits):
            for index, path in enumerate(paths):
                pairs = [(i, i ^ (1 << path[stage])) for i in range(groups)]
                sums[index].append(lax.ppermute(sends[index], "dp", pairs))
            if stage < dp_bits - 1:
                sends = sum_blocks(sums, sends[0].shape[0] // 2)
        out, *others = merge_blocks(sums)
        finished.append([out])
        for z, other_block in enumerate(others, 1):
            pairs = [(i, i ^ (2 * z)) for i in range(steps)]
            finished[-1].append(lax.ppermute(other_block, "seq", pairs))
    return mixed[None], finish(finished)


def solution(mesh):
    sizes = dict(mesh.shape)
    in_specs = (
        P("dp", "seq", None),
        P(),
        P("dp", "seq", None),
        P("dp", "seq", None),
        P("dp", None, "seq"),
        P(),
        P("dp", "seq", None),
    )
    out_specs = (P("dp", "seq", None), P("dp", "seq"))
    return jax.shard_map(
        functools.partial(per_device, sizes),
        mesh=mesh,
        in_specs=in_specs,
        out_specs=out_specs,
        check_vma=False,
    )
```

```python
import functools

import jax
import jax.numpy as jnp
from jax import lax
from jax.experimental import pallas as pl
from jax.experimental.pallas import tpu as pltpu
from jax.sharding import PartitionSpec as P

ITERS = 4
SUB = 128
EXTRA = 8


F32 = jnp.float32
BF16 = jnp.bfloat16


FULL = pltpu.CompilerParams(vmem_limit_bytes=67_043_328)


def whole(array):
    return pl.BlockSpec(array.shape, lambda *_: (0,) * len(array.shape))


def dot(left, right):
    return jnp.dot(left, right, preferred_element_type=F32)


def split(value):
    high = value.astype(BF16)
    low = (value - high.astype(F32)).astype(BF16)
    return high, low


def wide(value, axis=1):
    return jnp.concatenate(split(value), axis=axis)


def lane_shift(value, step):
    lanes = lax.broadcasted_iota(jnp.int32, value.shape, 1)
    return jnp.where(lanes >= step, pltpu.roll(value, step, 1), 0.0), lanes >= step


def cumulative_rows(value):
    step = 1
    while step < value.shape[1]:
        value = value + lane_shift(value, step)[0]
        step *= 2
    return value


def decayed_rows(value, cumulative):
    step = 1
    while step < value.shape[1]:
        earlier, inside = lane_shift(cumulative, step)
        factor = jnp.exp(jnp.where(inside, cumulative - earlier, 0.0))
        value = value + factor * lane_shift(value, step)[0]
        step *= 2
    return value


def decay_tables(decay_ref):
    rows = decay_ref.shape[1]
    offset = jnp.zeros((decay_ref.shape[0], 1), F32)
    local, full = [], []
    for c in range(rows // SUB):
        part = cumulative_rows(decay_ref[:, c * SUB : (c + 1) * SUB])
        local.append(part)
        full.append(part + offset)
        offset = offset + part[:, SUB - 1 : SUB]
    return local, jnp.exp(offset - jnp.concatenate(full, axis=1)), jnp.exp(offset)


def states_kernel(half, per, keys_ref, values_ref, decay_ref, near_ref, away_ref, table_ref, work_ref):
    rows, dim = keys_ref.shape[0], SUB
    core = lax.axis_index("seq") % 2
    row_at = lax.broadcasted_iota(jnp.int32, (dim, dim), 0)
    column_at = lax.broadcasted_iota(jnp.int32, (dim, dim), 1)
    local, tails, total = decay_tables(decay_ref)
    work_ref[0] = tails
    work_ref[2] = jnp.broadcast_to(total, tails.shape)
    first_gram = {}
    for slot in range(2 * half):
        out, block = (away_ref, 1 - core) if slot < half else (near_ref, core)
        i = slot % half
        for k in range(per):
            head = (block * half + i) * per + k
            column = pl.ds(pl.multiple_of(head * dim, dim), dim)
            key = keys_ref[:, column]
            tail = work_ref[0, pl.ds(head, 1), :]
            key_turned = key.astype(F32).T
            value_turned = values_ref[:, column].astype(F32).T
            work_ref[1, pl.ds(head, 1), :] = jnp.sum(key_turned * key_turned, axis=0, keepdims=True)
            high, low = split(jnp.concatenate([key_turned * tail, value_turned * tail], axis=0))
            state = dot(high, key) + dot(low, key)
            gram = state[0:dim]
            at, second = i // 2, i % 2
            out[k, at, (1 + second) * dim : (2 + second) * dim, :] = state[dim:]
            decay = work_ref[2, pl.ds(head, 1), :][:, 0:SUB]
            out[k, at, 3 * dim + second : 3 * dim + second + 1, :] = decay
            if second == 0:
                first_gram[k] = gram
            else:
                out[k, at, 0:dim, :] = jnp.where(row_at <= column_at, first_gram[k], gram)
                diagonal = jnp.sum(jnp.where(row_at == column_at, gram, 0.0), axis=0, keepdims=True)
                out[k, at, 3 * dim + 2 : 3 * dim + 3, :] = diagonal
                out[k, at, 3 * dim + 3 :, :] = jnp.zeros((EXTRA - 3, dim), F32)
    carry = jnp.zeros_like(total)
    for c in range(rows // SUB):
        lanes = slice(c * SUB, (c + 1) * SUB)
        part = decayed_rows(work_ref[1, :, lanes], local[c]) + jnp.exp(local[c]) * carry
        table_ref[0, :, lanes] = local[c]
        table_ref[1, :, lanes] = part
        carry = part[:, SUB - 1 : SUB]


def local_states(keys, values, decay, half, per):
    rows, columns = keys.shape
    heads = decay.shape[0]
    dim = columns // heads
    state = jax.ShapeDtypeStruct((per, half // 2, 3 * dim + EXTRA, dim), F32)
    table = jax.ShapeDtypeStruct((2, heads, rows), F32)
    return pl.pallas_call(
        functools.partial(states_kernel, half, per),
        out_shape=[state, state, table],
        in_specs=[whole(a) for a in (keys, values, decay)],
        out_specs=[whole(state), whole(state), whole(table)],
        scratch_shapes=[pltpu.VMEM((3, heads, rows), F32)],
        grid=(1,),
        compiler_params=FULL,
        cost_estimate=pl.CostEstimate(
            flops=16 * rows * dim * dim * half * per, bytes_accessed=8 * rows * columns, transcendentals=0
        ),
        name="local_states",
    )(keys, values, decay)


def join(earlier, later, dim):
    row_at = lax.broadcasted_iota(jnp.int32, later.shape, 1)
    column_at = lax.broadcasted_iota(jnp.int32, later.shape, 2)
    is_first = (row_at < dim) & (row_at <= column_at) | (row_at >= dim) & (row_at < 2 * dim)
    is_first = is_first | (row_at == 3 * dim)
    is_decay = (row_at == 3 * dim) | (row_at == 3 * dim + 1)
    factor = jnp.where(is_first, later[:, 3 * dim : 3 * dim + 1], later[:, 3 * dim + 1 : 3 * dim + 2])
    return factor * earlier + jnp.where(is_decay, 0.0, later)


def chip_kernel(dim, own_ref, came_ref, *out_refs):
    is_first = lax.axis_index("seq") % 2 == 0
    for k, out_ref in enumerate(out_refs):
        own, came = own_ref[k], came_ref[k]
        out_ref[...] = join(jnp.where(is_first, own, came), jnp.where(is_first, came, own), dim)


def start_kernel(dim, k, own_ref, came_ref, *refs):
    sent_refs, (mine_ref, other_ref) = refs[:-2], refs[-2:]
    is_first = lax.axis_index("seq") % 2 == 0
    before = sent_refs[-1][...]
    for ref in reversed(sent_refs[:-1]):
        before = join(before, ref[...], dim)
    after = join(before, jnp.where(is_first, own_ref[k], came_ref[k]), dim)
    mine_ref[...] = jnp.where(is_first, before, after)
    other_ref[...] = jnp.where(is_first, after, before)


def combine(kernel, arrays, shape, outs):
    out = jax.ShapeDtypeStruct(shape, F32)
    return pl.pallas_call(
        kernel,
        out_shape=[out] * outs,
        in_specs=[whole(a) for a in arrays],
        out_specs=[whole(out)] * outs,
        grid=(1,),
        compiler_params=FULL,
        cost_estimate=pl.CostEstimate(
            flops=0, bytes_accessed=8 * sum(a.size for a in arrays), transcendentals=0
        ),
    )(*arrays)


def solve_kernel(with_query, with_gradient, bounds, head_of, place_ref, regular_ref, *refs):
    refs = list(refs)
    q_ref = refs.pop(0) if with_query else None
    g_ref = refs.pop(0) if with_gradient else None
    k_ref, v_ref, rows_ref = refs[:3]
    state_refs, refs = refs[3 : 3 + len(bounds)], refs[3 + len(bounds) :]
    if with_gradient:
        half_ref, turned_ref = refs.pop(), refs.pop()
    mixed_ref = refs.pop() if with_query else None
    rows, dim = k_ref.shape
    pieces = range(rows // SUB)
    place = [slice(c * SUB, (c + 1) * SUB) for c in pieces]
    step = pl.program_id(0)
    head = head_of(step, place_ref)
    ridge = regular_ref[head]
    row_at = lax.broadcasted_iota(jnp.int32, (SUB, SUB), 0)
    column_at = lax.broadcasted_iota(jnp.int32, (SUB, SUB), 1)
    lower = row_at >= column_at

    is_second = lax.rem(step, 2) == 1

    def state(start, size):
        at = pl.ds(start, size)
        if len(state_refs) == 1:
            return state_refs[0][0, at, :]
        return jnp.where(step < bounds[1], state_refs[0][0, at, :], state_refs[1][0, at, :])

    packed = state(0, dim)
    direct = (row_at > column_at) == is_second
    start = jnp.where(direct, packed, packed.T)
    diagonal = state(3 * dim, EXTRA)[2:3]
    gram = [jnp.where((row_at == column_at) & is_second, diagonal, start)]
    memory = [state(pl.multiple_of((1 + lax.rem(step, 2)) * dim, dim), dim)]
    start_trace = jnp.sum(jnp.where(row_at == column_at, gram[0], 0.0), axis=0, keepdims=True)
    start_trace = jnp.sum(start_trace, axis=1, keepdims=True)
    cumulative_row = rows_ref[0, pl.ds(head, 1), :]
    cumulative = [cumulative_row[:, at] for at in place]
    last = [row[:, SUB - 1 : SUB] for row in cumulative]
    whole, offset = [], jnp.zeros((1, 1), F32)
    for c in pieces:
        whole.append(cumulative[c] + offset)
        offset = offset + last[c]
    trace = jnp.exp(jnp.concatenate(whole, axis=1)) * start_trace + rows_ref[1, pl.ds(head, 1), :]
    span = 0.5 * trace
    center = ridge + span
    alphas, gammas = [1.0 / center], []
    for i in range(1, ITERS):
        factor = 0.5 if i == 1 else 0.25
        product = span * alphas[-1]
        alphas.append(1.0 / (center - factor * span * product))
        gammas.append(alphas[-1] * (factor * span * product))
    table = jnp.concatenate(alphas + gammas + [cumulative_row], axis=0).T

    def column(index):
        return [jnp.broadcast_to(table[at, index : index + 1], (SUB, SUB)) for at in place]

    rise = column(2 * ITERS - 1)
    weights = [
        jnp.where(lower, jnp.exp(jnp.where(lower, rise[c] - cumulative[c], 0.0)), 0.0) for c in pieces
    ]
    scale = [jnp.exp(r) for r in rise]

    keys = [k_ref[at, :] for at in place]
    values = [v_ref[at, :] for at in place]
    keys_turned = [key.astype(F32).T for key in keys]
    values_turned = [value.astype(F32).T for value in values]
    for c in pieces[:-1]:
        tail = jnp.exp(last[c] - cumulative[c])
        decay = jnp.exp(last[c])
        both = jnp.concatenate([keys_turned[c] * tail, values_turned[c] * tail], axis=0)
        grown = dot(wide(both), jnp.concatenate([keys[c], keys[c]], axis=0))
        gram.append(decay * gram[-1] + grown[0:dim])
        memory.append(decay * memory[-1] + grown[dim:])
    keys_turned = [key.astype(BF16) for key in keys_turned]
    values_turned = [value.astype(BF16) for value in values_turned]

    def pair(left, right):
        return jnp.concatenate([left, right], axis=0)

    def each(value):
        return pair(value, value) if with_query and with_gradient else value

    residual = []
    for c in pieces:
        sides = []
        if with_query:
            sides.append(q_ref[place[c], :].astype(F32))
        if with_gradient:
            grad = g_ref[place[c], :]
            pulled = scale[c] * dot(jnp.concatenate([grad, grad], axis=1), wide(memory[c], 0))
            score = weights[c] * dot(grad, values_turned[c])
            sides.append(pulled + dot(wide(score), pair(keys[c], keys[c])))
        residual.append(jnp.concatenate(sides, axis=0) if len(sides) > 1 else sides[0])

    alpha = column(0)
    change = [each(alpha[c]) * residual[c] for c in pieces]
    solution = list(change)
    rights = [jnp.concatenate([keys_turned[c], gram[c].astype(BF16)], axis=1) for c in pieces]
    for i in range(1, ITERS):
        alpha, gamma = column(i), column(ITERS + i - 1)
        first = [dot(change[c].astype(BF16), rights[c]) for c in pieces]
        second = [
            dot((first[c][:, 0:SUB] * each(weights[c])).astype(BF16), keys[c]) for c in pieces
        ]
        for c in pieces:
            applied = ridge * change[c] + (each(scale[c]) * first[c][:, SUB:] + second[c])
            residual[c] = residual[c] - applied
            change[c] = each(alpha[c]) * residual[c] + each(gamma[c]) * change[c]
            solution[c] = solution[c] + change[c]

    if with_gradient:
        for c in pieces:
            turned = solution[c][-SUB:].T.astype(BF16)
            half_ref[0, :, place[c]] = turned
            turned_ref[0, :, place[c]] = turned.astype(F32)
    for c in pieces if with_query else ():
        high, low = split(solution[c][0:SUB])
        memory_high, memory_low = split(memory[c].T)
        right = jnp.concatenate([keys_turned[c], memory_high], axis=1)
        first = dot(jnp.concatenate([high, low], axis=1), pair(right, right))
        second = first[:, SUB:] + dot(high, memory_low)
        score = weights[c] * first[:, 0:SUB]
        output = scale[c] * second + dot(wide(score), pair(values[c], values[c]))
        mixed_ref[place[c], :] = output.astype(BF16)


def solve_heads(place, k, base, per, regular, queries, grads, keys, values, table, states, mixed, after):
    rows, columns = keys.shape
    heads = regular.shape[0]
    dim = columns // heads
    half = 2 * states[0].shape[0]
    groups, count = heads // per, half * len(states)
    with_query, with_gradient = queries is not None, grads is not None
    bounds = [half * i for i in range(len(states))]

    def head_of(step, place_ref):
        return lax.rem(place_ref[0] * half + base + step, groups) * per + k

    def at_head(step, place_ref, regular_ref):
        return (0, head_of(step, place_ref))

    wide_spec = pl.BlockSpec((rows, dim), at_head)
    operands = [a for a in (queries, grads, keys, values) if a is not None]
    in_specs = [wide_spec] * len(operands)
    operands.append(table)
    in_specs.append(whole(table))
    for bound, state in zip(bounds, states):

        def at_pair(step, *_, bound=bound):
            return (jnp.clip(step - bound, 0, half - 1) // 2, 0, 0)

        operands.append(state)
        in_specs.append(pl.BlockSpec((1,) + state.shape[1:], at_pair))
    aliases = {}
    if with_query and mixed is not None:
        operands.append(mixed)
        in_specs.append(pl.BlockSpec(memory_space=pl.ANY))
        aliases = {2 + len(operands) - 1: 0}
    if after is not None:
        operands.append(after)
        in_specs.append(pl.BlockSpec(memory_space=pl.ANY))
    shapes, out_specs = [], []
    if with_query:
        shapes.append(jax.ShapeDtypeStruct((rows, columns), BF16))
        out_specs.append(wide_spec)
    if with_gradient:
        shapes += [jax.ShapeDtypeStruct((count, dim, rows), kind) for kind in (F32, BF16)]
        out_specs += [pl.BlockSpec((1, dim, rows), lambda step, *_: (step, 0, 0))] * 2
    return pl.pallas_call(
        functools.partial(solve_kernel, with_query, with_gradient, bounds, head_of),
        out_shape=shapes,
        grid_spec=pltpu.PrefetchScalarGridSpec(
            num_scalar_prefetch=2, grid=(count,), in_specs=in_specs, out_specs=out_specs
        ),
        input_output_aliases=aliases,
        cost_estimate=pl.CostEstimate(
            flops=count * 80 * rows * dim * dim, bytes_accessed=count * 14 * rows * dim, transcendentals=0
        ),
        compiler_params=FULL,
        name="solve_heads",
    )(place, regular, *operands)


def pick_kernel(core_ref, tokens_ref, out_ref):
    out_ref[0] = tokens_ref[...].astype(F32)


def pick_columns(core, tokens, blocks):
    rows, width = tokens.shape
    size = width // (2 * blocks)
    return pl.pallas_call(
        pick_kernel,
        out_shape=jax.ShapeDtypeStruct((blocks, rows, size), F32),
        grid_spec=pltpu.PrefetchScalarGridSpec(
            num_scalar_prefetch=1,
            grid=(blocks,),
            in_specs=[pl.BlockSpec((rows, size), lambda z, core_ref: (0, 2 * z + 1 - core_ref[0]))],
            out_specs=pl.BlockSpec((1, rows, size), lambda z, core_ref: (z, 0, 0)),
        ),
        cost_estimate=pl.CostEstimate(flops=0, bytes_accessed=3 * rows * width, transcendentals=0),
        compiler_params=FULL,
        name="pick_columns",
    )(core, tokens)


def gradient_kernel(order, place_ref, own_ref, far_ref, tokens_ref, other_ref, *rest):
    outs, left_ref = rest[:-1], rest[-1]
    core, group = place_ref[0], place_ref[1]
    count, dim, rows = own_ref.shape
    half = count // 2
    middle = dim // 2

    @pl.when(pl.program_id(0) == 0)
    def _():
        for i in range(half):
            near, away = (core * half + i) ^ group, ((1 - core) * half + i) ^ group
            left_ref[near, :, 0:rows] = own_ref[i]
            left_ref[away, :, 0:rows] = own_ref[half + i]
            left_ref[near, :, rows:] = far_ref[half + i].astype(BF16)
            left_ref[away, :, rows:] = far_ref[i].astype(BF16)

    left = left_ref[...].reshape(2 * half * dim, 2 * rows)
    result = dot(left, jnp.concatenate([tokens_ref[...], other_ref[0].astype(BF16)], axis=0))
    for d in range(2 * half):
        for path in range(2):
            which, index = order[path][d]
            start = d * dim + path * middle
            outs[2 * path + which][index, 0] = result[start : start + middle]


def gradient_blocks(place, own, far, tokens, other, order):
    count, dim, rows = own.shape
    half = count // 2
    blocks, _, size = other.shape
    out = jax.ShapeDtypeStruct((half, blocks, dim // 2, size), F32)
    turned_spec = pl.BlockSpec((count, dim, rows), lambda z, p: (0, 0, 0))
    return pl.pallas_call(
        functools.partial(gradient_kernel, order),
        out_shape=[out] * 4,
        grid_spec=pltpu.PrefetchScalarGridSpec(
            num_scalar_prefetch=1,
            grid=(blocks,),
            in_specs=[turned_spec] * 2
            + [
                pl.BlockSpec((rows, size), lambda z, p: (0, 2 * (p[2] ^ z) + p[0])),
                pl.BlockSpec((1, rows, size), lambda z, p: (p[2] ^ z, 0, 0)),
            ],
            out_specs=[pl.BlockSpec((half, 1, dim // 2, size), lambda z, p: (0, z, 0, 0))] * 4,
            scratch_shapes=[pltpu.VMEM((2 * half, dim, 2 * rows), BF16)],
        ),
        cost_estimate=pl.CostEstimate(
            flops=8 * half * dim * rows * blocks * size,
            bytes_accessed=4 * (4 * half * dim * rows + blocks * rows * size + 2 * half * blocks * dim * size),
            transcendentals=0,
        ),
        compiler_params=FULL,
        name="gradient_blocks",
    )(place, own, far, tokens, other)


def sum_kernel(counts, *refs):
    arrays, outs = refs[: sum(counts)], refs[sum(counts) :]
    at = 0
    for count, out in zip(counts, outs):
        total = arrays[at][...]
        for ref in arrays[at + 1 : at + count]:
            total = total + ref[...]
        out[...] = total
        at += count


def sum_blocks(sums, length):
    counts = [len(arrays) for arrays in sums]
    arrays = [a for group in sums for a in group]
    out = jax.ShapeDtypeStruct((length,) + arrays[0].shape[1:], F32)
    return pl.pallas_call(
        functools.partial(sum_kernel, counts),
        out_shape=[out] * len(sums),
        in_specs=[pl.BlockSpec(out.shape, lambda _: (1, 0, 0, 0))] * len(arrays),
        out_specs=[whole(out)] * len(sums),
        grid=(1,),
        compiler_params=FULL,
        cost_estimate=pl.CostEstimate(
            flops=0, bytes_accessed=4 * (len(arrays) + 2) * out.size, transcendentals=0
        ),
        name="sum_blocks",
    )(*arrays)


def merge_kernel(counts, *refs):
    sums, outs = refs[: sum(counts)], refs[sum(counts) :]
    rows = sums[0].shape[2]
    at = 0
    for i, count in enumerate(counts):
        for z, out in enumerate(outs):
            total = sums[at][0, z]
            for ref in sums[at + 1 : at + count]:
                total = total + ref[0, z]
            out[i * rows : (i + 1) * rows, :] = total
        at += count


def merge_blocks(sums):
    counts = [len(arrays) for arrays in sums]
    arrays = [a for group in sums for a in group]
    _, chips, rows, size = arrays[0].shape
    out = jax.ShapeDtypeStruct((len(counts) * rows, size), F32)
    return pl.pallas_call(
        functools.partial(merge_kernel, counts),
        out_shape=[out] * chips,
        in_specs=[pl.BlockSpec((1, chips, rows, size), lambda _: (0, 0, 0, 0))] * len(arrays),
        out_specs=[whole(out)] * chips,
        grid=(1,),
        compiler_params=FULL,
        cost_estimate=pl.CostEstimate(
            flops=0, bytes_accessed=4 * (len(arrays) + 2) * chips * rows * size, transcendentals=0
        ),
        name="merge_blocks",
    )(*arrays)


def finish_kernel(count, *refs):
    out = refs[-1]
    rows = refs[0].shape[0]
    for k in range((len(refs) - 1) // count):
        total = refs[k * count][...]
        for ref in refs[k * count + 1 : (k + 1) * count]:
            total = total + ref[...]
        out[k * rows : (k + 1) * rows, :] = total


def finish(sets):
    arrays = [a for group in sets for a in group]
    rows, size = arrays[0].shape
    out = jax.ShapeDtypeStruct((rows * len(sets), size), F32)
    return pl.pallas_call(
        functools.partial(finish_kernel, len(sets[0])),
        out_shape=out,
        in_specs=[whole(a) for a in arrays],
        out_specs=whole(out),
        grid=(1,),
        compiler_params=FULL,
        cost_estimate=pl.CostEstimate(
            flops=0, bytes_accessed=5 * sum(a.size for a in arrays), transcendentals=0
        ),
        name="finish",
    )(*arrays)


def bit_order(bits):
    table = []
    for d in range(1 << len(bits)):
        code = 0
        for bit in bits:
            code = 2 * code + ((d >> bit) & 1)
        table.append(divmod(code, 1 << (len(bits) - 1)))
    return table


def per_device(sizes, *arrays):
    return program(sizes, *arrays)


def program(sizes, tokens, w_query, keys, values, log_decay, regular, grad_out):
    groups, steps = sizes["dp"], sizes["seq"]
    chips = steps // 2
    heads = log_decay.shape[1]
    columns = keys.shape[2]
    dim = columns // heads
    per = heads // groups
    half = groups // 2
    tokens, keys, values, grads, decay = tokens[0], keys[0], values[0], grad_out[0], log_decay[0]
    here = lax.axis_index("seq")
    core = here % 2
    place = jnp.stack([core, lax.axis_index("dp"), here // 2]).astype(jnp.int32)
    partner = [(i, i ^ 1) for i in range(steps)]

    own, away, table = local_states(keys, values, decay, half, per)
    came = lax.ppermute(away, "seq", partner)
    shape = own.shape[1:]
    chip_states = combine(functools.partial(chip_kernel, dim), [own, came], shape, per)
    starts = []
    for k, chip_state in enumerate(chip_states):
        sent = []
        for z in range(1, chips):
            pairs = [(i, i + 2 * z) for i in range(steps - 2 * z)]
            sent.append(lax.ppermute(chip_state, "seq", pairs))
        starting = functools.partial(start_kernel, dim, k)
        mine, others = combine(starting, [own, came, *sent], shape, 2)
        starts.append((mine, lax.ppermute(others, "seq", partner)))

    picked = pick_columns(place, tokens, chips)
    other = lax.ppermute(picked, "seq", partner)
    queries = jnp.dot(tokens, w_query, preferred_element_type=F32).astype(BF16)

    dp_bits = groups.bit_length() - 1
    paths = [list(range(dp_bits)), list(reversed(range(dp_bits)))]
    order = [bit_order(path) for path in paths]

    products, mixed = [], None
    for k, states in enumerate(starts):
        after = products[-1][0] if k > 0 else None
        joint = k < per - 1
        results = solve_heads(
            place, k, 0, per, regular, queries if joint else None, grads, keys, values, table, states, mixed, after
        )
        turned, own_rows = results[-2:]
        if joint:
            mixed = results[0]
        far = lax.ppermute(turned, "seq", partner)
        products.append(gradient_blocks(place, own_rows, far, tokens, other, order))
    for side in range(2):
        after = products[-1][0] if side == 0 else None
        (mixed,) = solve_heads(
            place, per - 1, side * half, per, regular, queries, None, keys, values, table,
            [starts[-1][side]], mixed, after,
        )

    finished = []
    for blocks in products:
        sums, sends = [[blocks[0]], [blocks[2]]], [blocks[1], blocks[3]]
        for stage in range(dp_bits):
            for index, path in enumerate(paths):
                pairs = [(i, i ^ (1 << path[stage])) for i in range(groups)]
                sums[index].append(lax.ppermute(sends[index], "dp", pairs))
            if stage < dp_bits - 1:
                sends = sum_blocks(sums, sends[0].shape[0] // 2)
        out, *others = merge_blocks(sums)
        finished.append([out])
        for z, other_block in enumerate(others, 1):
            pairs = [(i, i ^ (2 * z)) for i in range(steps)]
            finished[-1].append(lax.ppermute(other_block, "seq", pairs))
    return mixed[None], finish(finished)


def solution(mesh):
    sizes = dict(mesh.shape)
    in_specs = (
        P("dp", "seq", None),
        P(),
        P("dp", "seq", None),
        P("dp", "seq", None),
        P("dp", None, "seq"),
        P(),
        P("dp", "seq", None),
    )
    out_specs = (P("dp", "seq", None), P("dp", "seq"))
    return jax.shard_map(
        functools.partial(per_device, sizes),
        mesh=mesh,
        in_specs=in_specs,
        out_specs=out_specs,
        check_vma=False,
    )
```
